32 devices in a mesh: dp: 8 (over z, y), fsdp: 4 (over x, core).
Axes of the slice: x: 2, y: 2, z: 4, core: 2. Of those that a mesh axis runs over, the one named last changes fastest.
Arguments:
- suffix: bfloat16 [4, 32, 64, 768], P('fsdp', 'dp'), may hold values from -6 to 6
- memory: bfloat16 [4, 32, 256, 768], P('fsdp', None, 'dp'), may hold values from -6 to 6
- prefix_lengths: int32 [4, 32], P('fsdp', 'dp'), may hold values from 0 to 60, as said below
- suffix_lengths: int32 [4, 32], P('fsdp', 'dp'), may hold values from 1 to 64, as said below
- cotangent: bfloat16 [4, 32, 64, 768], P('fsdp', 'dp'), may hold values from -6 to 6
- self_weights: float32 [2359296], P(('dp', 'fsdp'))
- self_moment: float32 [2359296], P(('dp', 'fsdp')), may hold values from -0.0048828125 to 0.0048828125
- self_second: float32 [2359296], P(('dp', 'fsdp')), may hold values from 1.05963814e-07 to 4.2385525e-07
- cross_weights: float32 [2359296], P(('dp', 'fsdp'))
- cross_moment: float32 [2359296], P(('dp', 'fsdp')), may hold values from -0.0048828125 to 0.0048828125
- cross_second: float32 [2359296], P(('dp', 'fsdp')), may hold values from 1.05963814e-07 to 4.2385525e-07
- feed_weights: float32 [4718592], P(('dp', 'fsdp'))
- feed_moment: float32 [4718592], P(('dp', 'fsdp')), may hold values from -0.0048828125 to 0.0048828125
- feed_second: float32 [4718592], P(('dp', 'fsdp')), may hold values from 1.05963814e-07 to 4.2385525e-07
- vectors: float32 [8448], replicated
- vector_moment: float32 [8448], replicated, may hold values from -0.015625 to 0.015625
- vector_second: float32 [8448], replicated, may hold values from 9.536743e-07 to 3.8146973e-06
Outputs:
- layer_output: float32 [4, 32, 64, 768], P('fsdp', 'dp')
- suffix_gradient: float32 [4, 32, 64, 768], P('fsdp', 'dp')
- memory_gradient: float32 [4, 32, 256, 768], P('fsdp', None, 'dp')
- self_gradient: float32 [2359296], P(('dp', 'fsdp'))
- self_momentum: float32 [2359296], P(('dp', 'fsdp'))
- self_variance: float32 [2359296], P(('dp', 'fsdp'))
- self_master: float32 [2359296], P(('dp', 'fsdp'))
- cross_gradient: float32 [2359296], P(('dp', 'fsdp'))
- cross_momentum: float32 [2359296], P(('dp', 'fsdp'))
- cross_variance: float32 [2359296], P(('dp', 'fsdp'))
- cross_master: float32 [2359296], P(('dp', 'fsdp'))
- feed_gradient: float32 [4718592], P(('dp', 'fsdp'))
- feed_momentum: float32 [4718592], P(('dp', 'fsdp'))
- feed_variance: float32 [4718592], P(('dp', 'fsdp'))
- feed_master: float32 [4718592], P(('dp', 'fsdp'))
- vector_gradient: float32 [8448], replicated
- vector_momentum: float32 [8448], replicated
- vector_variance: float32 [8448], replicated
- vector_master: float32 [8448], replicated
- tensor_norms: float32 [2, 18], replicated
- global_norm: float32 [], replicated
The draws below stay inside these ranges and needn't reach their ends.
Inputs may be any that keep to these rules, and one draw needn't show every extreme that they name: The number of prefix text tokens of each example, zero for many; memory slots from 196 + prefix_lengths on are padding. The number of caption tokens of each example; slots from suffix_lengths on are padding.
All inputs are finite; a program needn't handle non-finite values.
Results may differ from the reference program's by a relative error of at most 0.014.
The reference program's roundings to bfloat16 on the way count: a program that leaves them out, or rounds other values in their place, can miss the bound.
Values may be sent and summed in bfloat16 or wider, within the bound.
A program may use at most 192 MiB of HBM per device.

```python
import math
import jax
import jax.numpy as jnp
from jax import lax

D = 768
H = 12
HD = 64
FF = 3072
PATCH = 196
PRE = 60
SUF = 64
EX_DEV = 4
MEMLEN = 256
GROUPS = 4
GROUP_EX = 32
ATTN_FLAT = 2359296
FEED_FLAT = 4718592
VEC = 8448


def draw_prefix_lengths(key, part):
    base_key = jax.random.fold_in(key, 101)
    key_one, key_two, key_three = jax.random.split(base_key, 3)
    number = GROUPS * GROUP_EX
    chosen = jax.random.randint(key_one, (number,), 1, PRE + 1, dtype=jnp.int32)
    coin_flips = jax.random.randint(key_two, (number,), 0, 2, dtype=jnp.int32)
    lengths = jnp.where(coin_flips == 0, jnp.zeros_like(chosen), chosen)
    chosen_spots = jax.random.permutation(key_three, number)[:2]
    lengths = lengths.at[chosen_spots[0]].set(PRE).at[chosen_spots[1]].set(0)
    return lengths.reshape(GROUPS, GROUP_EX).astype(jnp.int32)


def draw_suffix_lengths(key, part):
    base_key = jax.random.fold_in(key, 102)
    key_one, key_two = jax.random.split(base_key, 2)
    number = GROUPS * GROUP_EX
    lengths = jax.random.randint(key_one, (number,), 1, SUF + 1, dtype=jnp.int32)
    chosen_spots = jax.random.permutation(key_two, number)[:2]
    lengths = lengths.at[chosen_spots[0]].set(SUF).at[chosen_spots[1]].set(1)
    return lengths.reshape(GROUPS, GROUP_EX).astype(jnp.int32)


def attention_matrices(key):
    normal_draw = jax.random.normal(key, (4 * D * D,), jnp.float32)
    segment = jnp.arange(4 * D * D) // (D * D)
    factors = jnp.where(segment == 3, 4.0, 1.0) / math.sqrt(D)
    return normal_draw * factors


def draw_self_weights(key, part):
    return attention_matrices(jax.random.fold_in(key, 201))


def draw_cross_weights(key, part):
    return attention_matrices(jax.random.fold_in(key, 202))


def draw_feed_weights(key, part):
    normal_draw = jax.random.normal(jax.random.fold_in(key, 203), (2 * D * FF,), jnp.float32)
    position = jnp.arange(2 * D * FF)
    factors = jnp.where(position < D * FF, 1.0 / math.sqrt(D), 1.0 / math.sqrt(FF))
    return normal_draw * factors


def draw_vectors(key, part):
    normal_draw = jax.random.normal(jax.random.fold_in(key, 301), (7 * D + FF,), jnp.float32)
    segment = jnp.arange(7 * D + FF) // D
    is_gain = (segment == 0) | (segment == 2) | (segment == 4)
    return jnp.where(is_gain, 1.0 + 0.15 * normal_draw, 0.1 * normal_draw)


def level_of(key, shape, cuts, least, top_value):
    factor_of = 1.0
    for axis_at, blocks in cuts:
        steps = jax.random.uniform(jax.random.fold_in(jax.random.fold_in(key, 6), axis_at), (blocks,), jnp.float32, least / len(cuts), top_value / len(cuts))
        factor_of = factor_of * jnp.repeat(jnp.exp(steps), shape[axis_at] // blocks).reshape((-1,) + (1,) * (len(shape) - 1 - axis_at))
    return factor_of


def normal_values(key, dims, width, most, cuts=(), kind=jnp.bfloat16):
    result = width * jax.random.normal(key, dims, jnp.float32)
    if cuts:
        result = result * level_of(key, dims, cuts, -0.22, 0.18)
    return jnp.clip(result, -most, most).astype(kind)


def setup_inputs(seed: int = 0) -> dict:
    arg_keys = jax.random.split(jax.random.key(seed), 18)
    suffix = normal_values(arg_keys[0], (GROUPS, GROUP_EX, SUF, D), 1.0, 6.0, ((0, 4), (1, 8)))
    memory = normal_values(arg_keys[1], (GROUPS, GROUP_EX, MEMLEN, D), 1.0, 6.0, ((0, 4), (2, 8)))
    prefix_lengths = draw_prefix_lengths(jax.random.fold_in(arg_keys[17], 71), 0)
    suffix_lengths = draw_suffix_lengths(jax.random.fold_in(arg_keys[17], 71), 0)
    cotangent = normal_values(arg_keys[4], (GROUPS, GROUP_EX, SUF, D), 1.0, 6.0, ((0, 4), (1, 8)))
    self_weights = draw_self_weights(jax.random.fold_in(arg_keys[17], 71), 0)
    self_moment = normal_values(arg_keys[6], (ATTN_FLAT,), ((8 * D * D + 2 * D * FF) ** -0.5), 0.0048828125, ((0, 32),), jnp.float32)
    self_second = jnp.clip(jnp.exp(math.log(4.238552548940788e-07) - 1.3862944 * jax.random.uniform(arg_keys[7], (ATTN_FLAT,), jnp.float32) ** level_of(arg_keys[7], (ATTN_FLAT,), ((0, 32),), -0.2, 0.2)), 1.059638137235197e-07, 4.238552548940788e-07)
    cross_weights = draw_cross_weights(jax.random.fold_in(arg_keys[17], 71), 0)
    cross_moment = normal_values(arg_keys[9], (ATTN_FLAT,), ((8 * D * D + 2 * D * FF) ** -0.5), 0.0048828125, ((0, 32),), jnp.float32)
    cross_second = jnp.clip(jnp.exp(math.log(4.238552548940788e-07) - 1.3862944 * jax.random.uniform(arg_keys[10], (ATTN_FLAT,), jnp.float32) ** level_of(arg_keys[10], (ATTN_FLAT,), ((0, 32),), -0.2, 0.2)), 1.059638137235197e-07, 4.238552548940788e-07)
    feed_weights = draw_feed_weights(jax.random.fold_in(arg_keys[17], 71), 0)
    feed_moment = normal_values(arg_keys[12], (FEED_FLAT,), ((8 * D * D + 2 * D * FF) ** -0.5), 0.0048828125, ((0, 32),), jnp.float32)
    feed_second = jnp.clip(jnp.exp(math.log(4.238552548940788e-07) - 1.3862944 * jax.random.uniform(arg_keys[13], (FEED_FLAT,), jnp.float32) ** level_of(arg_keys[13], (FEED_FLAT,), ((0, 32),), -0.2, 0.2)), 1.059638137235197e-07, 4.238552548940788e-07)
    vectors = draw_vectors(jax.random.fold_in(arg_keys[17], 71), 0)
    vector_moment = normal_values(arg_keys[15], (VEC,), (3 * (8 * D * D + 2 * D * FF) ** -0.5), 0.015625, (), jnp.float32)
    vector_second = jnp.clip(jnp.exp(jax.random.uniform(arg_keys[16], (VEC,), jnp.float32, math.log(9.5367431640625e-07), math.log(3.814697265625e-06))), 9.5367431640625e-07, 3.814697265625e-06)
    return {"suffix": suffix, "memory": memory, "prefix_lengths": prefix_lengths, "suffix_lengths": suffix_lengths, "cotangent": cotangent, "self_weights": self_weights, "self_moment": self_moment, "self_second": self_second, "cross_weights": cross_weights, "cross_moment": cross_moment, "cross_second": cross_second, "feed_weights": feed_weights, "feed_moment": feed_moment, "feed_second": feed_second, "vectors": vectors, "vector_moment": vector_moment, "vector_second": vector_second}


@jax.custom_vjp
def low(v):
    return lax.optimization_barrier(v.astype(jnp.bfloat16)).astype(jnp.float32)

@jax.custom_vjp
def low_back(v):
    return v

def low_keep(v):
    return (low(v), None)

def low_pass(kept, grad):
    return (grad,)

def back_keep(v):
    return (v, None)

def back_low(kept, grad):
    return (low(grad),)
low.defvjp(low_keep, low_pass)
low_back.defvjp(back_keep, back_low)
beta_one = 0.5
beta_two = 0.55
step_count = 5
learn_rate = 0.5
decay_weight = 0.01
adam_eps = 1e-06
norm_eps = 1e-06
trust_eps = 1e-06
masked_score = -1e+30

def matmul(left, right):
    return jnp.matmul(left, right, precision=lax.Precision.HIGHEST)

def layer_norm(values, norm_gain, norm_shift):
    centred = values - lax.optimization_barrier(jnp.mean(values, axis=-1, keepdims=True))
    spread = lax.optimization_barrier(jnp.mean(centred * centred, axis=-1, keepdims=True))
    return centred * lax.rsqrt(spread + norm_eps) * norm_gain + norm_shift

def gelu_tanh(values):
    return jax.nn.gelu(values, approximate=True)

def attend(query_rows, key_rows, value_rows, allowed):
    number = query_rows.shape[0]
    query_len = query_rows.shape[1]
    query_heads = query_rows.reshape(number, query_len, H, HD)
    key_heads = key_rows.reshape(number, key_rows.shape[1], H, HD)
    value_heads = value_rows.reshape(number, value_rows.shape[1], H, HD)
    scores = jnp.einsum('bqhe,bkhe->bhqk', query_heads, key_heads, precision=lax.Precision.HIGHEST) * HD ** (-0.5)
    scores = low_back(scores)
    scores = jnp.where(allowed, scores, masked_score)
    attention = low(jax.nn.softmax(scores, axis=-1))
    mixed_rows = jnp.einsum('bhqk,bkhe->bqhe', attention, value_heads, precision=lax.Precision.HIGHEST)
    return low(low_back(mixed_rows.reshape(number, query_len, D)))

def decoder_block(inputs, sources, prefix_len, suffix_len, self_mats, cross_mats, up_mat, down_mat, vector_all):
    vector_parts = [vector_all[segment * D:(segment + 1) * D] for segment in range(7)]
    bias_up = vector_all[7 * D:]
    positions = jnp.arange(SUF, dtype=jnp.int32)
    causal = positions[:, None] >= positions[None, :]
    self_allowed = causal[None, None, :, :] & (positions[None, :] < suffix_len[:, None])[:, None, None, :]
    memory_pos = jnp.arange(MEMLEN, dtype=jnp.int32)
    cross_allowed = (memory_pos[None, :] < (PATCH + prefix_len)[:, None])[:, None, None, :]
    normed_one = low(layer_norm(inputs, vector_parts[0], vector_parts[1]))
    query_one = low(low_back(matmul(normed_one, self_mats[0])))
    key_one = low(low_back(matmul(normed_one, self_mats[1])))
    value_one = low(low_back(matmul(normed_one, self_mats[2])))
    mixed_one = attend(query_one, key_one, value_one, self_allowed)
    hidden_one = inputs + low_back(matmul(mixed_one, self_mats[3]))
    normed_two = low(layer_norm(hidden_one, vector_parts[2], vector_parts[3]))
    query_two = low(low_back(matmul(normed_two, cross_mats[0])))
    key_two = low(low_back(matmul(sources, cross_mats[1])))
    value_two = low(low_back(matmul(sources, cross_mats[2])))
    mixed_two = attend(query_two, key_two, value_two, cross_allowed)
    hidden_two = hidden_one + low_back(matmul(mixed_two, cross_mats[3]))
    normed_three = low(layer_norm(hidden_two, vector_parts[4], vector_parts[5]))
    pre_act = low_back(matmul(normed_three, up_mat) + bias_up)
    activated = low(gelu_tanh(pre_act))
    return hidden_two + low_back(matmul(activated, down_mat) + vector_parts[6])

def forward(suffix_all, memory_all, self_flat, cross_flat, feed_flat, vector_all, prefix_lengths, suffix_lengths):
    self_mats = low(self_flat).reshape(4, D, D)
    cross_mats = low(cross_flat).reshape(4, D, D)
    feed_low = low(feed_flat)
    up_mat = feed_low[:D * FF].reshape(D, FF)
    down_mat = feed_low[D * FF:].reshape(FF, D)
    batches = GROUPS * GROUP_EX // EX_DEV
    inputs = suffix_all.reshape(batches, EX_DEV, SUF, D)
    sources = memory_all.reshape(batches, EX_DEV, MEMLEN, D)
    prefixes = prefix_lengths.reshape(batches, EX_DEV)
    suffixes = suffix_lengths.reshape(batches, EX_DEV)

    def one_batch(batch_items):
        return decoder_block(batch_items[0], batch_items[1], batch_items[2], batch_items[3], self_mats, cross_mats, up_mat, down_mat, vector_all)
    outputs = lax.map(jax.checkpoint(one_batch), (inputs, sources, prefixes, suffixes))
    return outputs.reshape(GROUPS, GROUP_EX, SUF, D)

def lamb_step(weight, gradient, moment, second, clip_factor):
    clipped = clip_factor * gradient
    moment_new = beta_one * moment + (1.0 - beta_one) * clipped
    second_new = beta_two * second + (1.0 - beta_two) * clipped * clipped
    ratio = moment_new / (1.0 - beta_one ** step_count) / (jnp.sqrt(second_new / (1.0 - beta_two ** step_count)) + adam_eps) + decay_weight * weight
    return (moment_new, second_new, ratio)

def matrix_update(weight, gradient, moment, second, clip_factor, tensor_count):
    moment_new, second_new, ratio = lamb_step(weight, gradient, moment, second, clip_factor)
    weight_rows = weight.reshape(tensor_count, -1)
    ratio_rows = ratio.reshape(tensor_count, -1)
    weight_norms = jnp.sqrt(lax.optimization_barrier(jnp.sum(weight_rows * weight_rows, axis=1)))
    ratio_norms = jnp.sqrt(lax.optimization_barrier(jnp.sum(ratio_rows * ratio_rows, axis=1)))
    trust_ratio = weight_norms / (ratio_norms + trust_eps)
    master = (weight_rows - learn_rate * trust_ratio[:, None] * ratio_rows).reshape(-1)
    return (moment_new, second_new, master, weight_norms, ratio_norms)

def reference(suffix, memory, prefix_lengths, suffix_lengths, cotangent, self_weights, self_moment, self_second, cross_weights, cross_moment, cross_second, feed_weights, feed_moment, feed_second, vectors, vector_moment, vector_second):

    def wrapped(suffix_all, memory_all, self_flat, cross_flat, feed_flat, vector_all):
        return forward(suffix_all, memory_all, self_flat, cross_flat, feed_flat, vector_all, prefix_lengths, suffix_lengths)
    layer_output, pullback = jax.vjp(wrapped, suffix.astype(jnp.float32), memory.astype(jnp.float32), self_weights, cross_weights, feed_weights, vectors)
    valid_rows = (jnp.arange(SUF, dtype=jnp.int32)[None, None, :] < suffix_lengths[:, :, None]).astype(jnp.float32)
    seed_rows = cotangent.astype(jnp.float32) * valid_rows[..., None]
    suffix_gradient, memory_gradient, self_gradient, cross_gradient, feed_gradient, vector_gradient = pullback(seed_rows)
    squares = jnp.sum(self_gradient * self_gradient) + jnp.sum(cross_gradient * cross_gradient) + jnp.sum(feed_gradient * feed_gradient) + jnp.sum(vector_gradient * vector_gradient)
    global_norm = jnp.sqrt(squares)
    clip_factor = jnp.minimum(1.0, 1.0 / global_norm)
    self_momentum, self_variance, self_master, self_wn, self_rn = matrix_update(self_weights, self_gradient, self_moment, self_second, clip_factor, 4)
    cross_momentum, cross_variance, cross_master, cross_wn, cross_rn = matrix_update(cross_weights, cross_gradient, cross_moment, cross_second, clip_factor, 4)
    feed_momentum, feed_variance, feed_master, feed_wn, feed_rn = matrix_update(feed_weights, feed_gradient, feed_moment, feed_second, clip_factor, 2)
    vector_momentum, vector_variance, vector_ratio = lamb_step(vectors, vector_gradient, vector_moment, vector_second, clip_factor)
    edges = [0, D, 2 * D, 3 * D, 4 * D, 5 * D, 6 * D, 7 * D, 7 * D + FF]
    vector_wn = []
    vector_rn = []
    new_pieces = []
    for segment in range(8):
        weight_part = vectors[edges[segment]:edges[segment + 1]]
        ratio_part = vector_ratio[edges[segment]:edges[segment + 1]]
        weight_norm = jnp.sqrt(jnp.sum(weight_part * weight_part))
        ratio_norm = jnp.sqrt(jnp.sum(ratio_part * ratio_part))
        trust_ratio = weight_norm / (ratio_norm + trust_eps)
        vector_wn.append(weight_norm)
        vector_rn.append(ratio_norm)
        new_pieces.append(weight_part - learn_rate * trust_ratio * ratio_part)
    vector_master = jnp.concatenate(new_pieces)
    tensor_norms = jnp.stack([jnp.concatenate([self_wn, cross_wn, feed_wn, jnp.stack(vector_wn)]), jnp.concatenate([self_rn, cross_rn, feed_rn, jnp.stack(vector_rn)])])
    return (layer_output, suffix_gradient, memory_gradient, self_gradient, self_momentum, self_variance, self_master, cross_gradient, cross_momentum, cross_variance, cross_master, feed_gradient, feed_momentum, feed_variance, feed_master, vector_gradient, vector_momentum, vector_variance, vector_master, tensor_norms, global_norm)
```

```python
import jax
import jax.numpy as jnp
from jax import lax
from jax.experimental import pallas as pl
from jax.experimental.pallas import tpu as pltpu
from jax.sharding import PartitionSpec as P

D = 768
H = 12
HD = 64
FF = 3072
PATCH = 196
SUF = 64
EX_DEV = 4
MEMLEN = 256


beta_one = 0.5
beta_two = 0.55
step_count = 5
learn_rate = 0.5
decay_weight = 0.01
adam_eps = 1e-06
norm_eps = 1e-06
trust_eps = 1e-06
masked_score = -1e30


def layer_norm(values, norm_gain, norm_shift):
    centred = values - jnp.mean(values, axis=-1, keepdims=True)
    spread = jnp.mean(centred * centred, axis=-1, keepdims=True)
    return centred * lax.rsqrt(spread + norm_eps) * norm_gain + norm_shift


def gelu_tanh(values):
    return jax.nn.gelu(values, approximate=True)


def attend_forward(query_heads, key_heads, value_heads, allowed):
    score_scale = HD ** (-0.5)
    scores = (
        jnp.einsum("bqhe,bkhe->bhqk", query_heads, key_heads, preferred_element_type=jnp.float32)
        * score_scale
    )
    scores = jnp.where(allowed, scores, masked_score)
    attention = jax.nn.softmax(scores, axis=-1)
    totals = jax.nn.logsumexp(scores, axis=-1)
    mixed_rows = jnp.einsum(
        "bhqk,bkhe->bqhe",
        attention.astype(jnp.bfloat16),
        value_heads,
        preferred_element_type=jnp.float32,
    )
    return (mixed_rows, totals)


def attend_backward(query_heads, key_heads, value_heads, allowed, totals, mixed_grad):
    score_scale = HD ** (-0.5)
    scores = (
        jnp.einsum("bqhe,bkhe->bhqk", query_heads, key_heads, preferred_element_type=jnp.float32)
        * score_scale
    )
    scores = jnp.where(allowed, scores, masked_score)
    attention = jnp.exp(scores - totals[..., None])
    value_grad = jnp.einsum(
        "bhqk,bqhe->bkhe",
        attention.astype(jnp.bfloat16),
        mixed_grad,
        preferred_element_type=jnp.float32,
    )
    attention_grad = jnp.einsum(
        "bqhe,bkhe->bhqk", mixed_grad, value_heads, preferred_element_type=jnp.float32
    )
    score_grad = attention * (
        attention_grad - jnp.sum(attention * attention_grad, axis=-1, keepdims=True)
    )
    score_low = score_grad.astype(jnp.bfloat16)
    query_grad = (
        jnp.einsum("bhqk,bkhe->bqhe", score_low, key_heads, preferred_element_type=jnp.float32)
        * score_scale
    )
    key_grad = (
        jnp.einsum("bhqk,bqhe->bkhe", score_low, query_heads, preferred_element_type=jnp.float32)
        * score_scale
    )
    return (query_grad, key_grad, value_grad)


def lamb_step(weight, gradient, moment, second, clip_factor):
    clipped = clip_factor * gradient
    moment_new = beta_one * moment + (1.0 - beta_one) * clipped
    second_new = beta_two * second + (1.0 - beta_two) * clipped * clipped
    ratio = (
        moment_new
        / (1.0 - beta_one**step_count)
        / (jnp.sqrt(second_new / (1.0 - beta_two**step_count)) + adam_eps)
        + decay_weight * weight
    )
    return (moment_new, second_new, ratio)


def segment_sums(values, offset, segment_size, tensor_count):
    labels = (offset + jnp.arange(values.shape[0], dtype=jnp.int32)) // segment_size
    matches = labels[:, None] == jnp.arange(tensor_count, dtype=jnp.int32)[None, :]
    return jnp.sum(jnp.where(matches, values[:, None], 0.0), axis=0)


def segment_spread(factors, offset, length_here, segment_size):
    labels = (offset + jnp.arange(length_here, dtype=jnp.int32)) // segment_size
    matches = labels[:, None] == jnp.arange(factors.shape[0], dtype=jnp.int32)[None, :]
    return jnp.sum(jnp.where(matches, factors[None, :], 0.0), axis=1)


def shards(
    suffix,
    memory,
    prefix_lengths,
    suffix_lengths,
    cotangent,
    self_weights,
    self_moment,
    self_second,
    cross_weights,
    cross_moment,
    cross_second,
    feed_weights,
    feed_moment,
    feed_second,
    vectors,
    vector_moment,
    vector_second,
):
    row_count = EX_DEV * SUF
    attn_shard = self_weights.shape[0]
    feed_shard = feed_weights.shape[0]
    self_full, cross_full, feed_full = (
        lax.all_gather(self_weights.astype(jnp.bfloat16), ("dp", "fsdp"), axis=0, tiled=True),
        lax.all_gather(cross_weights.astype(jnp.bfloat16), ("dp", "fsdp"), axis=0, tiled=True),
        lax.all_gather(feed_weights.astype(jnp.bfloat16), ("dp", "fsdp"), axis=0, tiled=True),
    )
    self_mats = self_full.reshape(4, D, D)
    cross_mats = cross_full.reshape(4, D, D)
    up_mat = feed_full[: D * FF].reshape(D, FF)
    down_mat = feed_full[D * FF :].reshape(FF, D)
    vector_parts = [vectors[segment * D : (segment + 1) * D] for segment in range(7)]
    bias_up = vectors[7 * D :]
    own_memory = lax.all_to_all(memory, "dp", split_axis=1, concat_axis=2, tiled=True)
    memory_rows = own_memory.reshape(EX_DEV * MEMLEN, D)
    suffix_len = suffix_lengths[0]
    prefix_len = prefix_lengths[0]
    positions = jnp.arange(SUF, dtype=jnp.int32)
    causal = positions[:, None] >= positions[None, :]
    self_allowed = (
        causal[None, None, :, :] & (positions[None, :] < suffix_len[:, None])[:, None, None, :]
    )
    memory_pos = jnp.arange(MEMLEN, dtype=jnp.int32)
    cross_allowed = (memory_pos[None, :] < (PATCH + prefix_len)[:, None])[:, None, None, :]
    inputs = suffix.reshape(row_count, D).astype(jnp.float32)
    normed_one = layer_norm(inputs, vector_parts[0], vector_parts[1]).astype(jnp.bfloat16)
    self_qkv = jnp.einsum(
        "rd,jde->jre", normed_one, self_mats[0:3], preferred_element_type=jnp.float32
    ).astype(jnp.bfloat16)
    self_heads = self_qkv.reshape(3, EX_DEV, SUF, H, HD)
    mixed_one, totals_one = attend_forward(
        self_heads[0], self_heads[1], self_heads[2], self_allowed
    )
    mixed_one = mixed_one.reshape(row_count, D).astype(jnp.bfloat16)
    hidden_one = inputs + jnp.dot(mixed_one, self_mats[3], preferred_element_type=jnp.float32)
    normed_two = layer_norm(hidden_one, vector_parts[2], vector_parts[3]).astype(jnp.bfloat16)
    cross_query = jnp.dot(normed_two, cross_mats[0], preferred_element_type=jnp.float32).astype(
        jnp.bfloat16
    )
    cross_kv = jnp.einsum(
        "rd,jde->jre", memory_rows, cross_mats[1:3], preferred_element_type=jnp.float32
    ).astype(jnp.bfloat16)
    query_heads = cross_query.reshape(EX_DEV, SUF, H, HD)
    kv_heads = cross_kv.reshape(2, EX_DEV, MEMLEN, H, HD)
    mixed_two, totals_two = attend_forward(query_heads, kv_heads[0], kv_heads[1], cross_allowed)
    mixed_two = mixed_two.reshape(row_count, D).astype(jnp.bfloat16)
    hidden_two = hidden_one + jnp.dot(mixed_two, cross_mats[3], preferred_element_type=jnp.float32)
    normed_three = layer_norm(hidden_two, vector_parts[4], vector_parts[5]).astype(jnp.bfloat16)
    pre_act = jnp.dot(normed_three, up_mat, preferred_element_type=jnp.float32) + bias_up
    activated = gelu_tanh(pre_act).astype(jnp.bfloat16)
    layer_output = hidden_two + (
        jnp.dot(activated, down_mat, preferred_element_type=jnp.float32) + vector_parts[6]
    )
    valid_rows = (positions[None, :] < suffix_len[:, None]).astype(jnp.float32)
    seed_rows = (
        cotangent.reshape(EX_DEV, SUF, D).astype(jnp.float32) * valid_rows[:, :, None]
    ).reshape(row_count, D)
    seed_low = seed_rows.astype(jnp.bfloat16)
    bias_down_grad = jnp.sum(seed_low.astype(jnp.float32), axis=0)
    down_grad = jnp.einsum("rf,rd->fd", activated, seed_low, preferred_element_type=jnp.float32)
    activated_grad = jnp.einsum("rd,fd->rf", seed_low, down_mat, preferred_element_type=jnp.float32)
    _, gelu_back = jax.vjp(gelu_tanh, pre_act)
    pre_grad = gelu_back(activated_grad)[0].astype(jnp.bfloat16)
    bias_up_grad = jnp.sum(pre_grad.astype(jnp.float32), axis=0)
    up_grad = jnp.einsum("rd,rf->df", normed_three, pre_grad, preferred_element_type=jnp.float32)
    normed_three_grad = jnp.einsum(
        "rf,df->rd", pre_grad, up_mat, preferred_element_type=jnp.float32
    )
    _, norm_three_back = jax.vjp(layer_norm, hidden_two, vector_parts[4], vector_parts[5])
    through_three, gain_three_grad, shift_three_grad = norm_three_back(normed_three_grad)
    hidden_two_grad = seed_rows + through_three
    feed_flat = jnp.concatenate([up_grad.reshape(-1), down_grad.reshape(-1)])
    branch_two = hidden_two_grad.astype(jnp.bfloat16)
    cross_out_grad = jnp.einsum(
        "rd,re->de", mixed_two, branch_two, preferred_element_type=jnp.float32
    )
    mixed_two_grad = jnp.einsum(
        "re,de->rd", branch_two, cross_mats[3], preferred_element_type=jnp.float32
    ).astype(jnp.bfloat16)
    query_two_grad, key_two_grad, value_two_grad = attend_backward(
        query_heads,
        kv_heads[0],
        kv_heads[1],
        cross_allowed,
        totals_two,
        mixed_two_grad.reshape(EX_DEV, SUF, H, HD),
    )
    cross_query_grad = query_two_grad.reshape(row_count, D).astype(jnp.bfloat16)
    cross_kv_grad = (
        jnp.stack([key_two_grad, value_two_grad])
        .reshape(2, EX_DEV * MEMLEN, D)
        .astype(jnp.bfloat16)
    )
    query_weight_grad = jnp.einsum(
        "rd,re->de", normed_two, cross_query_grad, preferred_element_type=jnp.float32
    )
    kv_weight_grad = jnp.einsum(
        "rd,jre->jde", memory_rows, cross_kv_grad, preferred_element_type=jnp.float32
    )
    normed_two_grad = jnp.einsum(
        "re,de->rd", cross_query_grad, cross_mats[0], preferred_element_type=jnp.float32
    )
    memory_local_grad = jnp.einsum(
        "jre,jde->rd", cross_kv_grad, cross_mats[1:3], preferred_element_type=jnp.float32
    )
    memory_gradient = lax.all_to_all(
        memory_local_grad.reshape(1, EX_DEV, MEMLEN, D),
        "dp",
        split_axis=2,
        concat_axis=1,
        tiled=True,
    )
    _, norm_two_back = jax.vjp(layer_norm, hidden_one, vector_parts[2], vector_parts[3])
    through_two, gain_two_grad, shift_two_grad = norm_two_back(normed_two_grad)
    hidden_one_grad = hidden_two_grad + through_two
    cross_flat = jnp.concatenate(
        [query_weight_grad[None], kv_weight_grad, cross_out_grad[None]], axis=0
    ).reshape(-1)
    branch_one = hidden_one_grad.astype(jnp.bfloat16)
    self_out_grad = jnp.einsum(
        "rd,re->de", mixed_one, branch_one, preferred_element_type=jnp.float32
    )
    mixed_one_grad = jnp.einsum(
        "re,de->rd", branch_one, self_mats[3], preferred_element_type=jnp.float32
    ).astype(jnp.bfloat16)
    query_one_grad, key_one_grad, value_one_grad = attend_backward(
        self_heads[0],
        self_heads[1],
        self_heads[2],
        self_allowed,
        totals_one,
        mixed_one_grad.reshape(EX_DEV, SUF, H, HD),
    )
    self_qkv_grad = (
        jnp.stack([query_one_grad, key_one_grad, value_one_grad])
        .reshape(3, row_count, D)
        .astype(jnp.bfloat16)
    )
    qkv_weight_grad = jnp.einsum(
        "rd,jre->jde", normed_one, self_qkv_grad, preferred_element_type=jnp.float32
    )
    normed_one_grad = jnp.einsum(
        "jre,jde->rd", self_qkv_grad, self_mats[0:3], preferred_element_type=jnp.float32
    )
    _, norm_one_back = jax.vjp(layer_norm, inputs, vector_parts[0], vector_parts[1])
    through_one, gain_one_grad, shift_one_grad = norm_one_back(normed_one_grad)
    suffix_gradient = (hidden_one_grad + through_one).reshape(1, EX_DEV, SUF, D)
    self_flat = jnp.concatenate([qkv_weight_grad, self_out_grad[None]], axis=0).reshape(-1)
    owners = lax.axis_size(("dp", "fsdp"))
    joined = jnp.concatenate(
        [
            self_flat.reshape(owners, attn_shard),
            cross_flat.reshape(owners, attn_shard),
            feed_flat.reshape(owners, feed_shard),
        ],
        axis=1,
    ).reshape(-1)
    owned = lax.psum_scatter(joined, ("dp", "fsdp"), scatter_dimension=0, tiled=True)
    self_total = owned[:attn_shard]
    cross_total = owned[attn_shard : 2 * attn_shard]
    feed_total = owned[2 * attn_shard :]
    vector_partial = jnp.concatenate(
        [
            gain_one_grad,
            shift_one_grad,
            gain_two_grad,
            shift_two_grad,
            gain_three_grad,
            shift_three_grad,
            bias_down_grad,
            bias_up_grad,
        ]
    )
    shard_index = lax.axis_index(("dp", "fsdp"))
    attn_offset = shard_index * attn_shard
    feed_offset = shard_index * feed_shard
    grad_squares = jnp.concatenate(
        [
            segment_sums(self_total * self_total, attn_offset, D * D, 4),
            segment_sums(cross_total * cross_total, attn_offset, D * D, 4),
            segment_sums(feed_total * feed_total, feed_offset, D * FF, 2),
        ]
    )
    weight_squares = jnp.concatenate(
        [
            segment_sums(self_weights * self_weights, attn_offset, D * D, 4),
            segment_sums(cross_weights * cross_weights, attn_offset, D * D, 4),
            segment_sums(feed_weights * feed_weights, feed_offset, D * FF, 2),
        ]
    )
    vector_total, grad_summed, weight_summed = lax.psum(
        (vector_partial, grad_squares, weight_squares), ("dp", "fsdp")
    )
    squared_total = jnp.sum(grad_summed) + jnp.sum(vector_total * vector_total)
    global_norm = jnp.sqrt(squared_total)
    clip_factor = jnp.minimum(1.0, 1.0 / global_norm)
    self_momentum, self_variance, self_ratio = lamb_step(
        self_weights, self_total, self_moment, self_second, clip_factor
    )
    cross_momentum, cross_variance, cross_ratio = lamb_step(
        cross_weights, cross_total, cross_moment, cross_second, clip_factor
    )
    feed_momentum, feed_variance, feed_ratio = lamb_step(
        feed_weights, feed_total, feed_moment, feed_second, clip_factor
    )
    ratio_squares = jnp.concatenate(
        [
            segment_sums(self_ratio * self_ratio, attn_offset, D * D, 4),
            segment_sums(cross_ratio * cross_ratio, attn_offset, D * D, 4),
            segment_sums(feed_ratio * feed_ratio, feed_offset, D * FF, 2),
        ]
    )
    update_summed = lax.psum(ratio_squares, ("dp", "fsdp"))
    weight_norms = jnp.sqrt(weight_summed)
    ratio_norms = jnp.sqrt(update_summed)
    trust_ratio = weight_norms / (ratio_norms + trust_eps)
    self_master = (
        self_weights
        - learn_rate * segment_spread(trust_ratio[0:4], attn_offset, attn_shard, D * D) * self_ratio
    )
    cross_master = (
        cross_weights
        - learn_rate
        * segment_spread(trust_ratio[4:8], attn_offset, attn_shard, D * D)
        * cross_ratio
    )
    feed_master = (
        feed_weights
        - learn_rate
        * segment_spread(trust_ratio[8:10], feed_offset, feed_shard, D * FF)
        * feed_ratio
    )
    vector_momentum, vector_variance, vector_ratio = lamb_step(
        vectors, vector_total, vector_moment, vector_second, clip_factor
    )
    edges = [0, D, 2 * D, 3 * D, 4 * D, 5 * D, 6 * D, 7 * D, 7 * D + FF]
    vector_wn = []
    vector_rn = []
    new_pieces = []
    for segment in range(8):
        weight_part = vectors[edges[segment] : edges[segment + 1]]
        ratio_part = vector_ratio[edges[segment] : edges[segment + 1]]
        weight_norm = jnp.sqrt(jnp.sum(weight_part * weight_part))
        ratio_norm = jnp.sqrt(jnp.sum(ratio_part * ratio_part))
        piece_trust = weight_norm / (ratio_norm + trust_eps)
        vector_wn.append(weight_norm)
        vector_rn.append(ratio_norm)
        new_pieces.append(weight_part - learn_rate * piece_trust * ratio_part)
    vector_master = jnp.concatenate(new_pieces)
    tensor_norms = jnp.stack(
        [
            jnp.concatenate([weight_norms, jnp.stack(vector_wn)]),
            jnp.concatenate([ratio_norms, jnp.stack(vector_rn)]),
        ]
    )
    return (
        layer_output.reshape(1, EX_DEV, SUF, D),
        suffix_gradient,
        memory_gradient,
        self_total,
        self_momentum,
        self_variance,
        self_master,
        cross_total,
        cross_momentum,
        cross_variance,
        cross_master,
        feed_total,
        feed_momentum,
        feed_variance,
        feed_master,
        vector_total,
        vector_momentum,
        vector_variance,
        vector_master,
        tensor_norms,
        global_norm,
    )


BF = jnp.bfloat16
F32 = jnp.float32
MESH = pl.DeviceIdType.MESH
NZ = 4


def place():
    dp, fs = lax.axis_index("dp"), lax.axis_index("fsdp")
    return dp, fs, dp // 2, dp % 2, fs // 2, fs % 2


def peer_id(z, y, x, c):
    return (z * 2 + y, x * 2 + c)


def greet(ids):
    bar = pltpu.get_barrier_semaphore()
    for where in ids:
        pl.semaphore_signal(bar, inc=1, device_id=where, device_id_type=MESH)
    pl.semaphore_wait(bar, len(ids))


class Copies:
    def __init__(self, send, recv, local):
        self.send, self.recv, self.local = send, recv, local
        self.remotes, self.locals = 0, 0
        self.open = []

    def remote(self, src, dst, where):
        i = self.remotes
        self.remotes += 1
        cp = pltpu.make_async_remote_copy(
            src_ref=src,
            dst_ref=dst,
            send_sem=self.send.at[i],
            recv_sem=self.recv.at[i],
            device_id=where,
            device_id_type=MESH,
        )
        cp.start()
        self.open.append(cp)
        return cp

    def here(self, src, dst):
        cp = pltpu.make_async_copy(src, dst, self.local.at[self.locals])
        self.locals += 1
        cp.start()
        return cp

    def drain(self):
        for cp in self.open:
            cp.wait_send()


def gather_kernel(
    self_in, cross_in, feed_in, mem_in, self_out, cross_out, feed_out, mem_out, send, recv, local
):
    dp, fs, z, y, x, c = place()
    ndp = mem_out.shape[1]
    ex = mem_out.shape[0]
    to_y, to_x, to_c = peer_id(z, 1 - y, x, c), peer_id(z, y, 1 - x, c), peer_id(z, y, x, 1 - c)
    greet([((dp + k) % ndp, fs) for k in range(1, ndp)] + [to_x, to_c])
    cp = Copies(send, recv, local)

    chunks = []
    for src, dst, js in (
        (self_in, self_out, (0, 1)),
        (cross_in, cross_out, (0, 1)),
        (feed_in, feed_out, (0, 2)),
        (feed_in, feed_out, (2, 2)),
    ):
        rows = src.shape[1]
        cut = rows * 2 // 3
        chunks.append((src, dst, pl.ds(*js), pl.ds(0, cut), pl.ds(cut, rows - cut)))

    own = [cp.here(chunk[0].at[chunk[2]], chunk[1].at[z, y, x, c, chunk[2]]) for chunk in chunks]
    own_mem = cp.here(mem_in.at[pl.ds(ex * dp, ex)], mem_out.at[:, dp])

    zc, s2, s3, s4 = {}, {}, {}, {}

    def send_z(t):
        src, dst, js, r0, r1 = chunks[t]
        for k in range(1, NZ):
            zc[t, k] = cp.remote(
                src.at[js], dst.at[z, y, x, c, js], peer_id((z + k) % NZ, y, x, c)
            )

    def send_2(t, k):
        src, dst, js, r0, r1 = chunks[t]
        zz = (z + NZ - k) % NZ
        for part, rows, where in ((0, r0, to_y), (1, r1, to_x)):
            here = src.at[js, rows] if k == 0 else dst.at[zz, y, x, c, js, rows]
            s2[t, k, part] = cp.remote(here, dst.at[zz, y, x, c, js, rows], where)

    def send_3(t):
        src, dst, js, r0, r1 = chunks[t]
        s3[t, 0] = cp.remote(
            dst.at[:, :, x, c, js, r0], dst.at[:, :, x, c, js, r0], to_x
        )
        s3[t, 1] = cp.remote(
            dst.at[:, y, :, c, js, r1], dst.at[:, y, :, c, js, r1], to_y
        )

    def send_4(t):
        src, dst, js, r0, r1 = chunks[t]
        s4[t] = cp.remote(dst.at[:, :, :, c, js], dst.at[:, :, :, c, js], to_c)

    n = len(chunks)
    for t in range(n):
        send_z(t)
        send_2(t, 0)
    mem = [
        cp.remote(
            mem_in.at[pl.ds(ex * ((dp + k) % ndp), ex)],
            mem_out.at[:, dp],
            ((dp + k) % ndp, fs),
        )
        for k in range(1, ndp)
    ]
    for t in range(n + 2):
        if t < n:
            for k in range(1, NZ):
                zc[t, k].wait_recv()
                send_2(t, k)
        if 1 <= t <= n:
            own[t - 1].wait()
            for k in range(NZ):
                for part in (0, 1):
                    s2[t - 1, k, part].wait_recv()
            send_3(t - 1)
        if t >= 2:
            s3[t - 2, 0].wait_recv()
            s3[t - 2, 1].wait_recv()
            send_4(t - 2)
    for t in range(n):
        s4[t].wait_recv()
    own_mem.wait()
    for one in mem:
        one.wait_recv()
    cp.drain()


def gather_all(self_in, cross_in, feed_in, mem_in, ndp):
    any_space = pl.BlockSpec(memory_space=pl.ANY)
    shards_of = lambda a: jax.ShapeDtypeStruct((NZ, 2, 2, 2) + a.shape, BF)
    ex = mem_in.shape[0] // ndp
    return pl.pallas_call(
        gather_kernel,
        out_shape=[
            shards_of(self_in),
            shards_of(cross_in),
            shards_of(feed_in),
            jax.ShapeDtypeStruct((ex, ndp) + mem_in.shape[1:], BF),
        ],
        in_specs=[any_space] * 4,
        out_specs=[any_space] * 4,
        scratch_shapes=[
            pltpu.SemaphoreType.DMA((72,)),
            pltpu.SemaphoreType.DMA((72,)),
            pltpu.SemaphoreType.DMA((8,)),
        ],
        compiler_params=pltpu.CompilerParams(collective_id=1, has_side_effects=True),
        name="gather_all",
    )(self_in, cross_in, feed_in, mem_in)


def squares(v):
    rows, cols = v.shape
    w = jnp.sum((v * v).reshape(rows // 8, 8, cols), axis=0)
    total = w[:, 0:128]
    for i in range(1, cols // 128):
        total = total + w[:, i * 128 : (i + 1) * 128]
    return total


def sum_everywhere(cp, mine, slots_a, slots_b, dp, fs):
    nfs, ndp = slots_a.shape[0], slots_b.shape[0]
    slots_a[fs] = mine
    got = [
        cp.remote(slots_a.at[fs], slots_a.at[fs], (dp, (fs + k) % nfs)) for k in range(1, nfs)
    ]
    for one in got:
        one.wait_recv()
    total = slots_a[0]
    for k in range(1, nfs):
        total = total + slots_a[k]
    slots_b[dp] = total
    got = [
        cp.remote(slots_b.at[dp], slots_b.at[dp], ((dp + k) % ndp, fs)) for k in range(1, ndp)
    ]
    for one in got:
        one.wait_recv()
    total = slots_b[0]
    for k in range(1, ndp):
        total = total + slots_b[k]
    return total


def scatter_kernel(
    qkv_g, out_g, cq_g, ckv_g, co_g, up_g, dn_g, mem_g, vec,
    self_t, cross_t, feed_t, mem_t, vec_t, sq_t,
    send, recv, local,
    acc_s, acc_c, acc_f0, acc_f1, r1_s, r1_c, r1_f0, r1_f1,
    r2a_s, r2a_c, r2a_f0, r2a_f1, r2b_s, r2b_c, r2b_f0, r2b_f1,
    r3a_s, r3a_c, r3a_f0, r3a_f1, r3b_s, r3b_c, r3b_f0, r3b_f1,
    rz_s, rz_c, rz_f0, rz_f1,
    v_send, v_recv, v_z, slots_a, slots_b,
):
    dp, fs, z, y, x, c = place()
    ndp = mem_g.shape[1]
    ex = mem_g.shape[0]
    to_y, to_x, to_c = peer_id(z, 1 - y, x, c), peer_id(z, y, 1 - x, c), peer_id(z, y, x, 1 - c)
    nfs = slots_a.shape[0]
    greet(
        [((dp + k) % ndp, fs) for k in range(1, ndp)] + [(dp, (fs + k) % nfs) for k in range(1, nfs)]
    )
    cp = Copies(send, recv, local)

    def self_src(zz, j, cc):
        return qkv_g.at[zz, :, :, cc] if zz < 3 else out_g.at[:, :, cc]

    def cross_src(zz, j, cc):
        if zz == 0:
            return cq_g.at[:, :, cc]
        return ckv_g.at[zz - 1, :, :, cc] if zz < 3 else co_g.at[:, :, cc]

    def feed_src(first):
        def src(zz, j, cc):
            if zz < 2:
                return up_g.at[first + j, zz, :, :, cc]
            return dn_g.at[zz - 2, :, :, cc, first + j]

        return src

    chunks = (
        (feed_src(0), acc_f0, r1_f0, r2a_f0, r2b_f0, r3a_f0, r3b_f0, rz_f0),
        (feed_src(2), acc_f1, r1_f1, r2a_f1, r2b_f1, r3a_f1, r3b_f1, rz_f1),
        (cross_src, acc_c, r1_c, r2a_c, r2b_c, r3a_c, r3b_c, rz_c),
        (self_src, acc_s, r1_s, r2a_s, r2b_s, r3a_s, r3b_s, rz_s),
    )
    n = len(chunks)
    sc, sl, s1, s2, sz = {}, {}, {}, {}, {}

    vcp = cp.remote(vec, v_recv.at[0], to_c)
    for t, (src, acc, r1, *_) in enumerate(chunks):
        for zz in range(NZ):
            for j in range(acc.shape[3]):
                sc[t, zz, j] = cp.remote(src(zz, j, 1 - c), r1.at[zz, :, :, j], to_c)
                sl[t, zz, j] = cp.here(src(zz, j, c), acc.at[zz, :, :, j])
    own_mem = cp.here(mem_g.at[:, dp], mem_t.at[pl.ds(ex * dp, ex)])
    mem = [
        cp.remote(mem_g.at[:, (dp + k) % ndp], mem_t.at[pl.ds(ex * dp, ex)], ((dp + k) % ndp, fs))
        for k in range(1, ndp)
    ]

    def cuts(acc):
        rows = acc.shape[4]
        cut = rows * 2 // 3
        return pl.ds(0, cut), pl.ds(cut, rows - cut)

    def add_c(acc, r1, fixed_y, fixed_x, rows):
        def body(i, _):
            zz, o = i // 2, i % 2
            yy = o if fixed_y is None else fixed_y
            xx = o if fixed_x is None else fixed_x
            for j in range(acc.shape[3]):
                acc[zz, yy, xx, j, rows] = acc[zz, yy, xx, j, rows] + r1[zz, yy, xx, j, rows]
            return 0

        lax.fori_loop(0, NZ * 2, body, 0)

    def phase_c(t):
        src, acc, r1, r2a, r2b, *_ = chunks[t]
        r0, r1_rows = cuts(acc)
        for zz in range(NZ):
            for j in range(acc.shape[3]):
                sc[t, zz, j].wait_recv()
                sl[t, zz, j].wait()
        add_c(acc, r1, None, 1 - x, r0)
        s1[t, 0] = cp.remote(acc.at[:, :, 1 - x, :, r0], r2a, to_x)
        add_c(acc, r1, 1 - y, None, r1_rows)
        s1[t, 1] = cp.remote(acc.at[:, 1 - y, :, :, r1_rows], r2b, to_y)
        add_c(acc, r1, None, x, r0)
        add_c(acc, r1, y, None, r1_rows)

    def phase_1(t):
        src, acc, r1, r2a, r2b, r3a, r3b, rz = chunks[t]
        r0, r1_rows = cuts(acc)

        def body_a(yy):
            def body(zz, _):
                for j in range(acc.shape[3]):
                    acc[zz, yy, x, j, r0] = acc[zz, yy, x, j, r0] + r2a[zz, yy, j]
                return 0

            return body

        def body_b(xx):
            def body(zz, _):
                for j in range(acc.shape[3]):
                    acc[zz, y, xx, j, r1_rows] = acc[zz, y, xx, j, r1_rows] + r2b[zz, xx, j]
                return 0

            return body

        s1[t, 0].wait_recv()
        lax.fori_loop(0, NZ, body_a(1 - y), 0)
        s2[t, 0] = cp.remote(acc.at[:, 1 - y, x, :, r0], r3a, to_y)
        s1[t, 1].wait_recv()
        lax.fori_loop(0, NZ, body_b(1 - x), 0)
        s2[t, 1] = cp.remote(acc.at[:, y, 1 - x, :, r1_rows], r3b, to_x)
        lax.fori_loop(0, NZ, body_a(y), 0)
        lax.fori_loop(0, NZ, body_b(x), 0)

    def phase_2(t):
        src, acc, r1, r2a, r2b, r3a, r3b, rz = chunks[t]
        r0, r1_rows = cuts(acc)
        s2[t, 0].wait_recv()
        s2[t, 1].wait_recv()

        def body(zz, _):
            for j in range(acc.shape[3]):
                acc[zz, y, x, j, r0] = acc[zz, y, x, j, r0] + r3a[zz, j]
                acc[zz, y, x, j, r1_rows] = acc[zz, y, x, j, r1_rows] + r3b[zz, j]
            return 0

        lax.fori_loop(0, NZ, body, 0)
        for k in range(1, NZ):
            zt = (z + k) % NZ
            sz[t, k] = cp.remote(acc.at[zt, y, x], rz.at[k - 1], peer_id(zt, y, x, c))

    sums = []

    def phase_z(t, out, first):
        src, acc, r1, r2a, r2b, r3a, r3b, rz = chunks[t]
        for k in range(1, NZ):
            sz[t, k].wait_recv()
        for j in range(acc.shape[3]):
            total = acc[z, y, x, j].astype(F32)
            for k in range(1, NZ):
                total = total + rz[k - 1, j].astype(F32)
            out[first + j] = total
            sums.append(squares(total))

    def vec_step(i):
        nonlocal vcp
        vcp.wait_recv()
        if i < 3:
            before = vec[...] if i == 0 else v_send[i - 1]
            v_send[i] = before + v_recv[i]
            if i < 2:
                vcp = cp.remote(v_send.at[i], v_recv.at[i + 1], (to_x, to_y)[i])

    for t in range(n + 3):
        if t < n:
            phase_c(t)
        if t < 3:
            vec_step(t)
        if t == 2:
            v_z[z] = v_send[2]
            vz = [
                cp.remote(v_send.at[2], v_z.at[z], peer_id((z + k) % NZ, y, x, c))
                for k in range(1, NZ)
            ]
        if 1 <= t <= n:
            phase_1(t - 1)
        if 2 <= t <= n + 1:
            phase_2(t - 2)
        if t >= 3:
            phase_z(t - 3, (feed_t, feed_t, cross_t, self_t)[t - 3], (0, 2, 0, 0)[t - 3])
    for one in vz:
        one.wait_recv()
    vec_t[...] = (v_z[0] + v_z[1]) + (v_z[2] + v_z[3])
    total = sums[0]
    for one in sums[1:]:
        total = total + one
    sq_t[...] = sum_everywhere(cp, total, slots_a, slots_b, dp, fs)
    own_mem.wait()
    for one in mem:
        one.wait_recv()
    cp.drain()


def scatter_all(grads, mem_g, vec, rows_a, rows_f, ndp, nfs):
    any_space = pl.BlockSpec(memory_space=pl.ANY)
    vmem = pl.BlockSpec(memory_space=pltpu.VMEM)
    ex, _, pos, width = mem_g.shape
    kinds = ((1, rows_a), (1, rows_a), (2, rows_f), (2, rows_f))
    acc = [pltpu.VMEM((NZ, 2, 2, j, r, width), BF) for j, r in kinds]
    r2a = [pltpu.VMEM((NZ, 2, j, r * 2 // 3, width), BF) for j, r in kinds]
    r2b = [pltpu.VMEM((NZ, 2, j, r - r * 2 // 3, width), BF) for j, r in kinds]
    r3a = [pltpu.VMEM((NZ, j, r * 2 // 3, width), BF) for j, r in kinds]
    r3b = [pltpu.VMEM((NZ, j, r - r * 2 // 3, width), BF) for j, r in kinds]
    rz = [pltpu.VMEM((NZ - 1, j, r, width), BF) for j, r in kinds]
    return pl.pallas_call(
        scatter_kernel,
        out_shape=[
            jax.ShapeDtypeStruct((1, rows_a, width), F32),
            jax.ShapeDtypeStruct((1, rows_a, width), F32),
            jax.ShapeDtypeStruct((4, rows_f, width), F32),
            jax.ShapeDtypeStruct((ndp * ex, pos, width), BF),
            jax.ShapeDtypeStruct(vec.shape, F32),
            jax.ShapeDtypeStruct((8, 128), F32),
        ],
        in_specs=[any_space] * 8 + [vmem],
        out_specs=[vmem, vmem, vmem, any_space, vmem, vmem],
        scratch_shapes=[
            pltpu.SemaphoreType.DMA((80,)),
            pltpu.SemaphoreType.DMA((80,)),
            pltpu.SemaphoreType.DMA((32,)),
            *acc,
            *acc,
            *r2a,
            *r2b,
            *r3a,
            *r3b,
            *rz,
            pltpu.VMEM((3,) + vec.shape, F32),
            pltpu.VMEM((3,) + vec.shape, F32),
            pltpu.VMEM((NZ,) + vec.shape, F32),
            pltpu.VMEM((nfs, 8, 128), F32),
            pltpu.VMEM((ndp, 8, 128), F32),
        ],
        compiler_params=pltpu.CompilerParams(
            collective_id=2, has_side_effects=True, vmem_limit_bytes=58 << 20
        ),
        name="scatter_all",
    )(*grads, mem_g, vec)


def ratio_kernel(
    gs, gc, gf, ws, wc, wf, ms, mc, mf, vs, vc, vf, clip, out, send, recv, local, slots_a, slots_b
):
    dp, fs, z, y, x, c = place()
    nfs, ndp = slots_a.shape[0], slots_b.shape[0]
    greet(
        [((dp + k) % ndp, fs) for k in range(1, ndp)] + [(dp, (fs + k) % nfs) for k in range(1, nfs)]
    )
    cp = Copies(send, recv, local)
    factor = clip[0:1, 0:1]
    rows = lax.broadcasted_iota(jnp.int32, (32, 128), 0)
    tile = jnp.zeros((32, 128), F32)
    for g, w, m, v, row in (
        (gs, ws, ms, vs, z),
        (gc, wc, mc, vc, NZ + z),
        (gf, wf, mf, vf, 2 * NZ + z // 2),
    ):
        ratio = lamb_step(w[...], g[...], m[...], v[...], factor)[2]
        for first, a in ((0, ratio), (16, w[...])):
            part = jnp.sum(a * a, axis=0, keepdims=True)
            tile = tile + jnp.where(rows == first + row, part, 0.0)
    out[...] = sum_everywhere(cp, tile, slots_a, slots_b, dp, fs)
    cp.drain()


def ratio_all(args, clip, ndp, nfs):
    vmem = pl.BlockSpec(memory_space=pltpu.VMEM)
    return pl.pallas_call(
        ratio_kernel,
        out_shape=jax.ShapeDtypeStruct((32, 128), F32),
        in_specs=[vmem] * 13,
        out_specs=vmem,
        scratch_shapes=[
            pltpu.SemaphoreType.DMA((16,)),
            pltpu.SemaphoreType.DMA((16,)),
            pltpu.SemaphoreType.DMA((1,)),
            pltpu.VMEM((nfs, 32, 128), F32),
            pltpu.VMEM((ndp, 32, 128), F32),
        ],
        compiler_params=pltpu.CompilerParams(
            collective_id=3, has_side_effects=True, vmem_limit_bytes=40 << 20
        ),
        name="ratio_all",
    )(*args, clip)


def fast_shards(
    suffix,
    memory,
    prefix_lengths,
    suffix_lengths,
    cotangent,
    self_weights,
    self_moment,
    self_second,
    cross_weights,
    cross_moment,
    cross_second,
    feed_weights,
    feed_moment,
    feed_second,
    vectors,
    vector_moment,
    vector_second,
):
    row_count = EX_DEV * SUF
    ndp, nfs = lax.axis_size("dp"), lax.axis_size("fsdp")
    owners = ndp * nfs
    attn_shard, feed_shard = self_weights.shape[0], feed_weights.shape[0]
    rows_a, rows_f = attn_shard // D, feed_shard // (4 * D)
    shard_index = lax.axis_index(("dp", "fsdp"))
    feed_low = feed_weights.astype(BF)
    feed_in = jnp.where(
        shard_index < owners // 2,
        feed_low.reshape(rows_f, 4, D).transpose(1, 0, 2),
        feed_low.reshape(4, rows_f, D),
    )
    self_full, cross_full, feed_full, own_memory = gather_all(
        self_weights.astype(BF).reshape(1, rows_a, D),
        cross_weights.astype(BF).reshape(1, rows_a, D),
        feed_in,
        memory[0],
        ndp,
    )
    self_mats = self_full.reshape(4, D, D)
    cross_mats = cross_full.reshape(4, D, D)
    feed_full = feed_full.reshape(2, owners // 2, 4, rows_f, D)
    up_mats = feed_full[0].transpose(1, 0, 2, 3).reshape(4, D, D)
    down_mat = feed_full[1].reshape(FF, D)
    memory_rows = own_memory.reshape(EX_DEV * MEMLEN, D)
    vector_parts = [vectors[segment * D : (segment + 1) * D] for segment in range(7)]
    bias_up = vectors[7 * D :]
    suffix_len = suffix_lengths[0]
    prefix_len = prefix_lengths[0]
    positions = jnp.arange(SUF, dtype=jnp.int32)
    causal = positions[:, None] >= positions[None, :]
    self_allowed = (
        causal[None, None, :, :] & (positions[None, :] < suffix_len[:, None])[:, None, None, :]
    )
    memory_pos = jnp.arange(MEMLEN, dtype=jnp.int32)
    cross_allowed = (memory_pos[None, :] < (PATCH + prefix_len)[:, None])[:, None, None, :]
    inputs = suffix.reshape(row_count, D).astype(jnp.float32)
    normed_one = layer_norm(inputs, vector_parts[0], vector_parts[1]).astype(jnp.bfloat16)
    self_qkv = jnp.einsum(
        "rd,jde->jre", normed_one, self_mats[0:3], preferred_element_type=jnp.float32
    ).astype(jnp.bfloat16)
    self_heads = self_qkv.reshape(3, EX_DEV, SUF, H, HD)
    mixed_one, totals_one = attend_forward(
        self_heads[0], self_heads[1], self_heads[2], self_allowed
    )
    mixed_one = mixed_one.reshape(row_count, D).astype(jnp.bfloat16)
    hidden_one = inputs + jnp.dot(mixed_one, self_mats[3], preferred_element_type=jnp.float32)
    normed_two = layer_norm(hidden_one, vector_parts[2], vector_parts[3]).astype(jnp.bfloat16)
    cross_query = jnp.dot(normed_two, cross_mats[0], preferred_element_type=jnp.float32).astype(
        jnp.bfloat16
    )
    cross_kv = jnp.einsum(
        "rd,jde->jre", memory_rows, cross_mats[1:3], preferred_element_type=jnp.float32
    ).astype(jnp.bfloat16)
    query_heads = cross_query.reshape(EX_DEV, SUF, H, HD)
    kv_heads = cross_kv.reshape(2, EX_DEV, MEMLEN, H, HD)
    mixed_two, totals_two = attend_forward(query_heads, kv_heads[0], kv_heads[1], cross_allowed)
    mixed_two = mixed_two.reshape(row_count, D).astype(jnp.bfloat16)
    hidden_two = hidden_one + jnp.dot(mixed_two, cross_mats[3], preferred_element_type=jnp.float32)
    normed_three = layer_norm(hidden_two, vector_parts[4], vector_parts[5]).astype(jnp.bfloat16)
    pre_act = (
        jnp.einsum(
            "rd,jde->jre", normed_three, up_mats, preferred_element_type=jnp.float32
        )
        + bias_up.reshape(4, 1, D)
    )
    activated = gelu_tanh(pre_act).astype(jnp.bfloat16)
    layer_output = hidden_two + (
        jnp.einsum(
            "jre,jed->rd", activated, down_mat.reshape(4, D, D), preferred_element_type=jnp.float32
        )
        + vector_parts[6]
    )
    valid_rows = (positions[None, :] < suffix_len[:, None]).astype(jnp.float32)
    seed_rows = (
        cotangent.reshape(EX_DEV, SUF, D).astype(jnp.float32) * valid_rows[:, :, None]
    ).reshape(row_count, D)
    seed_low = seed_rows.astype(jnp.bfloat16)
    bias_down_grad = jnp.sum(seed_low.astype(jnp.float32), axis=0)
    down_grad = jnp.einsum(
        "jre,rd->jed", activated, seed_low, preferred_element_type=jnp.float32
    ).astype(BF)
    activated_grad = jnp.einsum(
        "rd,jed->jre", seed_low, down_mat.reshape(4, D, D), preferred_element_type=jnp.float32
    )
    _, gelu_back = jax.vjp(gelu_tanh, pre_act)
    pre_grad = gelu_back(activated_grad)[0].astype(jnp.bfloat16)
    bias_up_grad = jnp.sum(pre_grad.astype(jnp.float32), axis=1).reshape(FF)
    up_grad = jnp.einsum(
        "rd,jre->jde", normed_three, pre_grad, preferred_element_type=jnp.float32
    ).astype(BF)
    normed_three_grad = jnp.einsum(
        "jre,jde->rd", pre_grad, up_mats, preferred_element_type=jnp.float32
    )
    _, norm_three_back = jax.vjp(layer_norm, hidden_two, vector_parts[4], vector_parts[5])
    through_three, gain_three_grad, shift_three_grad = norm_three_back(normed_three_grad)
    hidden_two_grad = seed_rows + through_three
    branch_two = hidden_two_grad.astype(jnp.bfloat16)
    cross_out_grad = jnp.einsum(
        "rd,re->de", mixed_two, branch_two, preferred_element_type=jnp.float32
    ).astype(BF)
    mixed_two_grad = jnp.einsum(
        "re,de->rd", branch_two, cross_mats[3], preferred_element_type=jnp.float32
    ).astype(jnp.bfloat16)
    query_two_grad, key_two_grad, value_two_grad = attend_backward(
        query_heads,
        kv_heads[0],
        kv_heads[1],
        cross_allowed,
        totals_two,
        mixed_two_grad.reshape(EX_DEV, SUF, H, HD),
    )
    cross_query_grad = query_two_grad.reshape(row_count, D).astype(jnp.bfloat16)
    cross_kv_grad = (
        jnp.stack([key_two_grad, value_two_grad])
        .reshape(2, EX_DEV * MEMLEN, D)
        .astype(jnp.bfloat16)
    )
    query_weight_grad = jnp.einsum(
        "rd,re->de", normed_two, cross_query_grad, preferred_element_type=jnp.float32
    ).astype(BF)
    kv_weight_grad = jnp.einsum(
        "rd,jre->jde", memory_rows, cross_kv_grad, preferred_element_type=jnp.float32
    ).astype(BF)
    normed_two_grad = jnp.einsum(
        "re,de->rd", cross_query_grad, cross_mats[0], preferred_element_type=jnp.float32
    )
    memory_local_grad = jnp.einsum(
        "jre,jde->rd", cross_kv_grad, cross_mats[1:3], preferred_element_type=jnp.float32
    ).astype(BF)
    _, norm_two_back = jax.vjp(layer_norm, hidden_one, vector_parts[2], vector_parts[3])
    through_two, gain_two_grad, shift_two_grad = norm_two_back(normed_two_grad)
    hidden_one_grad = hidden_two_grad + through_two
    branch_one = hidden_one_grad.astype(jnp.bfloat16)
    self_out_grad = jnp.einsum(
        "rd,re->de", mixed_one, branch_one, preferred_element_type=jnp.float32
    ).astype(BF)
    mixed_one_grad = jnp.einsum(
        "re,de->rd", branch_one, self_mats[3], preferred_element_type=jnp.float32
    ).astype(jnp.bfloat16)
    query_one_grad, key_one_grad, value_one_grad = attend_backward(
        self_heads[0],
        self_heads[1],
        self_heads[2],
        self_allowed,
        totals_one,
        mixed_one_grad.reshape(EX_DEV, SUF, H, HD),
    )
    self_qkv_grad = (
        jnp.stack([query_one_grad, key_one_grad, value_one_grad])
        .reshape(3, row_count, D)
        .astype(jnp.bfloat16)
    )
    qkv_weight_grad = jnp.einsum(
        "rd,jre->jde", normed_one, self_qkv_grad, preferred_element_type=jnp.float32
    ).astype(BF)
    normed_one_grad = jnp.einsum(
        "jre,jde->rd", self_qkv_grad, self_mats[0:3], preferred_element_type=jnp.float32
    )
    _, norm_one_back = jax.vjp(layer_norm, inputs, vector_parts[0], vector_parts[1])
    through_one, gain_one_grad, shift_one_grad = norm_one_back(normed_one_grad)
    suffix_gradient = (hidden_one_grad + through_one).reshape(1, EX_DEV, SUF, D)
    vector_partial = jnp.concatenate(
        [
            gain_one_grad,
            shift_one_grad,
            gain_two_grad,
            shift_two_grad,
            gain_three_grad,
            shift_three_grad,
            bias_down_grad,
            bias_up_grad,
        ]
    )
    vec_rows = vectors.shape[0] // 128
    vec_pad = (vec_rows + 7) // 8 * 8
    vector_in = jnp.pad(vector_partial.reshape(vec_rows, 128), ((0, vec_pad - vec_rows), (0, 0)))
    split = (2, 2, 2)
    self_total, cross_total, feed_total, memory_back, vec_sum, squared = scatter_all(
        (
            qkv_weight_grad.reshape((3,) + split + (rows_a, D)),
            self_out_grad.reshape(split + (rows_a, D)),
            query_weight_grad.reshape(split + (rows_a, D)),
            kv_weight_grad.reshape((2,) + split + (rows_a, D)),
            cross_out_grad.reshape(split + (rows_a, D)),
            up_grad.reshape((4, 2) + split + (rows_f, D)),
            down_grad.reshape((2,) + split + (4, rows_f, D)),
        ),
        memory_local_grad.reshape(EX_DEV, ndp, MEMLEN // ndp, D),
        vector_in,
        rows_a,
        rows_f,
        ndp,
        nfs,
    )
    memory_gradient = memory_back.astype(F32)[None]
    self_total = self_total.reshape(-1)
    cross_total = cross_total.reshape(-1)
    feed_total = jnp.where(
        shard_index < owners // 2, feed_total.transpose(1, 0, 2).reshape(-1), feed_total.reshape(-1)
    )
    vector_total = vec_sum[:vec_rows].reshape(-1)
    squared_total = jnp.sum(squared) + jnp.sum(vector_total * vector_total)
    global_norm = jnp.sqrt(squared_total)
    clip_factor = jnp.minimum(1.0, 1.0 / global_norm)
    flat = lambda *group: [a.reshape(-1, 128) for a in group]
    sums = ratio_all(
        flat(
            self_total, cross_total, feed_total,
            self_weights, cross_weights, feed_weights,
            self_moment, cross_moment, feed_moment,
            self_second, cross_second, feed_second,
        ),
        jnp.broadcast_to(clip_factor, (8, 128)),
        ndp,
        nfs,
    )
    norms = jnp.sqrt(jnp.sum(sums, axis=1))
    ratio_norms, weight_norms = norms[0:10], norms[16:26]
    trust_ratio = weight_norms / (ratio_norms + trust_eps)
    z = shard_index // 8
    new = []
    for weights, total, moment, second, row in (
        (self_weights, self_total, self_moment, self_second, z),
        (cross_weights, cross_total, cross_moment, cross_second, 4 + z),
        (feed_weights, feed_total, feed_moment, feed_second, 8 + z // 2),
    ):
        momentum, variance, ratio = lamb_step(weights, total, moment, second, clip_factor)
        new += [total, momentum, variance, weights - learn_rate * trust_ratio[row] * ratio]
    vector_momentum, vector_variance, vector_ratio = lamb_step(
        vectors, vector_total, vector_moment, vector_second, clip_factor
    )
    edges = [0, D, 2 * D, 3 * D, 4 * D, 5 * D, 6 * D, 7 * D, 7 * D + FF]
    vector_wn = []
    vector_rn = []
    new_pieces = []
    for segment in range(8):
        weight_part = vectors[edges[segment] : edges[segment + 1]]
        ratio_part = vector_ratio[edges[segment] : edges[segment + 1]]
        weight_norm = jnp.sqrt(jnp.sum(weight_part * weight_part))
        ratio_norm = jnp.sqrt(jnp.sum(ratio_part * ratio_part))
        piece_trust = weight_norm / (ratio_norm + trust_eps)
        vector_wn.append(weight_norm)
        vector_rn.append(ratio_norm)
        new_pieces.append(weight_part - learn_rate * piece_trust * ratio_part)
    vector_master = jnp.concatenate(new_pieces)
    tensor_norms = jnp.stack(
        [
            jnp.concatenate([weight_norms, jnp.stack(vector_wn)]),
            jnp.concatenate([ratio_norms, jnp.stack(vector_rn)]),
        ]
    )
    return (
        layer_output.reshape(1, EX_DEV, SUF, D),
        suffix_gradient,
        memory_gradient,
        *new,
        vector_total,
        vector_momentum,
        vector_variance,
        vector_master,
        tensor_norms,
        global_norm,
    )


def pick(mesh):
    if mesh.shape["dp"] == 8 and mesh.shape["fsdp"] == 4:
        return fast_shards
    return shards


def solution(mesh):
    return jax.shard_map(
        pick(mesh),
        mesh=mesh,
        in_specs=(
            P("fsdp", "dp", None, None),
            P("fsdp", None, "dp", None),
            P("fsdp", "dp"),
            P("fsdp", "dp"),
            P("fsdp", "dp", None, None),
            P(("dp", "fsdp")),
            P(("dp", "fsdp")),
            P(("dp", "fsdp")),
            P(("dp", "fsdp")),
            P(("dp", "fsdp")),
            P(("dp", "fsdp")),
            P(("dp", "fsdp")),
            P(("dp", "fsdp")),
            P(("dp", "fsdp")),
            P(),
            P(),
            P(),
        ),
        out_specs=(
            P("fsdp", "dp", None, None),
            P("fsdp", "dp", None, None),
            P("fsdp", None, "dp", None),
            P(("dp", "fsdp")),
            P(("dp", "fsdp")),
            P(("dp", "fsdp")),
            P(("dp", "fsdp")),
            P(("dp", "fsdp")),
            P(("dp", "fsdp")),
            P(("dp", "fsdp")),
            P(("dp", "fsdp")),
            P(("dp", "fsdp")),
            P(("dp", "fsdp")),
            P(("dp", "fsdp")),
            P(("dp", "fsdp")),
            P(),
            P(),
            P(),
            P(),
            P(),
            P(),
        ),
        check_vma=False,
    )
```

```python
import jax
import jax.numpy as jnp
from jax import lax
from jax.experimental import pallas as pl
from jax.experimental.pallas import tpu as pltpu
from jax.sharding import PartitionSpec as P

D = 768
H = 12
HD = 64
FF = 3072
PATCH = 196
SUF = 64
EX_DEV = 4
MEMLEN = 256


beta_one = 0.5
beta_two = 0.55
step_count = 5
learn_rate = 0.5
decay_weight = 0.01
adam_eps = 1e-06
norm_eps = 1e-06
trust_eps = 1e-06
masked_score = -1e30


def layer_norm(values, norm_gain, norm_shift):
    centred = values - jnp.mean(values, axis=-1, keepdims=True)
    spread = jnp.mean(centred * centred, axis=-1, keepdims=True)
    return centred * lax.rsqrt(spread + norm_eps) * norm_gain + norm_shift


def gelu_tanh(values):
    return jax.nn.gelu(values, approximate=True)


def attend_forward(query_heads, key_heads, value_heads, allowed):
    score_scale = HD ** (-0.5)
    scores = (
        jnp.einsum("bqhe,bkhe->bhqk", query_heads, key_heads, preferred_element_type=jnp.float32)
        * score_scale
    )
    scores = jnp.where(allowed, scores, masked_score)
    attention = jax.nn.softmax(scores, axis=-1)
    totals = jax.nn.logsumexp(scores, axis=-1)
    mixed_rows = jnp.einsum(
        "bhqk,bkhe->bqhe",
        attention.astype(jnp.bfloat16),
        value_heads,
        preferred_element_type=jnp.float32,
    )
    return (mixed_rows, totals)


def attend_backward(query_heads, key_heads, value_heads, allowed, totals, mixed_grad):
    score_scale = HD ** (-0.5)
    scores = (
        jnp.einsum("bqhe,bkhe->bhqk", query_heads, key_heads, preferred_element_type=jnp.float32)
        * score_scale
    )
    scores = jnp.where(allowed, scores, masked_score)
    attention = jnp.exp(scores - totals[..., None])
    value_grad = jnp.einsum(
        "bhqk,bqhe->bkhe",
        attention.astype(jnp.bfloat16),
        mixed_grad,
        preferred_element_type=jnp.float32,
    )
    attention_grad = jnp.einsum(
        "bqhe,bkhe->bhqk", mixed_grad, value_heads, preferred_element_type=jnp.float32
    )
    score_grad = attention * (
        attention_grad - jnp.sum(attention * attention_grad, axis=-1, keepdims=True)
    )
    score_low = score_grad.astype(jnp.bfloat16)
    query_grad = (
        jnp.einsum("bhqk,bkhe->bqhe", score_low, key_heads, preferred_element_type=jnp.float32)
        * score_scale
    )
    key_grad = (
        jnp.einsum("bhqk,bqhe->bkhe", score_low, query_heads, preferred_element_type=jnp.float32)
        * score_scale
    )
    return (query_grad, key_grad, value_grad)


def lamb_step(weight, gradient, moment, second, clip_factor):
    clipped = clip_factor * gradient
    moment_new = beta_one * moment + (1.0 - beta_one) * clipped
    second_new = beta_two * second + (1.0 - beta_two) * clipped * clipped
    ratio = (
        moment_new
        / (1.0 - beta_one**step_count)
        / (jnp.sqrt(second_new / (1.0 - beta_two**step_count)) + adam_eps)
        + decay_weight * weight
    )
    return (moment_new, second_new, ratio)


def segment_sums(values, offset, segment_size, tensor_count):
    labels = (offset + jnp.arange(values.shape[0], dtype=jnp.int32)) // segment_size
    matches = labels[:, None] == jnp.arange(tensor_count, dtype=jnp.int32)[None, :]
    return jnp.sum(jnp.where(matches, values[:, None], 0.0), axis=0)


def segment_spread(factors, offset, length_here, segment_size):
    labels = (offset + jnp.arange(length_here, dtype=jnp.int32)) // segment_size
    matches = labels[:, None] == jnp.arange(factors.shape[0], dtype=jnp.int32)[None, :]
    return jnp.sum(jnp.where(matches, factors[None, :], 0.0), axis=1)


def shards(
    suffix,
    memory,
    prefix_lengths,
    suffix_lengths,
    cotangent,
    self_weights,
    self_moment,
    self_second,
    cross_weights,
    cross_moment,
    cross_second,
    feed_weights,
    feed_moment,
    feed_second,
    vectors,
    vector_moment,
    vector_second,
):
    row_count = EX_DEV * SUF
    attn_shard = self_weights.shape[0]
    feed_shard = feed_weights.shape[0]
    self_full, cross_full, feed_full = (
        lax.all_gather(self_weights.astype(jnp.bfloat16), ("dp", "fsdp"), axis=0, tiled=True),
        lax.all_gather(cross_weights.astype(jnp.bfloat16), ("dp", "fsdp"), axis=0, tiled=True),
        lax.all_gather(feed_weights.astype(jnp.bfloat16), ("dp", "fsdp"), axis=0, tiled=True),
    )
    self_mats = self_full.reshape(4, D, D)
    cross_mats = cross_full.reshape(4, D, D)
    up_mat = feed_full[: D * FF].reshape(D, FF)
    down_mat = feed_full[D * FF :].reshape(FF, D)
    vector_parts = [vectors[segment * D : (segment + 1) * D] for segment in range(7)]
    bias_up = vectors[7 * D :]
    own_memory = lax.all_to_all(memory, "dp", split_axis=1, concat_axis=2, tiled=True)
    memory_rows = own_memory.reshape(EX_DEV * MEMLEN, D)
    suffix_len = suffix_lengths[0]
    prefix_len = prefix_lengths[0]
    positions = jnp.arange(SUF, dtype=jnp.int32)
    causal = positions[:, None] >= positions[None, :]
    self_allowed = (
        causal[None, None, :, :] & (positions[None, :] < suffix_len[:, None])[:, None, None, :]
    )
    memory_pos = jnp.arange(MEMLEN, dtype=jnp.int32)
    cross_allowed = (memory_pos[None, :] < (PATCH + prefix_len)[:, None])[:, None, None, :]
    inputs = suffix.reshape(row_count, D).astype(jnp.float32)
    normed_one = layer_norm(inputs, vector_parts[0], vector_parts[1]).astype(jnp.bfloat16)
    self_qkv = jnp.einsum(
        "rd,jde->jre", normed_one, self_mats[0:3], preferred_element_type=jnp.float32
    ).astype(jnp.bfloat16)
    self_heads = self_qkv.reshape(3, EX_DEV, SUF, H, HD)
    mixed_one, totals_one = attend_forward(
        self_heads[0], self_heads[1], self_heads[2], self_allowed
    )
    mixed_one = mixed_one.reshape(row_count, D).astype(jnp.bfloat16)
    hidden_one = inputs + jnp.dot(mixed_one, self_mats[3], preferred_element_type=jnp.float32)
    normed_two = layer_norm(hidden_one, vector_parts[2], vector_parts[3]).astype(jnp.bfloat16)
    cross_query = jnp.dot(normed_two, cross_mats[0], preferred_element_type=jnp.float32).astype(
        jnp.bfloat16
    )
    cross_kv = jnp.einsum(
        "rd,jde->jre", memory_rows, cross_mats[1:3], preferred_element_type=jnp.float32
    ).astype(jnp.bfloat16)
    query_heads = cross_query.reshape(EX_DEV, SUF, H, HD)
    kv_heads = cross_kv.reshape(2, EX_DEV, MEMLEN, H, HD)
    mixed_two, totals_two = attend_forward(query_heads, kv_heads[0], kv_heads[1], cross_allowed)
    mixed_two = mixed_two.reshape(row_count, D).astype(jnp.bfloat16)
    hidden_two = hidden_one + jnp.dot(mixed_two, cross_mats[3], preferred_element_type=jnp.float32)
    normed_three = layer_norm(hidden_two, vector_parts[4], vector_parts[5]).astype(jnp.bfloat16)
    pre_act = jnp.dot(normed_three, up_mat, preferred_element_type=jnp.float32) + bias_up
    activated = gelu_tanh(pre_act).astype(jnp.bfloat16)
    layer_output = hidden_two + (
        jnp.dot(activated, down_mat, preferred_element_type=jnp.float32) + vector_parts[6]
    )
    valid_rows = (positions[None, :] < suffix_len[:, None]).astype(jnp.float32)
    seed_rows = (
        cotangent.reshape(EX_DEV, SUF, D).astype(jnp.float32) * valid_rows[:, :, None]
    ).reshape(row_count, D)
    seed_low = seed_rows.astype(jnp.bfloat16)
    bias_down_grad = jnp.sum(seed_low.astype(jnp.float32), axis=0)
    down_grad = jnp.einsum("rf,rd->fd", activated, seed_low, preferred_element_type=jnp.float32)
    activated_grad = jnp.einsum("rd,fd->rf", seed_low, down_mat, preferred_element_type=jnp.float32)
    _, gelu_back = jax.vjp(gelu_tanh, pre_act)
    pre_grad = gelu_back(activated_grad)[0].astype(jnp.bfloat16)
    bias_up_grad = jnp.sum(pre_grad.astype(jnp.float32), axis=0)
    up_grad = jnp.einsum("rd,rf->df", normed_three, pre_grad, preferred_element_type=jnp.float32)
    normed_three_grad = jnp.einsum(
        "rf,df->rd", pre_grad, up_mat, preferred_element_type=jnp.float32
    )
    _, norm_three_back = jax.vjp(layer_norm, hidden_two, vector_parts[4], vector_parts[5])
    through_three, gain_three_grad, shift_three_grad = norm_three_back(normed_three_grad)
    hidden_two_grad = seed_rows + through_three
    feed_flat = jnp.concatenate([up_grad.reshape(-1), down_grad.reshape(-1)])
    branch_two = hidden_two_grad.astype(jnp.bfloat16)
    cross_out_grad = jnp.einsum(
        "rd,re->de", mixed_two, branch_two, preferred_element_type=jnp.float32
    )
    mixed_two_grad = jnp.einsum(
        "re,de->rd", branch_two, cross_mats[3], preferred_element_type=jnp.float32
    ).astype(jnp.bfloat16)
    query_two_grad, key_two_grad, value_two_grad = attend_backward(
        query_heads,
        kv_heads[0],
        kv_heads[1],
        cross_allowed,
        totals_two,
        mixed_two_grad.reshape(EX_DEV, SUF, H, HD),
    )
    cross_query_grad = query_two_grad.reshape(row_count, D).astype(jnp.bfloat16)
    cross_kv_grad = (
        jnp.stack([key_two_grad, value_two_grad])
        .reshape(2, EX_DEV * MEMLEN, D)
        .astype(jnp.bfloat16)
    )
    query_weight_grad = jnp.einsum(
        "rd,re->de", normed_two, cross_query_grad, preferred_element_type=jnp.float32
    )
    kv_weight_grad = jnp.einsum(
        "rd,jre->jde", memory_rows, cross_kv_grad, preferred_element_type=jnp.float32
    )
    normed_two_grad = jnp.einsum(
        "re,de->rd", cross_query_grad, cross_mats[0], preferred_element_type=jnp.float32
    )
    memory_local_grad = jnp.einsum(
        "jre,jde->rd", cross_kv_grad, cross_mats[1:3], preferred_element_type=jnp.float32
    )
    memory_gradient = lax.all_to_all(
        memory_local_grad.reshape(1, EX_DEV, MEMLEN, D),
        "dp",
        split_axis=2,
        concat_axis=1,
        tiled=True,
    )
    _, norm_two_back = jax.vjp(layer_norm, hidden_one, vector_parts[2], vector_parts[3])
    through_two, gain_two_grad, shift_two_grad = norm_two_back(normed_two_grad)
    hidden_one_grad = hidden_two_grad + through_two
    cross_flat = jnp.concatenate(
        [query_weight_grad[None], kv_weight_grad, cross_out_grad[None]], axis=0
    ).reshape(-1)
    branch_one = hidden_one_grad.astype(jnp.bfloat16)
    self_out_grad = jnp.einsum(
        "rd,re->de", mixed_one, branch_one, preferred_element_type=jnp.float32
    )
    mixed_one_grad = jnp.einsum(
        "re,de->rd", branch_one, self_mats[3], preferred_element_type=jnp.float32
    ).astype(jnp.bfloat16)
    query_one_grad, key_one_grad, value_one_grad = attend_backward(
        self_heads[0],
        self_heads[1],
        self_heads[2],
        self_allowed,
        totals_one,
        mixed_one_grad.reshape(EX_DEV, SUF, H, HD),
    )
    self_qkv_grad = (
        jnp.stack([query_one_grad, key_one_grad, value_one_grad])
        .reshape(3, row_count, D)
        .astype(jnp.bfloat16)
    )
    qkv_weight_grad = jnp.einsum(
        "rd,jre->jde", normed_one, self_qkv_grad, preferred_element_type=jnp.float32
    )
    normed_one_grad = jnp.einsum(
        "jre,jde->rd", self_qkv_grad, self_mats[0:3], preferred_element_type=jnp.float32
    )
    _, norm_one_back = jax.vjp(layer_norm, inputs, vector_parts[0], vector_parts[1])
    through_one, gain_one_grad, shift_one_grad = norm_one_back(normed_one_grad)
    suffix_gradient = (hidden_one_grad + through_one).reshape(1, EX_DEV, SUF, D)
    self_flat = jnp.concatenate([qkv_weight_grad, self_out_grad[None]], axis=0).reshape(-1)
    owners = lax.axis_size(("dp", "fsdp"))
    joined = jnp.concatenate(
        [
            self_flat.reshape(owners, attn_shard),
            cross_flat.reshape(owners, attn_shard),
            feed_flat.reshape(owners, feed_shard),
        ],
        axis=1,
    ).reshape(-1)
    owned = lax.psum_scatter(joined, ("dp", "fsdp"), scatter_dimension=0, tiled=True)
    self_total = owned[:attn_shard]
    cross_total = owned[attn_shard : 2 * attn_shard]
    feed_total = owned[2 * attn_shard :]
    vector_partial = jnp.concatenate(
        [
            gain_one_grad,
            shift_one_grad,
            gain_two_grad,
            shift_two_grad,
            gain_three_grad,
            shift_three_grad,
            bias_down_grad,
            bias_up_grad,
        ]
    )
    shard_index = lax.axis_index(("dp", "fsdp"))
    attn_offset = shard_index * attn_shard
    feed_offset = shard_index * feed_shard
    grad_squares = jnp.concatenate(
        [
            segment_sums(self_total * self_total, attn_offset, D * D, 4),
            segment_sums(cross_total * cross_total, attn_offset, D * D, 4),
            segment_sums(feed_total * feed_total, feed_offset, D * FF, 2),
        ]
    )
    weight_squares = jnp.concatenate(
        [
            segment_sums(self_weights * self_weights, attn_offset, D * D, 4),
            segment_sums(cross_weights * cross_weights, attn_offset, D * D, 4),
            segment_sums(feed_weights * feed_weights, feed_offset, D * FF, 2),
        ]
    )
    vector_total, grad_summed, weight_summed = lax.psum(
        (vector_partial, grad_squares, weight_squares), ("dp", "fsdp")
    )
    squared_total = jnp.sum(grad_summed) + jnp.sum(vector_total * vector_total)
    global_norm = jnp.sqrt(squared_total)
    clip_factor = jnp.minimum(1.0, 1.0 / global_norm)
    self_momentum, self_variance, self_ratio = lamb_step(
        self_weights, self_total, self_moment, self_second, clip_factor
    )
    cross_momentum, cross_variance, cross_ratio = lamb_step(
        cross_weights, cross_total, cross_moment, cross_second, clip_factor
    )
    feed_momentum, feed_variance, feed_ratio = lamb_step(
        feed_weights, feed_total, feed_moment, feed_second, clip_factor
    )
    ratio_squares = jnp.concatenate(
        [
            segment_sums(self_ratio * self_ratio, attn_offset, D * D, 4),
            segment_sums(cross_ratio * cross_ratio, attn_offset, D * D, 4),
            segment_sums(feed_ratio * feed_ratio, feed_offset, D * FF, 2),
        ]
    )
    update_summed = lax.psum(ratio_squares, ("dp", "fsdp"))
    weight_norms = jnp.sqrt(weight_summed)
    ratio_norms = jnp.sqrt(update_summed)
    trust_ratio = weight_norms / (ratio_norms + trust_eps)
    self_master = (
        self_weights
        - learn_rate * segment_spread(trust_ratio[0:4], attn_offset, attn_shard, D * D) * self_ratio
    )
    cross_master = (
        cross_weights
        - learn_rate
        * segment_spread(trust_ratio[4:8], attn_offset, attn_shard, D * D)
        * cross_ratio
    )
    feed_master = (
        feed_weights
        - learn_rate
        * segment_spread(trust_ratio[8:10], feed_offset, feed_shard, D * FF)
        * feed_ratio
    )
    vector_momentum, vector_variance, vector_ratio = lamb_step(
        vectors, vector_total, vector_moment, vector_second, clip_factor
    )
    edges = [0, D, 2 * D, 3 * D, 4 * D, 5 * D, 6 * D, 7 * D, 7 * D + FF]
    vector_wn = []
    vector_rn = []
    new_pieces = []
    for segment in range(8):
        weight_part = vectors[edges[segment] : edges[segment + 1]]
        ratio_part = vector_ratio[edges[segment] : edges[segment + 1]]
        weight_norm = jnp.sqrt(jnp.sum(weight_part * weight_part))
        ratio_norm = jnp.sqrt(jnp.sum(ratio_part * ratio_part))
        piece_trust = weight_norm / (ratio_norm + trust_eps)
        vector_wn.append(weight_norm)
        vector_rn.append(ratio_norm)
        new_pieces.append(weight_part - learn_rate * piece_trust * ratio_part)
    vector_master = jnp.concatenate(new_pieces)
    tensor_norms = jnp.stack(
        [
            jnp.concatenate([weight_norms, jnp.stack(vector_wn)]),
            jnp.concatenate([ratio_norms, jnp.stack(vector_rn)]),
        ]
    )
    return (
        layer_output.reshape(1, EX_DEV, SUF, D),
        suffix_gradient,
        memory_gradient,
        self_total,
        self_momentum,
        self_variance,
        self_master,
        cross_total,
        cross_momentum,
        cross_variance,
        cross_master,
        feed_total,
        feed_momentum,
        feed_variance,
        feed_master,
        vector_total,
        vector_momentum,
        vector_variance,
        vector_master,
        tensor_norms,
        global_norm,
    )


BF = jnp.bfloat16
F32 = jnp.float32
MESH = pl.DeviceIdType.MESH
NZ = 4


def place():
    dp, fs = lax.axis_index("dp"), lax.axis_index("fsdp")
    return dp, fs, dp // 2, dp % 2, fs // 2, fs % 2


def peer_id(z, y, x, c):
    return (z * 2 + y, x * 2 + c)


def greet(ids):
    bar = pltpu.get_barrier_semaphore()
    for where in ids:
        pl.semaphore_signal(bar, inc=1, device_id=where, device_id_type=MESH)
    pl.semaphore_wait(bar, len(ids))


class Copies:
    def __init__(self, send, recv, local):
        self.send, self.recv, self.local = send, recv, local
        self.remotes, self.locals = 0, 0
        self.open = []

    def remote(self, src, dst, where):
        i = self.remotes
        self.remotes += 1
        cp = pltpu.make_async_remote_copy(
            src_ref=src,
            dst_ref=dst,
            send_sem=self.send.at[i],
            recv_sem=self.recv.at[i],
            device_id=where,
            device_id_type=MESH,
        )
        cp.start()
        self.open.append(cp)
        return cp

    def here(self, src, dst):
        cp = pltpu.make_async_copy(src, dst, self.local.at[self.locals])
        self.locals += 1
        cp.start()
        return cp

    def drain(self):
        for cp in self.open:
            cp.wait_send()


def gather_kernel(
    self_in, cross_in, feed_in, mem_in, self_out, cross_out, feed_out, mem_out, send, recv, local
):
    dp, fs, z, y, x, c = place()
    ndp = mem_out.shape[1]
    ex = mem_out.shape[0]
    to_y, to_x, to_c = peer_id(z, 1 - y, x, c), peer_id(z, y, 1 - x, c), peer_id(z, y, x, 1 - c)
    greet([((dp + k) % ndp, fs) for k in range(1, ndp)] + [to_x, to_c])
    cp = Copies(send, recv, local)

    chunks = []
    for src, dst, js in (
        (self_in, self_out, (0, 1)),
        (cross_in, cross_out, (0, 1)),
        (feed_in, feed_out, (0, 2)),
        (feed_in, feed_out, (2, 2)),
    ):
        rows = src.shape[1]
        cut = rows * 2 // 3
        chunks.append((src, dst, pl.ds(*js), pl.ds(0, cut), pl.ds(cut, rows - cut)))

    own = [cp.here(chunk[0].at[chunk[2]], chunk[1].at[z, y, x, c, chunk[2]]) for chunk in chunks]
    own_mem = cp.here(mem_in.at[pl.ds(ex * dp, ex)], mem_out.at[:, dp])

    zc, s2, s3, s4 = {}, {}, {}, {}

    def send_z(t):
        src, dst, js, r0, r1 = chunks[t]
        for k in range(1, NZ):
            zc[t, k] = cp.remote(
                src.at[js], dst.at[z, y, x, c, js], peer_id((z + k) % NZ, y, x, c)
            )

    def send_2(t, k):
        src, dst, js, r0, r1 = chunks[t]
        zz = (z + NZ - k) % NZ
        for part, rows, where in ((0, r0, to_y), (1, r1, to_x)):
            here = src.at[js, rows] if k == 0 else dst.at[zz, y, x, c, js, rows]
            s2[t, k, part] = cp.remote(here, dst.at[zz, y, x, c, js, rows], where)

    def send_3(t):
        src, dst, js, r0, r1 = chunks[t]
        s3[t, 0] = cp.remote(
            dst.at[:, :, x, c, js, r0], dst.at[:, :, x, c, js, r0], to_x
        )
        s3[t, 1] = cp.remote(
            dst.at[:, y, :, c, js, r1], dst.at[:, y, :, c, js, r1], to_y
        )

    def send_4(t):
        src, dst, js, r0, r1 = chunks[t]
        s4[t] = cp.remote(dst.at[:, :, :, c, js], dst.at[:, :, :, c, js], to_c)

    n = len(chunks)
    for t in range(n):
        send_z(t)
        send_2(t, 0)
    mem = [
        cp.remote(
            mem_in.at[pl.ds(ex * ((dp + k) % ndp), ex)],
            mem_out.at[:, dp],
            ((dp + k) % ndp, fs),
        )
        for k in range(1, ndp)
    ]
    for t in range(n + 2):
        if t < n:
            for k in range(1, NZ):
                zc[t, k].wait_recv()
                send_2(t, k)
        if 1 <= t <= n:
            own[t - 1].wait()
            for k in range(NZ):
                for part in (0, 1):
                    s2[t - 1, k, part].wait_recv()
            send_3(t - 1)
        if t >= 2:
            s3[t - 2, 0].wait_recv()
            s3[t - 2, 1].wait_recv()
            send_4(t - 2)
    for t in range(n):
        s4[t].wait_recv()
    own_mem.wait()
    for one in mem:
        one.wait_recv()
    cp.drain()


def gather_all(self_in, cross_in, feed_in, mem_in, ndp):
    any_space = pl.BlockSpec(memory_space=pl.ANY)
    shards_of = lambda a: jax.ShapeDtypeStruct((NZ, 2, 2, 2) + a.shape, BF)
    ex = mem_in.shape[0] // ndp
    return pl.pallas_call(
        gather_kernel,
        out_shape=[
            shards_of(self_in),
            shards_of(cross_in),
            shards_of(feed_in),
            jax.ShapeDtypeStruct((ex, ndp) + mem_in.shape[1:], BF),
        ],
        in_specs=[any_space] * 4,
        out_specs=[any_space] * 4,
        scratch_shapes=[
            pltpu.SemaphoreType.DMA((72,)),
            pltpu.SemaphoreType.DMA((72,)),
            pltpu.SemaphoreType.DMA((8,)),
        ],
        compiler_params=pltpu.CompilerParams(collective_id=1, has_side_effects=True),
        name="gather_all",
    )(self_in, cross_in, feed_in, mem_in)


def squares(v):
    rows, cols = v.shape
    w = jnp.sum((v * v).reshape(rows // 8, 8, cols), axis=0)
    total = w[:, 0:128]
    for i in range(1, cols // 128):
        total = total + w[:, i * 128 : (i + 1) * 128]
    return total


def sum_everywhere(cp, mine, slots_a, slots_b, dp, fs):
    nfs, ndp = slots_a.shape[0], slots_b.shape[0]
    slots_a[fs] = mine
    got = [
        cp.remote(slots_a.at[fs], slots_a.at[fs], (dp, (fs + k) % nfs)) for k in range(1, nfs)
    ]
    for one in got:
        one.wait_recv()
    total = slots_a[0]
    for k in range(1, nfs):
        total = total + slots_a[k]
    slots_b[dp] = total
    got = [
        cp.remote(slots_b.at[dp], slots_b.at[dp], ((dp + k) % ndp, fs)) for k in range(1, ndp)
    ]
    for one in got:
        one.wait_recv()
    total = slots_b[0]
    for k in range(1, ndp):
        total = total + slots_b[k]
    return total


def scatter_kernel(
    qkv_g, out_g, cq_g, ckv_g, co_g, up_g, dn_g, mem_g, vec,
    self_t, cross_t, feed_t, mem_t, vec_t, sq_t,
    send, recv, local,
    acc_s, acc_c, acc_f0, acc_f1, r1_s, r1_c, r1_f0, r1_f1,
    r2a_s, r2a_c, r2a_f0, r2a_f1, r2b_s, r2b_c, r2b_f0, r2b_f1,
    r3a_s, r3a_c, r3a_f0, r3a_f1, r3b_s, r3b_c, r3b_f0, r3b_f1,
    rz_s, rz_c, rz_f0, rz_f1,
    v_send, v_recv, v_z, slots_a, slots_b,
):
    dp, fs, z, y, x, c = place()
    ndp = mem_g.shape[1]
    ex = mem_g.shape[0]
    to_y, to_x, to_c = peer_id(z, 1 - y, x, c), peer_id(z, y, 1 - x, c), peer_id(z, y, x, 1 - c)
    nfs = slots_a.shape[0]
    greet(
        [((dp + k) % ndp, fs) for k in range(1, ndp)] + [(dp, (fs + k) % nfs) for k in range(1, nfs)]
    )
    cp = Copies(send, recv, local)

    def self_src(zz, j, cc):
        return qkv_g.at[zz, :, :, cc] if zz < 3 else out_g.at[:, :, cc]

    def cross_src(zz, j, cc):
        if zz == 0:
            return cq_g.at[:, :, cc]
        return ckv_g.at[zz - 1, :, :, cc] if zz < 3 else co_g.at[:, :, cc]

    def feed_src(first):
        def src(zz, j, cc):
            if zz < 2:
                return up_g.at[first + j, zz, :, :, cc]
            return dn_g.at[zz - 2, :, :, cc, first + j]

        return src

    chunks = (
        (feed_src(0), acc_f0, r1_f0, r2a_f0, r2b_f0, r3a_f0, r3b_f0, rz_f0),
        (feed_src(2), acc_f1, r1_f1, r2a_f1, r2b_f1, r3a_f1, r3b_f1, rz_f1),
        (cross_src, acc_c, r1_c, r2a_c, r2b_c, r3a_c, r3b_c, rz_c),
        (self_src, acc_s, r1_s, r2a_s, r2b_s, r3a_s, r3b_s, rz_s),
    )
    n = len(chunks)
    sc, sl, s1, s2, sz = {}, {}, {}, {}, {}

    vcp = cp.remote(vec, v_recv.at[0], to_c)
    for t, (src, acc, r1, *_) in enumerate(chunks):
        for zz in range(NZ):
            for j in range(acc.shape[3]):
                sc[t, zz, j] = cp.remote(src(zz, j, 1 - c), r1.at[zz, :, :, j], to_c)
                sl[t, zz, j] = cp.here(src(zz, j, c), acc.at[zz, :, :, j])
    own_mem = cp.here(mem_g.at[:, dp], mem_t.at[pl.ds(ex * dp, ex)])
    mem = [
        cp.remote(mem_g.at[:, (dp + k) % ndp], mem_t.at[pl.ds(ex * dp, ex)], ((dp + k) % ndp, fs))
        for k in range(1, ndp)
    ]

    def cuts(acc):
        rows = acc.shape[4]
        cut = rows * 2 // 3
        return pl.ds(0, cut), pl.ds(cut, rows - cut)

    def add_c(acc, r1, fixed_y, fixed_x, rows):
        def body(i, _):
            zz, o = i // 2, i % 2
            yy = o if fixed_y is None else fixed_y
            xx = o if fixed_x is None else fixed_x
            for j in range(acc.shape[3]):
                acc[zz, yy, xx, j, rows] = acc[zz, yy, xx, j, rows] + r1[zz, yy, xx, j, rows]
            return 0

        lax.fori_loop(0, NZ * 2, body, 0)

    def phase_c(t):
        src, acc, r1, r2a, r2b, *_ = chunks[t]
        r0, r1_rows = cuts(acc)
        for zz in range(NZ):
            for j in range(acc.shape[3]):
                sc[t, zz, j].wait_recv()
                sl[t, zz, j].wait()
        add_c(acc, r1, None, 1 - x, r0)
        s1[t, 0] = cp.remote(acc.at[:, :, 1 - x, :, r0], r2a, to_x)
        add_c(acc, r1, 1 - y, None, r1_rows)
        s1[t, 1] = cp.remote(acc.at[:, 1 - y, :, :, r1_rows], r2b, to_y)
        add_c(acc, r1, None, x, r0)
        add_c(acc, r1, y, None, r1_rows)

    def phase_1(t):
        src, acc, r1, r2a, r2b, r3a, r3b, rz = chunks[t]
        r0, r1_rows = cuts(acc)

        def body_a(yy):
            def body(zz, _):
                for j in range(acc.shape[3]):
                    acc[zz, yy, x, j, r0] = acc[zz, yy, x, j, r0] + r2a[zz, yy, j]
                return 0

            return body

        def body_b(xx):
            def body(zz, _):
                for j in range(acc.shape[3]):
                    acc[zz, y, xx, j, r1_rows] = acc[zz, y, xx, j, r1_rows] + r2b[zz, xx, j]
                return 0

            return body

        s1[t, 0].wait_recv()
        lax.fori_loop(0, NZ, body_a(1 - y), 0)
        s2[t, 0] = cp.remote(acc.at[:, 1 - y, x, :, r0], r3a, to_y)
        s1[t, 1].wait_recv()
        lax.fori_loop(0, NZ, body_b(1 - x), 0)
        s2[t, 1] = cp.remote(acc.at[:, y, 1 - x, :, r1_rows], r3b, to_x)
        lax.fori_loop(0, NZ, body_a(y), 0)
        lax.fori_loop(0, NZ, body_b(x), 0)

    def phase_2(t):
        src, acc, r1, r2a, r2b, r3a, r3b, rz = chunks[t]
        r0, r1_rows = cuts(acc)
        s2[t, 0].wait_recv()
        s2[t, 1].wait_recv()

        def body(zz, _):
            for j in range(acc.shape[3]):
                acc[zz, y, x, j, r0] = acc[zz, y, x, j, r0] + r3a[zz, j]
                acc[zz, y, x, j, r1_rows] = acc[zz, y, x, j, r1_rows] + r3b[zz, j]
            return 0

        lax.fori_loop(0, NZ, body, 0)
        for k in range(1, NZ):
            zt = (z + k) % NZ
            sz[t, k] = cp.remote(acc.at[zt, y, x], rz.at[k - 1], peer_id(zt, y, x, c))

    sums = []

    def phase_z(t, out, first):
        src, acc, r1, r2a, r2b, r3a, r3b, rz = chunks[t]
        for k in range(1, NZ):
            sz[t, k].wait_recv()
        for j in range(acc.shape[3]):
            total = acc[z, y, x, j].astype(F32)
            for k in range(1, NZ):
                total = total + rz[k - 1, j].astype(F32)
            out[first + j] = total
            sums.append(squares(total))

    def vec_step(i):
        nonlocal vcp
        vcp.wait_recv()
        if i < 3:
            before = vec[...] if i == 0 else v_send[i - 1]
            v_send[i] = before + v_recv[i]
            if i < 2:
                vcp = cp.remote(v_send.at[i], v_recv.at[i + 1], (to_x, to_y)[i])

    for t in range(n + 3):
        if t < n:
            phase_c(t)
        if t < 3:
            vec_step(t)
        if t == 2:
            v_z[z] = v_send[2]
            vz = [
                cp.remote(v_send.at[2], v_z.at[z], peer_id((z + k) % NZ, y, x, c))
                for k in range(1, NZ)
            ]
        if 1 <= t <= n:
            phase_1(t - 1)
        if 2 <= t <= n + 1:
            phase_2(t - 2)
        if t >= 3:
            phase_z(t - 3, (feed_t, feed_t, cross_t, self_t)[t - 3], (0, 2, 0, 0)[t - 3])
    for one in vz:
        one.wait_recv()
    vec_t[...] = (v_z[0] + v_z[1]) + (v_z[2] + v_z[3])
    total = sums[0]
    for one in sums[1:]:
        total = total + one
    sq_t[...] = sum_everywhere(cp, total, slots_a, slots_b, dp, fs)
    own_mem.wait()
    for one in mem:
        one.wait_recv()
    cp.drain()


def scatter_all(grads, mem_g, vec, rows_a, rows_f, ndp, nfs):
    any_space = pl.BlockSpec(memory_space=pl.ANY)
    vmem = pl.BlockSpec(memory_space=pltpu.VMEM)
    ex, _, pos, width = mem_g.shape
    kinds = ((1, rows_a), (1, rows_a), (2, rows_f), (2, rows_f))
    acc = [pltpu.VMEM((NZ, 2, 2, j, r, width), BF) for j, r in kinds]
    r2a = [pltpu.VMEM((NZ, 2, j, r * 2 // 3, width), BF) for j, r in kinds]
    r2b = [pltpu.VMEM((NZ, 2, j, r - r * 2 // 3, width), BF) for j, r in kinds]
    r3a = [pltpu.VMEM((NZ, j, r * 2 // 3, width), BF) for j, r in kinds]
    r3b = [pltpu.VMEM((NZ, j, r - r * 2 // 3, width), BF) for j, r in kinds]
    rz = [pltpu.VMEM((NZ - 1, j, r, width), BF) for j, r in kinds]
    return pl.pallas_call(
        scatter_kernel,
        out_shape=[
            jax.ShapeDtypeStruct((1, rows_a, width), F32),
            jax.ShapeDtypeStruct((1, rows_a, width), F32),
            jax.ShapeDtypeStruct((4, rows_f, width), F32),
            jax.ShapeDtypeStruct((ndp * ex, pos, width), BF),
            jax.ShapeDtypeStruct(vec.shape, F32),
            jax.ShapeDtypeStruct((8, 128), F32),
        ],
        in_specs=[any_space] * 8 + [vmem],
        out_specs=[vmem, vmem, vmem, any_space, vmem, vmem],
        scratch_shapes=[
            pltpu.SemaphoreType.DMA((80,)),
            pltpu.SemaphoreType.DMA((80,)),
            pltpu.SemaphoreType.DMA((32,)),
            *acc,
            *acc,
            *r2a,
            *r2b,
            *r3a,
            *r3b,
            *rz,
            pltpu.VMEM((3,) + vec.shape, F32),
            pltpu.VMEM((3,) + vec.shape, F32),
            pltpu.VMEM((NZ,) + vec.shape, F32),
            pltpu.VMEM((nfs, 8, 128), F32),
            pltpu.VMEM((ndp, 8, 128), F32),
        ],
        compiler_params=pltpu.CompilerParams(
            collective_id=2, has_side_effects=True, vmem_limit_bytes=58 << 20
        ),
        name="scatter_all",
    )(*grads, mem_g, vec)


def ratio_kernel(
    gs, gc, gf, ws, wc, wf, ms, mc, mf, vs, vc, vf, clip, out, send, recv, local, slots_a, slots_b
):
    dp, fs, z, y, x, c = place()
    nfs, ndp = slots_a.shape[0], slots_b.shape[0]
    greet(
        [((dp + k) % ndp, fs) for k in range(1, ndp)] + [(dp, (fs + k) % nfs) for k in range(1, nfs)]
    )
    cp = Copies(send, recv, local)
    factor = clip[0:1, 0:1]
    rows = lax.broadcasted_iota(jnp.int32, (32, 128), 0)
    tile = jnp.zeros((32, 128), F32)
    for g, w, m, v, row in (
        (gs, ws, ms, vs, z),
        (gc, wc, mc, vc, NZ + z),
        (gf, wf, mf, vf, 2 * NZ + z // 2),
    ):
        ratio = lamb_step(w[...], g[...], m[...], v[...], factor)[2]
        for first, a in ((0, ratio), (16, w[...])):
            part = jnp.sum(a * a, axis=0, keepdims=True)
            tile = tile + jnp.where(rows == first + row, part, 0.0)
    out[...] = sum_everywhere(cp, tile, slots_a, slots_b, dp, fs)
    cp.drain()


def ratio_all(args, clip, ndp, nfs):
    vmem = pl.BlockSpec(memory_space=pltpu.VMEM)
    return pl.pallas_call(
        ratio_kernel,
        out_shape=jax.ShapeDtypeStruct((32, 128), F32),
        in_specs=[vmem] * 13,
        out_specs=vmem,
        scratch_shapes=[
            pltpu.SemaphoreType.DMA((16,)),
            pltpu.SemaphoreType.DMA((16,)),
            pltpu.SemaphoreType.DMA((1,)),
            pltpu.VMEM((nfs, 32, 128), F32),
            pltpu.VMEM((ndp, 32, 128), F32),
        ],
        compiler_params=pltpu.CompilerParams(
            collective_id=3, has_side_effects=True, vmem_limit_bytes=40 << 20
        ),
        name="ratio_all",
    )(*args, clip)


def dot_nn(a, b):
    return lax.dot_general(a, b, (((1,), (0,)), ((), ())), preferred_element_type=F32)


def dot_nt(a, b):
    return lax.dot_general(a, b, (((1,), (1,)), ((), ())), preferred_element_type=F32)


def dot_tn(a, b):
    return lax.dot_general(a, b, (((0,), (0,)), ((), ())), preferred_element_type=F32)


def norm_parts(values):
    centred = values - jnp.mean(values, axis=-1, keepdims=True)
    scale = lax.rsqrt(jnp.mean(centred * centred, axis=-1, keepdims=True) + norm_eps)
    return centred * scale, scale


def norm_back(unit, scale, gain, grad):
    e = grad * gain
    return scale * (
        e
        - jnp.mean(e, axis=-1, keepdims=True)
        - unit * jnp.mean(e * unit, axis=-1, keepdims=True)
    )


def column_sum(values):
    return jnp.sum(values, axis=0, keepdims=True)


def split_heads(pair):
    low = lax.broadcasted_iota(jnp.int32, pair.shape, 1) < HD
    zero = jnp.zeros_like(pair)
    return jnp.concatenate([jnp.where(low, pair, zero), jnp.where(low, zero, pair)], axis=0)


def join_heads(stacked):
    rows = stacked.shape[0] // 2
    low = lax.broadcasted_iota(jnp.int32, (rows, 2 * HD), 1) < HD
    return jnp.where(low, stacked[:rows], stacked[rows:])


def soft_rows(scores, allowed):
    scores = jnp.where(allowed, scores * HD ** (-0.5), masked_score)
    top = jnp.max(scores, axis=-1, keepdims=True)
    p = jnp.exp(scores - top)
    return p / jnp.sum(p, axis=-1, keepdims=True)


def self_mask(lens):
    shape = (2 * SUF, SUF)
    query = lax.broadcasted_iota(jnp.int32, shape, 0) % SUF
    key = lax.broadcasted_iota(jnp.int32, shape, 1)
    return (key <= query) & (key < lens[0:1, 0:SUF])


def cross_mask(lens):
    key = lax.broadcasted_iota(jnp.int32, (2 * SUF, MEMLEN), 1)
    seen = jnp.concatenate([lens[0:1]] * (MEMLEN // 128), axis=1)
    return key < PATCH + seen


PAIRS = H // 2


def attend(mask_of, lens, q_ref, k_ref, v_ref, o_ref, p_ref, key_rows):
    def body(ex, _):
        allowed = mask_of(lens[ex])
        rows = pl.ds(pl.multiple_of(ex * SUF, SUF), SUF)
        keys = pl.ds(pl.multiple_of(ex * key_rows, key_rows), key_rows)
        for pair in range(PAIRS):
            lanes = pl.ds(pair * 2 * HD, 2 * HD)
            p = soft_rows(dot_nt(split_heads(q_ref[rows, lanes]), k_ref[keys, lanes]), allowed)
            p_ref[ex * PAIRS + pair] = p
            o_ref[rows, lanes] = join_heads(dot_nn(p.astype(BF), v_ref[keys, lanes])).astype(BF)
        return 0

    lax.fori_loop(0, EX_DEV, body, 0)


def attend_back(q_ref, k_ref, v_ref, p_ref, do_ref, dq_ref, dk_ref, dv_ref, key_rows):
    scale = HD ** (-0.5)

    def body(ex, _):
        rows = pl.ds(pl.multiple_of(ex * SUF, SUF), SUF)
        keys = pl.ds(pl.multiple_of(ex * key_rows, key_rows), key_rows)
        for pair in range(PAIRS):
            lanes = pl.ds(pair * 2 * HD, 2 * HD)
            p = p_ref[ex * PAIRS + pair]
            d_out = split_heads(do_ref[rows, lanes])
            dv_ref[keys, lanes] = dot_tn(p.astype(BF), d_out).astype(BF)
            dp = dot_nt(d_out, v_ref[keys, lanes])
            ds = (p * (dp - jnp.sum(p * dp, axis=-1, keepdims=True))).astype(BF)
            dq_ref[rows, lanes] = (join_heads(dot_nn(ds, k_ref[keys, lanes])) * scale).astype(BF)
            dk_ref[keys, lanes] = (
                dot_tn(ds, split_heads(q_ref[rows, lanes])) * scale
            ).astype(BF)
        return 0

    lax.fori_loop(0, EX_DEV, body, 0)


def gelu_parts(u):
    rate = (2.0 / jnp.pi) ** 0.5
    square = u * u
    t = jnp.tanh(rate * (u + 0.044715 * u * square))
    half = 0.5 * (1.0 + t)
    slope = half + 0.5 * u * (1.0 - t * t) * (rate * (1.0 + 3 * 0.044715 * square))
    return u * half, slope


def layer_kernel(
    x_ref, cot_ref, vec_ref, slen_ref, plen_ref, self_h, cross_h, up_h, dn_h, mem_h,
    out_ref, sg_ref, vecg_ref, qkv_g, wo_g, cq_g, ckv_g, co_g, up_g, dn_g, mem_g,
    sw, cw, uw, dw, mem, ring, dmem, a1, q1, k1, v1, o1, a2, q2, o2, a3, k2, v2,
    db, dq, dk1, dv1, dk2, dv2, e3, z_ref, slope, unit1, unit2, unit3, h1, h2, dh, ps, pc,
    loads, stores, mem_sem,
):
    sources = (
        [(self_h.at[i], sw.at[i]) for i in range(4)]
        + [(mem_h, mem)]
        + [(cross_h.at[i], cw.at[i]) for i in range(4)]
        + [(up_h.at[pl.ds(0, uw.shape[1]), j], uw.at[j]) for j in range(4)]
        + [(dn_h.at[4 + j], dw.at[j]) for j in range(4)]
    )
    fetched = []
    for i, (src, dst) in enumerate(sources):
        fetched.append(pltpu.make_async_copy(src, dst, loads.at[i]))
        fetched[-1].start()
    self_ok, mem_ok, cross_ok = fetched[0:4], fetched[4], fetched[5:9]
    up_ok, dn_ok = fetched[9:13], fetched[13:17]

    depth = ring.shape[0]
    pending = []

    def give(value, dst):
        slot = len(pending) % depth
        if len(pending) >= depth:
            pending[-depth].wait()
        ring[slot] = value.astype(BF)
        pending.append(pltpu.make_async_copy(ring.at[slot], dst, stores.at[slot]))
        pending[-1].start()

    def row(i):
        return vec_ref[i : i + 1, :]

    g1, b1, g2, b2, g3, b3, bdn = [row(i) for i in range(7)]

    x = x_ref[...].astype(F32)
    unit, r1 = norm_parts(x)
    unit1[...] = unit
    a1[...] = (unit * g1 + b1).astype(BF)
    for i, ref in enumerate((q1, k1, v1)):
        self_ok[i].wait()
        ref[...] = dot_nn(a1[...], sw[i]).astype(BF)
    attend(self_mask, slen_ref, q1, k1, v1, o1, ps, SUF)
    self_ok[3].wait()
    h1[...] = x_ref[...].astype(F32) + dot_nn(o1[...], sw[3])

    unit, r2 = norm_parts(h1[...])
    unit2[...] = unit
    a2[...] = (unit * g2 + b2).astype(BF)
    cross_ok[0].wait()
    q2[...] = dot_nn(a2[...], cw[0]).astype(BF)
    mem_ok.wait()
    for i, ref in ((1, k2), (2, v2)):
        cross_ok[i].wait()
        ref[...] = dot_nn(mem[...], cw[i]).astype(BF)
    attend(cross_mask, plen_ref, q2, k2, v2, o2, pc, MEMLEN)
    cross_ok[3].wait()
    h2[...] = h1[...] + dot_nn(o2[...], cw[3])

    unit, r3 = norm_parts(h2[...])
    unit3[...] = unit
    a3[...] = (unit * g3 + b3).astype(BF)
    out_ref[...] = h2[...] + bdn
    ones = lax.broadcasted_iota(jnp.int32, (SUF, D), 0)
    for ex in range(EX_DEV):
        rows = pl.ds(ex * SUF, SUF)
        length = jnp.concatenate([slen_ref[ex, 0:1]] * (D // 128), axis=1)
        seed = cot_ref[rows].astype(F32) * (ones < length).astype(F32)
        dh[rows] = seed
        e3[rows] = seed.astype(BF)
    vecg_ref[6:7] = column_sum(e3[...].astype(F32))
    width = uw.shape[1] * uw.shape[2]
    for j in range(4):
        up_ok[j].wait()
        dn_ok[j].wait()
        u = dot_nn(a3[...], uw[j].reshape(width, D)) + row(7 + j)
        act, bend = gelu_parts(u)
        z_ref[...] = act.astype(BF)
        slope[...] = bend
        out_ref[...] += dot_nn(z_ref[...], dw[j])
        give(dot_tn(z_ref[...], e3[...]), dn_g.at[j])
        db[...] = (dot_nt(e3[...], dw[j]) * slope[...]).astype(BF)
        vecg_ref[7 + j : 8 + j] = column_sum(db[...].astype(F32))
        give(dot_tn(a3[...], db[...]), up_g.at[j])
        part = dot_nt(db[...], uw[j].reshape(width, D))
        if j == 0:
            h2[...] = part
        else:
            h2[...] += part

    grad = h2[...]
    vecg_ref[4:5] = column_sum(grad * unit3[...])
    vecg_ref[5:6] = column_sum(grad)
    dh[...] += norm_back(unit3[...], r3, g3, grad)
    db[...] = dh[...].astype(BF)
    give(dot_tn(o2[...], db[...]), co_g)
    e3[...] = dot_nt(db[...], cw[3]).astype(BF)
    attend_back(q2, k2, v2, pc, e3, dq, dk2, dv2, MEMLEN)
    give(dot_tn(a2[...], dq[...]), cq_g)
    give(dot_tn(mem[...], dk2[...]), ckv_g.at[0])
    give(dot_tn(mem[...], dv2[...]), ckv_g.at[1])
    outs = []
    for ex in range(EX_DEV):
        keys = pl.ds(ex * MEMLEN, MEMLEN)
        dmem[ex] = (dot_nt(dk2[keys], cw[1]) + dot_nt(dv2[keys], cw[2])).astype(BF)
        outs.append(pltpu.make_async_copy(dmem.at[ex], mem_g.at[ex], mem_sem.at[ex]))
        outs[-1].start()
    grad = dot_nt(dq[...], cw[0])
    vecg_ref[2:3] = column_sum(grad * unit2[...])
    vecg_ref[3:4] = column_sum(grad)
    dh[...] += norm_back(unit2[...], r2, g2, grad)
    db[...] = dh[...].astype(BF)
    give(dot_tn(o1[...], db[...]), wo_g)
    e3[...] = dot_nt(db[...], sw[3]).astype(BF)
    attend_back(q1, k1, v1, ps, e3, dq, dk1, dv1, SUF)
    for i, ref in enumerate((dq, dk1, dv1)):
        give(dot_tn(a1[...], ref[...]), qkv_g.at[i])
    grad = dot_nt(dq[...], sw[0]) + dot_nt(dk1[...], sw[1]) + dot_nt(dv1[...], sw[2])
    vecg_ref[0:1] = column_sum(grad * unit1[...])
    vecg_ref[1:2] = column_sum(grad)
    sg_ref[...] = dh[...] + norm_back(unit1[...], r1, g1, grad)
    for one in outs + pending[-depth:]:
        one.wait()


def layer_all(x, cot, vec, slen, plen, self_mats, cross_mats, up_view, dn_view, mem_rows):
    anywhere = pl.BlockSpec(memory_space=pl.ANY)
    vmem = pl.BlockSpec(memory_space=pltpu.VMEM)
    rows, mem_count = x.shape[0], mem_rows.shape[0]
    mats = lambda n: pltpu.VMEM((n, D, D), BF)
    low = pltpu.VMEM((rows, D), BF)
    wide = pltpu.VMEM((rows, D), F32)
    mem_low = pltpu.VMEM((mem_count, D), BF)
    shape = lambda *dims, dtype=BF: jax.ShapeDtypeStruct(dims, dtype)
    half = up_view.shape[0] // 2
    return pl.pallas_call(
        layer_kernel,
        out_shape=[
            shape(rows, D, dtype=F32),
            shape(rows, D, dtype=F32),
            shape(*vec.shape, dtype=F32),
            shape(3, D, D),
            shape(D, D),
            shape(D, D),
            shape(2, D, D),
            shape(D, D),
            shape(4, D, D),
            shape(4, D, D),
            shape(EX_DEV, MEMLEN, D),
        ],
        in_specs=[vmem] * 5 + [anywhere] * 5,
        out_specs=[vmem] * 3 + [anywhere] * 8,
        scratch_shapes=[
            mats(4), mats(4), pltpu.VMEM((4, half) + up_view.shape[2:], BF), mats(4),
            mem_low, mats(4), pltpu.VMEM((EX_DEV, MEMLEN, D), BF),
            low, low, low, low, low, low, low, low, low, mem_low, mem_low,
            low, low, low, low, mem_low, mem_low, low, low,
            wide, wide, wide, wide, wide, wide, wide,
            pltpu.VMEM((EX_DEV * PAIRS, 2 * SUF, SUF), F32),
            pltpu.VMEM((EX_DEV * PAIRS, 2 * SUF, MEMLEN), F32),
            pltpu.SemaphoreType.DMA((17,)),
            pltpu.SemaphoreType.DMA((4,)),
            pltpu.SemaphoreType.DMA((EX_DEV,)),
        ],
        compiler_params=pltpu.CompilerParams(vmem_limit_bytes=60 << 20),
        name="layer_all",
    )(x, cot, vec, slen, plen, self_mats, cross_mats, up_view, dn_view, mem_rows)


def fast_shards(
    suffix,
    memory,
    prefix_lengths,
    suffix_lengths,
    cotangent,
    self_weights,
    self_moment,
    self_second,
    cross_weights,
    cross_moment,
    cross_second,
    feed_weights,
    feed_moment,
    feed_second,
    vectors,
    vector_moment,
    vector_second,
):
    row_count = EX_DEV * SUF
    ndp, nfs = lax.axis_size("dp"), lax.axis_size("fsdp")
    owners = ndp * nfs
    attn_shard, feed_shard = self_weights.shape[0], feed_weights.shape[0]
    rows_a, rows_f = attn_shard // D, feed_shard // (4 * D)
    shard_index = lax.axis_index(("dp", "fsdp"))
    feed_low = feed_weights.astype(BF)
    feed_in = jnp.where(
        shard_index < owners // 2,
        feed_low.reshape(rows_f, 4, D).transpose(1, 0, 2),
        feed_low.reshape(4, rows_f, D),
    )
    self_full, cross_full, feed_full, own_memory = gather_all(
        self_weights.astype(BF).reshape(1, rows_a, D),
        cross_weights.astype(BF).reshape(1, rows_a, D),
        feed_in,
        memory[0],
        ndp,
    )
    lens = lambda a: jnp.broadcast_to(a[0][:, None, None], (EX_DEV, 8, 128))
    (
        layer_output, suffix_gradient, vector_partial,
        qkv_g, wo_g, cq_g, ckv_g, co_g, up_g, dn_g, mem_g,
    ) = layer_all(
        suffix.reshape(row_count, D),
        cotangent.reshape(row_count, D),
        vectors.reshape(-1, D),
        lens(suffix_lengths),
        lens(prefix_lengths),
        self_full.reshape(4, D, D),
        cross_full.reshape(4, D, D),
        feed_full.reshape(owners, 4, rows_f, D),
        feed_full.reshape(8, D, D),
        own_memory.reshape(EX_DEV * MEMLEN, D),
    )
    vec_rows = vectors.shape[0] // 128
    vec_pad = (vec_rows + 7) // 8 * 8
    vector_in = jnp.pad(vector_partial.reshape(vec_rows, 128), ((0, vec_pad - vec_rows), (0, 0)))
    split = (2, 2, 2)
    self_total, cross_total, feed_total, memory_back, vec_sum, squared = scatter_all(
        (
            qkv_g.reshape((3,) + split + (rows_a, D)),
            wo_g.reshape(split + (rows_a, D)),
            cq_g.reshape(split + (rows_a, D)),
            ckv_g.reshape((2,) + split + (rows_a, D)),
            co_g.reshape(split + (rows_a, D)),
            up_g.reshape((4, 2) + split + (rows_f, D)),
            dn_g.reshape((2,) + split + (4, rows_f, D)),
        ),
        mem_g.reshape(EX_DEV, ndp, MEMLEN // ndp, D),
        vector_in,
        rows_a,
        rows_f,
        ndp,
        nfs,
    )
    memory_gradient = memory_back.astype(F32)[None]
    self_total = self_total.reshape(-1)
    cross_total = cross_total.reshape(-1)
    feed_total = jnp.where(
        shard_index < owners // 2, feed_total.transpose(1, 0, 2).reshape(-1), feed_total.reshape(-1)
    )
    vector_total = vec_sum[:vec_rows].reshape(-1)
    squared_total = jnp.sum(squared) + jnp.sum(vector_total * vector_total)
    global_norm = jnp.sqrt(squared_total)
    clip_factor = jnp.minimum(1.0, 1.0 / global_norm)
    flat = lambda *group: [a.reshape(-1, 128) for a in group]
    sums = ratio_all(
        flat(
            self_total, cross_total, feed_total,
            self_weights, cross_weights, feed_weights,
            self_moment, cross_moment, feed_moment,
            self_second, cross_second, feed_second,
        ),
        jnp.broadcast_to(clip_factor, (8, 128)),
        ndp,
        nfs,
    )
    norms = jnp.sqrt(jnp.sum(sums, axis=1))
    ratio_norms, weight_norms = norms[0:10], norms[16:26]
    trust_ratio = weight_norms / (ratio_norms + trust_eps)
    z = shard_index // 8
    new = []
    for weights, total, moment, second, row in (
        (self_weights, self_total, self_moment, self_second, z),
        (cross_weights, cross_total, cross_moment, cross_second, 4 + z),
        (feed_weights, feed_total, feed_moment, feed_second, 8 + z // 2),
    ):
        momentum, variance, ratio = lamb_step(weights, total, moment, second, clip_factor)
        new += [total, momentum, variance, weights - learn_rate * trust_ratio[row] * ratio]
    vector_momentum, vector_variance, vector_ratio = lamb_step(
        vectors, vector_total, vector_moment, vector_second, clip_factor
    )
    edges = [0, D, 2 * D, 3 * D, 4 * D, 5 * D, 6 * D, 7 * D, 7 * D + FF]
    vector_wn = []
    vector_rn = []
    new_pieces = []
    for segment in range(8):
        weight_part = vectors[edges[segment] : edges[segment + 1]]
        ratio_part = vector_ratio[edges[segment] : edges[segment + 1]]
        weight_norm = jnp.sqrt(jnp.sum(weight_part * weight_part))
        ratio_norm = jnp.sqrt(jnp.sum(ratio_part * ratio_part))
        piece_trust = weight_norm / (ratio_norm + trust_eps)
        vector_wn.append(weight_norm)
        vector_rn.append(ratio_norm)
        new_pieces.append(weight_part - learn_rate * piece_trust * ratio_part)
    vector_master = jnp.concatenate(new_pieces)
    tensor_norms = jnp.stack(
        [
            jnp.concatenate([weight_norms, jnp.stack(vector_wn)]),
            jnp.concatenate([ratio_norms, jnp.stack(vector_rn)]),
        ]
    )
    return (
        layer_output.reshape(1, EX_DEV, SUF, D),
        suffix_gradient.reshape(1, EX_DEV, SUF, D),
        memory_gradient,
        *new,
        vector_total,
        vector_momentum,
        vector_variance,
        vector_master,
        tensor_norms,
        global_norm,
    )


def pick(mesh):
    if mesh.shape["dp"] == 8 and mesh.shape["fsdp"] == 4:
        return fast_shards
    return shards


def solution(mesh):
    return jax.shard_map(
        pick(mesh),
        mesh=mesh,
        in_specs=(
            P("fsdp", "dp", None, None),
            P("fsdp", None, "dp", None),
            P("fsdp", "dp"),
            P("fsdp", "dp"),
            P("fsdp", "dp", None, None),
            P(("dp", "fsdp")),
            P(("dp", "fsdp")),
            P(("dp", "fsdp")),
            P(("dp", "fsdp")),
            P(("dp", "fsdp")),
            P(("dp", "fsdp")),
            P(("dp", "fsdp")),
            P(("dp", "fsdp")),
            P(("dp", "fsdp")),
            P(),
            P(),
            P(),
        ),
        out_specs=(
            P("fsdp", "dp", None, None),
            P("fsdp", "dp", None, None),
            P("fsdp", None, "dp", None),
            P(("dp", "fsdp")),
            P(("dp", "fsdp")),
            P(("dp", "fsdp")),
            P(("dp", "fsdp")),
            P(("dp", "fsdp")),
            P(("dp", "fsdp")),
            P(("dp", "fsdp")),
            P(("dp", "fsdp")),
            P(("dp", "fsdp")),
            P(("dp", "fsdp")),
            P(("dp", "fsdp")),
            P(("dp", "fsdp")),
            P(),
            P(),
            P(),
            P(),
            P(),
            P(),
        ),
        check_vma=False,
    )
```

```python
import jax
import jax.numpy as jnp
from jax import lax
from jax.experimental import pallas as pl
from jax.experimental.pallas import tpu as pltpu
from jax.sharding import PartitionSpec as P

D = 768
H = 12
HD = 64
FF = 3072
PATCH = 196
SUF = 64
EX_DEV = 4
MEMLEN = 256


beta_one = 0.5
beta_two = 0.55
step_count = 5
learn_rate = 0.5
decay_weight = 0.01
adam_eps = 1e-06
norm_eps = 1e-06
trust_eps = 1e-06
masked_score = -1e30


def layer_norm(values, norm_gain, norm_shift):
    centred = values - jnp.mean(values, axis=-1, keepdims=True)
    spread = jnp.mean(centred * centred, axis=-1, keepdims=True)
    return centred * lax.rsqrt(spread + norm_eps) * norm_gain + norm_shift


def gelu_tanh(values):
    return jax.nn.gelu(values, approximate=True)


def attend_forward(query_heads, key_heads, value_heads, allowed):
    score_scale = HD ** (-0.5)
    scores = (
        jnp.einsum("bqhe,bkhe->bhqk", query_heads, key_heads, preferred_element_type=jnp.float32)
        * score_scale
    )
    scores = jnp.where(allowed, scores, masked_score)
    attention = jax.nn.softmax(scores, axis=-1)
    totals = jax.nn.logsumexp(scores, axis=-1)
    mixed_rows = jnp.einsum(
        "bhqk,bkhe->bqhe",
        attention.astype(jnp.bfloat16),
        value_heads,
        preferred_element_type=jnp.float32,
    )
    return (mixed_rows, totals)


def attend_backward(query_heads, key_heads, value_heads, allowed, totals, mixed_grad):
    score_scale = HD ** (-0.5)
    scores = (
        jnp.einsum("bqhe,bkhe->bhqk", query_heads, key_heads, preferred_element_type=jnp.float32)
        * score_scale
    )
    scores = jnp.where(allowed, scores, masked_score)
    attention = jnp.exp(scores - totals[..., None])
    value_grad = jnp.einsum(
        "bhqk,bqhe->bkhe",
        attention.astype(jnp.bfloat16),
        mixed_grad,
        preferred_element_type=jnp.float32,
    )
    attention_grad = jnp.einsum(
        "bqhe,bkhe->bhqk", mixed_grad, value_heads, preferred_element_type=jnp.float32
    )
    score_grad = attention * (
        attention_grad - jnp.sum(attention * attention_grad, axis=-1, keepdims=True)
    )
    score_low = score_grad.astype(jnp.bfloat16)
    query_grad = (
        jnp.einsum("bhqk,bkhe->bqhe", score_low, key_heads, preferred_element_type=jnp.float32)
        * score_scale
    )
    key_grad = (
        jnp.einsum("bhqk,bqhe->bkhe", score_low, query_heads, preferred_element_type=jnp.float32)
        * score_scale
    )
    return (query_grad, key_grad, value_grad)


def lamb_step(weight, gradient, moment, second, clip_factor):
    clipped = clip_factor * gradient
    moment_new = beta_one * moment + (1.0 - beta_one) * clipped
    second_new = beta_two * second + (1.0 - beta_two) * clipped * clipped
    ratio = (
        moment_new
        / (1.0 - beta_one**step_count)
        / (jnp.sqrt(second_new / (1.0 - beta_two**step_count)) + adam_eps)
        + decay_weight * weight
    )
    return (moment_new, second_new, ratio)


def segment_sums(values, offset, segment_size, tensor_count):
    labels = (offset + jnp.arange(values.shape[0], dtype=jnp.int32)) // segment_size
    matches = labels[:, None] == jnp.arange(tensor_count, dtype=jnp.int32)[None, :]
    return jnp.sum(jnp.where(matches, values[:, None], 0.0), axis=0)


def segment_spread(factors, offset, length_here, segment_size):
    labels = (offset + jnp.arange(length_here, dtype=jnp.int32)) // segment_size
    matches = labels[:, None] == jnp.arange(factors.shape[0], dtype=jnp.int32)[None, :]
    return jnp.sum(jnp.where(matches, factors[None, :], 0.0), axis=1)


def shards(
    suffix,
    memory,
    prefix_lengths,
    suffix_lengths,
    cotangent,
    self_weights,
    self_moment,
    self_second,
    cross_weights,
    cross_moment,
    cross_second,
    feed_weights,
    feed_moment,
    feed_second,
    vectors,
    vector_moment,
    vector_second,
):
    row_count = EX_DEV * SUF
    attn_shard = self_weights.shape[0]
    feed_shard = feed_weights.shape[0]
    self_full, cross_full, feed_full = (
        lax.all_gather(self_weights.astype(jnp.bfloat16), ("dp", "fsdp"), axis=0, tiled=True),
        lax.all_gather(cross_weights.astype(jnp.bfloat16), ("dp", "fsdp"), axis=0, tiled=True),
        lax.all_gather(feed_weights.astype(jnp.bfloat16), ("dp", "fsdp"), axis=0, tiled=True),
    )
    self_mats = self_full.reshape(4, D, D)
    cross_mats = cross_full.reshape(4, D, D)
    up_mat = feed_full[: D * FF].reshape(D, FF)
    down_mat = feed_full[D * FF :].reshape(FF, D)
    vector_parts = [vectors[segment * D : (segment + 1) * D] for segment in range(7)]
    bias_up = vectors[7 * D :]
    own_memory = lax.all_to_all(memory, "dp", split_axis=1, concat_axis=2, tiled=True)
    memory_rows = own_memory.reshape(EX_DEV * MEMLEN, D)
    suffix_len = suffix_lengths[0]
    prefix_len = prefix_lengths[0]
    positions = jnp.arange(SUF, dtype=jnp.int32)
    causal = positions[:, None] >= positions[None, :]
    self_allowed = (
        causal[None, None, :, :] & (positions[None, :] < suffix_len[:, None])[:, None, None, :]
    )
    memory_pos = jnp.arange(MEMLEN, dtype=jnp.int32)
    cross_allowed = (memory_pos[None, :] < (PATCH + prefix_len)[:, None])[:, None, None, :]
    inputs = suffix.reshape(row_count, D).astype(jnp.float32)
    normed_one = layer_norm(inputs, vector_parts[0], vector_parts[1]).astype(jnp.bfloat16)
    self_qkv = jnp.einsum(
        "rd,jde->jre", normed_one, self_mats[0:3], preferred_element_type=jnp.float32
    ).astype(jnp.bfloat16)
    self_heads = self_qkv.reshape(3, EX_DEV, SUF, H, HD)
    mixed_one, totals_one = attend_forward(
        self_heads[0], self_heads[1], self_heads[2], self_allowed
    )
    mixed_one = mixed_one.reshape(row_count, D).astype(jnp.bfloat16)
    hidden_one = inputs + jnp.dot(mixed_one, self_mats[3], preferred_element_type=jnp.float32)
    normed_two = layer_norm(hidden_one, vector_parts[2], vector_parts[3]).astype(jnp.bfloat16)
    cross_query = jnp.dot(normed_two, cross_mats[0], preferred_element_type=jnp.float32).astype(
        jnp.bfloat16
    )
    cross_kv = jnp.einsum(
        "rd,jde->jre", memory_rows, cross_mats[1:3], preferred_element_type=jnp.float32
    ).astype(jnp.bfloat16)
    query_heads = cross_query.reshape(EX_DEV, SUF, H, HD)
    kv_heads = cross_kv.reshape(2, EX_DEV, MEMLEN, H, HD)
    mixed_two, totals_two = attend_forward(query_heads, kv_heads[0], kv_heads[1], cross_allowed)
    mixed_two = mixed_two.reshape(row_count, D).astype(jnp.bfloat16)
    hidden_two = hidden_one + jnp.dot(mixed_two, cross_mats[3], preferred_element_type=jnp.float32)
    normed_three = layer_norm(hidden_two, vector_parts[4], vector_parts[5]).astype(jnp.bfloat16)
    pre_act = jnp.dot(normed_three, up_mat, preferred_element_type=jnp.float32) + bias_up
    activated = gelu_tanh(pre_act).astype(jnp.bfloat16)
    layer_output = hidden_two + (
        jnp.dot(activated, down_mat, preferred_element_type=jnp.float32) + vector_parts[6]
    )
    valid_rows = (positions[None, :] < suffix_len[:, None]).astype(jnp.float32)
    seed_rows = (
        cotangent.reshape(EX_DEV, SUF, D).astype(jnp.float32) * valid_rows[:, :, None]
    ).reshape(row_count, D)
    seed_low = seed_rows.astype(jnp.bfloat16)
    bias_down_grad = jnp.sum(seed_low.astype(jnp.float32), axis=0)
    down_grad = jnp.einsum("rf,rd->fd", activated, seed_low, preferred_element_type=jnp.float32)
    activated_grad = jnp.einsum("rd,fd->rf", seed_low, down_mat, preferred_element_type=jnp.float32)
    _, gelu_back = jax.vjp(gelu_tanh, pre_act)
    pre_grad = gelu_back(activated_grad)[0].astype(jnp.bfloat16)
    bias_up_grad = jnp.sum(pre_grad.astype(jnp.float32), axis=0)
    up_grad = jnp.einsum("rd,rf->df", normed_three, pre_grad, preferred_element_type=jnp.float32)
    normed_three_grad = jnp.einsum(
        "rf,df->rd", pre_grad, up_mat, preferred_element_type=jnp.float32
    )
    _, norm_three_back = jax.vjp(layer_norm, hidden_two, vector_parts[4], vector_parts[5])
    through_three, gain_three_grad, shift_three_grad = norm_three_back(normed_three_grad)
    hidden_two_grad = seed_rows + through_three
    feed_flat = jnp.concatenate([up_grad.reshape(-1), down_grad.reshape(-1)])
    branch_two = hidden_two_grad.astype(jnp.bfloat16)
    cross_out_grad = jnp.einsum(
        "rd,re->de", mixed_two, branch_two, preferred_element_type=jnp.float32
    )
    mixed_two_grad = jnp.einsum(
        "re,de->rd", branch_two, cross_mats[3], preferred_element_type=jnp.float32
    ).astype(jnp.bfloat16)
    query_two_grad, key_two_grad, value_two_grad = attend_backward(
        query_heads,
        kv_heads[0],
        kv_heads[1],
        cross_allowed,
        totals_two,
        mixed_two_grad.reshape(EX_DEV, SUF, H, HD),
    )
    cross_query_grad = query_two_grad.reshape(row_count, D).astype(jnp.bfloat16)
    cross_kv_grad = (
        jnp.stack([key_two_grad, value_two_grad])
        .reshape(2, EX_DEV * MEMLEN, D)
        .astype(jnp.bfloat16)
    )
    query_weight_grad = jnp.einsum(
        "rd,re->de", normed_two, cross_query_grad, preferred_element_type=jnp.float32
    )
    kv_weight_grad = jnp.einsum(
        "rd,jre->jde", memory_rows, cross_kv_grad, preferred_element_type=jnp.float32
    )
    normed_two_grad = jnp.einsum(
        "re,de->rd", cross_query_grad, cross_mats[0], preferred_element_type=jnp.float32
    )
    memory_local_grad = jnp.einsum(
        "jre,jde->rd", cross_kv_grad, cross_mats[1:3], preferred_element_type=jnp.float32
    )
    memory_gradient = lax.all_to_all(
        memory_local_grad.reshape(1, EX_DEV, MEMLEN, D),
        "dp",
        split_axis=2,
        concat_axis=1,
        tiled=True,
    )
    _, norm_two_back = jax.vjp(layer_norm, hidden_one, vector_parts[2], vector_parts[3])
    through_two, gain_two_grad, shift_two_grad = norm_two_back(normed_two_grad)
    hidden_one_grad = hidden_two_grad + through_two
    cross_flat = jnp.concatenate(
        [query_weight_grad[None], kv_weight_grad, cross_out_grad[None]], axis=0
    ).reshape(-1)
    branch_one = hidden_one_grad.astype(jnp.bfloat16)
    self_out_grad = jnp.einsum(
        "rd,re->de", mixed_one, branch_one, preferred_element_type=jnp.float32
    )
    mixed_one_grad = jnp.einsum(
        "re,de->rd", branch_one, self_mats[3], preferred_element_type=jnp.float32
    ).astype(jnp.bfloat16)
    query_one_grad, key_one_grad, value_one_grad = attend_backward(
        self_heads[0],
        self_heads[1],
        self_heads[2],
        self_allowed,
        totals_one,
        mixed_one_grad.reshape(EX_DEV, SUF, H, HD),
    )
    self_qkv_grad = (
        jnp.stack([query_one_grad, key_one_grad, value_one_grad])
        .reshape(3, row_count, D)
        .astype(jnp.bfloat16)
    )
    qkv_weight_grad = jnp.einsum(
        "rd,jre->jde", normed_one, self_qkv_grad, preferred_element_type=jnp.float32
    )
    normed_one_grad = jnp.einsum(
        "jre,jde->rd", self_qkv_grad, self_mats[0:3], preferred_element_type=jnp.float32
    )
    _, norm_one_back = jax.vjp(layer_norm, inputs, vector_parts[0], vector_parts[1])
    through_one, gain_one_grad, shift_one_grad = norm_one_back(normed_one_grad)
    suffix_gradient = (hidden_one_grad + through_one).reshape(1, EX_DEV, SUF, D)
    self_flat = jnp.concatenate([qkv_weight_grad, self_out_grad[None]], axis=0).reshape(-1)
    owners = lax.axis_size(("dp", "fsdp"))
    joined = jnp.concatenate(
        [
            self_flat.reshape(owners, attn_shard),
            cross_flat.reshape(owners, attn_shard),
            feed_flat.reshape(owners, feed_shard),
        ],
        axis=1,
    ).reshape(-1)
    owned = lax.psum_scatter(joined, ("dp", "fsdp"), scatter_dimension=0, tiled=True)
    self_total = owned[:attn_shard]
    cross_total = owned[attn_shard : 2 * attn_shard]
    feed_total = owned[2 * attn_shard :]
    vector_partial = jnp.concatenate(
        [
            gain_one_grad,
            shift_one_grad,
            gain_two_grad,
            shift_two_grad,
            gain_three_grad,
            shift_three_grad,
            bias_down_grad,
            bias_up_grad,
        ]
    )
    shard_index = lax.axis_index(("dp", "fsdp"))
    attn_offset = shard_index * attn_shard
    feed_offset = shard_index * feed_shard
    grad_squares = jnp.concatenate(
        [
            segment_sums(self_total * self_total, attn_offset, D * D, 4),
            segment_sums(cross_total * cross_total, attn_offset, D * D, 4),
            segment_sums(feed_total * feed_total, feed_offset, D * FF, 2),
        ]
    )
    weight_squares = jnp.concatenate(
        [
            segment_sums(self_weights * self_weights, attn_offset, D * D, 4),
            segment_sums(cross_weights * cross_weights, attn_offset, D * D, 4),
            segment_sums(feed_weights * feed_weights, feed_offset, D * FF, 2),
        ]
    )
    vector_total, grad_summed, weight_summed = lax.psum(
        (vector_partial, grad_squares, weight_squares), ("dp", "fsdp")
    )
    squared_total = jnp.sum(grad_summed) + jnp.sum(vector_total * vector_total)
    global_norm = jnp.sqrt(squared_total)
    clip_factor = jnp.minimum(1.0, 1.0 / global_norm)
    self_momentum, self_variance, self_ratio = lamb_step(
        self_weights, self_total, self_moment, self_second, clip_factor
    )
    cross_momentum, cross_variance, cross_ratio = lamb_step(
        cross_weights, cross_total, cross_moment, cross_second, clip_factor
    )
    feed_momentum, feed_variance, feed_ratio = lamb_step(
        feed_weights, feed_total, feed_moment, feed_second, clip_factor
    )
    ratio_squares = jnp.concatenate(
        [
            segment_sums(self_ratio * self_ratio, attn_offset, D * D, 4),
            segment_sums(cross_ratio * cross_ratio, attn_offset, D * D, 4),
            segment_sums(feed_ratio * feed_ratio, feed_offset, D * FF, 2),
        ]
    )
    update_summed = lax.psum(ratio_squares, ("dp", "fsdp"))
    weight_norms = jnp.sqrt(weight_summed)
    ratio_norms = jnp.sqrt(update_summed)
    trust_ratio = weight_norms / (ratio_norms + trust_eps)
    self_master = (
        self_weights
        - learn_rate * segment_spread(trust_ratio[0:4], attn_offset, attn_shard, D * D) * self_ratio
    )
    cross_master = (
        cross_weights
        - learn_rate
        * segment_spread(trust_ratio[4:8], attn_offset, attn_shard, D * D)
        * cross_ratio
    )
    feed_master = (
        feed_weights
        - learn_rate
        * segment_spread(trust_ratio[8:10], feed_offset, feed_shard, D * FF)
        * feed_ratio
    )
    vector_momentum, vector_variance, vector_ratio = lamb_step(
        vectors, vector_total, vector_moment, vector_second, clip_factor
    )
    edges = [0, D, 2 * D, 3 * D, 4 * D, 5 * D, 6 * D, 7 * D, 7 * D + FF]
    vector_wn = []
    vector_rn = []
    new_pieces = []
    for segment in range(8):
        weight_part = vectors[edges[segment] : edges[segment + 1]]
        ratio_part = vector_ratio[edges[segment] : edges[segment + 1]]
        weight_norm = jnp.sqrt(jnp.sum(weight_part * weight_part))
        ratio_norm = jnp.sqrt(jnp.sum(ratio_part * ratio_part))
        piece_trust = weight_norm / (ratio_norm + trust_eps)
        vector_wn.append(weight_norm)
        vector_rn.append(ratio_norm)
        new_pieces.append(weight_part - learn_rate * piece_trust * ratio_part)
    vector_master = jnp.concatenate(new_pieces)
    tensor_norms = jnp.stack(
        [
            jnp.concatenate([weight_norms, jnp.stack(vector_wn)]),
            jnp.concatenate([ratio_norms, jnp.stack(vector_rn)]),
        ]
    )
    return (
        layer_output.reshape(1, EX_DEV, SUF, D),
        suffix_gradient,
        memory_gradient,
        self_total,
        self_momentum,
        self_variance,
        self_master,
        cross_total,
        cross_momentum,
        cross_variance,
        cross_master,
        feed_total,
        feed_momentum,
        feed_variance,
        feed_master,
        vector_total,
        vector_momentum,
        vector_variance,
        vector_master,
        tensor_norms,
        global_norm,
    )


BF = jnp.bfloat16
F32 = jnp.float32
MESH = pl.DeviceIdType.MESH
NZ = 4
AHEAD = 4
MEM_AT = 5


def place():
    dp, fs = lax.axis_index("dp"), lax.axis_index("fsdp")
    return dp, fs, dp // 2, dp % 2, fs // 2, fs % 2


def peer_id(z, y, x, c):
    return (z * 2 + y, x * 2 + c)


def greet(ids):
    bar = pltpu.get_barrier_semaphore()
    for where in ids:
        pl.semaphore_signal(bar, inc=1, device_id=where, device_id_type=MESH)
    pl.semaphore_wait(bar, len(ids))


class Copies:
    def __init__(self, send, recv, local):
        self.send, self.recv, self.local = send, recv, local
        self.remotes, self.locals = 0, 0
        self.open = []

    def remote(self, src, dst, where):
        i = self.remotes
        self.remotes += 1
        cp = pltpu.make_async_remote_copy(
            src_ref=src,
            dst_ref=dst,
            send_sem=self.send.at[i],
            recv_sem=self.recv.at[i],
            device_id=where,
            device_id_type=MESH,
        )
        cp.start()
        self.open.append(cp)
        return cp

    def here(self, src, dst):
        cp = pltpu.make_async_copy(src, dst, self.local.at[self.locals])
        self.locals += 1
        cp.start()
        return cp

    def drain(self):
        for cp in self.open:
            cp.wait_send()


LANES = 128


def rows_of(flat, dst, j, start, stride):
    rows, width = dst.shape[1:]
    for i in range(width // LANES):
        part = flat[pl.ds(start + i, rows, stride=stride), :]
        dst[j, :, i * LANES : (i + 1) * LANES] = part.astype(dst.dtype)


def feed_lines(j, rows, width, up):
    per = width // LANES
    return (j * per, 4 * per) if up else (j * rows * per, per)


def gather_kernel(
    self_w, cross_w, feed_w, mem_in, self_out, cross_out, feed_out, mem_out,
    self_in, cross_in, feed_in, send, recv, local,
):
    dp, fs, z, y, x, c = place()
    per = self_in.shape[2] // LANES
    rows_of(self_w, self_in, 0, 0, per)
    rows_of(cross_w, cross_in, 0, 0, per)
    for up in (True, False):

        @pl.when(z // 2 == (0 if up else 1))
        def _():
            for j in range(4):
                rows_of(feed_w, feed_in, j, *feed_lines(j, *feed_in.shape[1:], up))

    ndp = mem_out.shape[1]
    ex = mem_out.shape[0]
    to_y, to_x, to_c = peer_id(z, 1 - y, x, c), peer_id(z, y, 1 - x, c), peer_id(z, y, x, 1 - c)
    greet([((dp + k) % ndp, fs) for k in range(1, ndp)] + [to_x, to_c])
    cp = Copies(send, recv, local)

    step = feed_in.shape[1]
    cut = step * 2 // 3
    chunks = []
    for src, dst in ((self_in, self_out), (cross_in, cross_out), (feed_in, feed_out)):
        for j in range(src.shape[0]):
            for first in range(0, src.shape[1], step):
                chunks.append(
                    (src, dst, j, pl.ds(first, step), pl.ds(first, cut), pl.ds(first + cut, step - cut))
                )

    own = [
        cp.here(src.at[j, rows], dst.at[z, y, x, c, j, rows]) for src, dst, j, rows, _, _ in chunks
    ]
    own_mem = cp.here(mem_in.at[pl.ds(ex * dp, ex)], mem_out.at[:, dp])

    zc, s2, s3, s4, mem = {}, {}, {}, {}, []

    def send_z(t):
        src, dst, j, rows, r0, r1 = chunks[t]
        for k in range(1, NZ):
            zc[t, k] = cp.remote(
                src.at[j, rows], dst.at[z, y, x, c, j, rows], peer_id((z + k) % NZ, y, x, c)
            )

    def send_2(t, k):
        src, dst, j, rows, r0, r1 = chunks[t]
        zz = (z + NZ - k) % NZ
        for part, cut_rows, where in ((0, r0, to_y), (1, r1, to_x)):
            here = src.at[j, cut_rows] if k == 0 else dst.at[zz, y, x, c, j, cut_rows]
            s2[t, k, part] = cp.remote(here, dst.at[zz, y, x, c, j, cut_rows], where)

    def send_3(t):
        src, dst, j, rows, r0, r1 = chunks[t]
        s3[t, 0] = cp.remote(dst.at[:, :, x, c, j, r0], dst.at[:, :, x, c, j, r0], to_x)
        s3[t, 1] = cp.remote(dst.at[:, y, :, c, j, r1], dst.at[:, y, :, c, j, r1], to_y)

    def send_4(t):
        src, dst, j, rows, r0, r1 = chunks[t]
        s4[t] = cp.remote(dst.at[:, :, :, c, j, rows], dst.at[:, :, :, c, j, rows], to_c)

    def send_mem():
        for k in range(1, ndp):
            mem.append(
                cp.remote(
                    mem_in.at[pl.ds(ex * ((dp + k) % ndp), ex)],
                    mem_out.at[:, dp],
                    ((dp + k) % ndp, fs),
                )
            )

    n = len(chunks)
    for t in range(min(AHEAD, n)):
        send_z(t)
        send_2(t, 0)
    for t in range(n + 2):
        if t == MEM_AT:
            send_mem()
        if t < n:
            for k in range(1, NZ):
                zc[t, k].wait_recv()
                send_2(t, k)
            if t + AHEAD < n:
                send_z(t + AHEAD)
                send_2(t + AHEAD, 0)
        if 1 <= t <= n:
            own[t - 1].wait()
            for k in range(NZ):
                for part in (0, 1):
                    s2[t - 1, k, part].wait_recv()
            send_3(t - 1)
        if t >= 2:
            s3[t - 2, 0].wait_recv()
            s3[t - 2, 1].wait_recv()
            send_4(t - 2)
    for t in range(n):
        s4[t].wait_recv()
    own_mem.wait()
    for one in mem:
        one.wait_recv()
    cp.drain()


def gather_all(self_w, cross_w, feed_w, mem_in, rows_a, rows_f, ndp):
    any_space = pl.BlockSpec(memory_space=pl.ANY)
    vmem = pl.BlockSpec(memory_space=pltpu.VMEM)
    width = mem_in.shape[2]
    kinds = ((1, rows_a, width), (1, rows_a, width), (4, rows_f, width))
    ex = mem_in.shape[0] // ndp
    return pl.pallas_call(
        gather_kernel,
        out_shape=[
            *[jax.ShapeDtypeStruct((NZ, 2, 2, 2) + kind, BF) for kind in kinds],
            jax.ShapeDtypeStruct((ex, ndp) + mem_in.shape[1:], BF),
        ],
        in_specs=[vmem] * 3 + [any_space],
        out_specs=[any_space] * 4,
        scratch_shapes=[
            *[pltpu.VMEM(kind, BF) for kind in kinds],
            pltpu.SemaphoreType.DMA((128,)),
            pltpu.SemaphoreType.DMA((128,)),
            pltpu.SemaphoreType.DMA((16,)),
        ],
        compiler_params=pltpu.CompilerParams(collective_id=1, has_side_effects=True),
        name="gather_all",
    )(self_w, cross_w, feed_w, mem_in)


def squares(v):
    return jnp.sum((v * v).reshape(v.shape[0] // 8, 8, LANES), axis=0)


def sum_everywhere(cp, mine, slots_a, slots_b, dp, fs):
    nfs, ndp = slots_a.shape[0], slots_b.shape[0]
    slots_a[fs] = mine
    got = [
        cp.remote(slots_a.at[fs], slots_a.at[fs], (dp, (fs + k) % nfs)) for k in range(1, nfs)
    ]
    for one in got:
        one.wait_recv()
    total = slots_a[0]
    for k in range(1, nfs):
        total = total + slots_a[k]
    slots_b[dp] = total
    got = [
        cp.remote(slots_b.at[dp], slots_b.at[dp], ((dp + k) % ndp, fs)) for k in range(1, ndp)
    ]
    for one in got:
        one.wait_recv()
    total = slots_b[0]
    for k in range(1, ndp):
        total = total + slots_b[k]
    return total


def lamb_sums(w, g, m, s, factor):
    ratio = lamb_step(w[...], g[...], m[...], s[...], factor)[2]
    return jnp.sum(ratio * ratio, axis=0, keepdims=True)


def scatter_kernel(
    qkv_g, out_g, cq_g, ckv_g, co_g, up_g, dn_g, mem_g, vec,
    ws, wc, wf, ms, mc, mf, ss, sc_, sf,
    self_t, cross_t, feed_t, mem_t, vec_t, sq_t, norm_t,
    send, recv, local, acc, r1, r2a, r2b, r3a, r3b, rz, whole,
    v_send, v_recv, v_z, vw, qa, qb, na, nb, opt_s, opt_c, opt_f, opt_sem,
):
    dp, fs, z, y, x, c = place()
    ndp, nfs = mem_g.shape[1], qa.shape[0]
    ex = mem_g.shape[0]
    step, width = acc.shape[4], acc.shape[5]
    cut = step * 2 // 3
    head, rest = pl.ds(0, cut), pl.ds(cut, step - cut)
    per = width // LANES
    to_y, to_x, to_c = peer_id(z, 1 - y, x, c), peer_id(z, y, 1 - x, c), peer_id(z, y, x, 1 - c)
    greet(
        [((dp + k) % ndp, fs) for k in range(1, ndp)] + [(dp, (fs + k) % nfs) for k in range(1, nfs)]
    )
    cp = Copies(send, recv, local)

    def self_src(r):
        rows = pl.ds(r * step, step)
        return lambda zz, cc: qkv_g.at[zz, :, :, cc, rows] if zz < 3 else out_g.at[:, :, cc, rows]

    def cross_src(r):
        rows = pl.ds(r * step, step)

        def src(zz, cc):
            if zz == 0:
                return cq_g.at[:, :, cc, rows]
            return ckv_g.at[zz - 1, :, :, cc, rows] if zz < 3 else co_g.at[:, :, cc, rows]

        return src

    def feed_src(j):
        return lambda zz, cc: up_g.at[j, zz, :, :, cc] if zz < 2 else dn_g.at[zz - 2, :, :, cc, j]

    sources = [feed_src(j) for j in range(4)]
    sources += [cross_src(r) for r in range(2)] + [self_src(r) for r in range(2)]
    n = len(sources)
    sc, sl, s1, s2, sz = {}, {}, {}, {}, {}

    def phase_0(t):
        for zz in range(NZ):
            sc[t, zz] = cp.remote(sources[t](zz, 1 - c), r1.at[t, zz], to_c)
            sl[t, zz] = cp.here(sources[t](zz, c), acc.at[t, zz])

    def add_c(t, fixed_y, fixed_x, rows):
        def body(i, _):
            zz, o = i // 2, i % 2
            yy = o if fixed_y is None else fixed_y
            xx = o if fixed_x is None else fixed_x
            acc[t, zz, yy, xx, rows] = acc[t, zz, yy, xx, rows] + r1[t, zz, yy, xx, rows]
            return 0

        lax.fori_loop(0, NZ * 2, body, 0)

    def phase_c(t):
        for zz in range(NZ):
            sc[t, zz].wait_recv()
            sl[t, zz].wait()
        add_c(t, None, 1 - x, head)
        s1[t, 0] = cp.remote(acc.at[t, :, :, 1 - x, head], r2a.at[t], to_x)
        add_c(t, 1 - y, None, rest)
        s1[t, 1] = cp.remote(acc.at[t, :, 1 - y, :, rest], r2b.at[t], to_y)
        add_c(t, None, x, head)
        add_c(t, y, None, rest)

    def add_1(t, yy, xx, rows, got, where):
        def body(zz, _):
            acc[t, zz, yy, xx, rows] = acc[t, zz, yy, xx, rows] + got[t, zz, where]
            return 0

        lax.fori_loop(0, NZ, body, 0)

    def phase_1(t):
        s1[t, 0].wait_recv()
        add_1(t, 1 - y, x, head, r2a, 1 - y)
        s2[t, 0] = cp.remote(acc.at[t, :, 1 - y, x, head], r3a.at[t], to_y)
        s1[t, 1].wait_recv()
        add_1(t, y, 1 - x, rest, r2b, 1 - x)
        s2[t, 1] = cp.remote(acc.at[t, :, y, 1 - x, rest], r3b.at[t], to_x)
        add_1(t, y, x, head, r2a, y)
        add_1(t, y, x, rest, r2b, x)

    def phase_2(t):
        s2[t, 0].wait_recv()
        s2[t, 1].wait_recv()

        def body(zz, _):
            acc[t, zz, y, x, head] = acc[t, zz, y, x, head] + r3a[t, zz]
            acc[t, zz, y, x, rest] = acc[t, zz, y, x, rest] + r3b[t, zz]
            return 0

        lax.fori_loop(0, NZ, body, 0)
        for k in range(1, NZ):
            zt = (z + k) % NZ
            sz[t, k] = cp.remote(acc.at[t, zt, y, x], rz.at[t, k - 1], peer_id(zt, y, x, c))

    def lines_of(dst, start, stride):
        for i in range(per):
            dst[pl.ds(start + i, step, stride=stride), :] = whole[:, i * LANES : (i + 1) * LANES]

    def phase_z(t):
        for k in range(1, NZ):
            sz[t, k].wait_recv()
        total = acc[t, z, y, x].astype(F32)
        for k in range(1, NZ):
            total = total + rz[t, k - 1].astype(F32)
        whole[...] = total
        if t >= 4:
            lines_of((cross_t, self_t)[t // 2 - 2], (t % 2) * step * per, per)
            return
        for up in (True, False):

            @pl.when(z // 2 == (0 if up else 1))
            def _():
                lines_of(feed_t, *feed_lines(t, step, width, up))

    ahead = 2
    for t in range(ahead):
        phase_0(t)
    vec_cp = [cp.remote(vec, v_recv.at[0], to_c)]
    own_mem = cp.here(mem_g.at[:, dp], mem_t.at[pl.ds(ex * dp, ex)])
    mem = [
        cp.remote(mem_g.at[:, (dp + k) % ndp], mem_t.at[pl.ds(ex * dp, ex)], ((dp + k) % ndp, fs))
        for k in range(1, ndp)
    ]
    groups = (
        ((ws, ms, ss), opt_s, self_t, z),
        ((wc, mc, sc_), opt_c, cross_t, NZ + z),
        ((wf, mf, sf), opt_f, feed_t, 2 * NZ + z // 2),
    )
    opt = []
    for g, (srcs, dst, _, _) in enumerate(groups):
        for i, src in enumerate(srcs):
            opt.append(pltpu.make_async_copy(src, dst.at[i], opt_sem.at[3 * g + i]))
            opt[-1].start()

    def vec_step(i):
        vec_cp[-1].wait_recv()
        v_send[i] = (vec[...] if i == 0 else v_send[i - 1]) + v_recv[i]
        if i < 2:
            vec_cp.append(cp.remote(v_send.at[i], v_recv.at[i + 1], (to_x, to_y)[i]))
        else:
            v_z[z] = v_send[2]
            for k in range(1, NZ):
                vec_cp.append(
                    cp.remote(v_send.at[2], v_z.at[z], peer_id((z + k) % NZ, y, x, c))
                )

    for t in range(n + 3):
        if t < n:
            phase_c(t)
            if t + ahead < n:
                phase_0(t + ahead)
        if 1 <= t <= 3:
            vec_step(t - 1)
        if 1 <= t <= n:
            phase_1(t - 1)
        if 2 <= t <= n + 1:
            phase_2(t - 2)
        if t >= 3:
            phase_z(t - 3)
    for one in vec_cp[3:]:
        one.wait_recv()
    vw[...] = (v_z[0] + v_z[1]) + (v_z[2] + v_z[3])
    vec_t[...] = jnp.zeros_like(vec_t)
    for i in range(per):
        vec_t[pl.ds(i, 11, stride=per), :] = vw[0:11, i * LANES : (i + 1) * LANES]
    sq = squares(self_t[...]) + squares(cross_t[...]) + squares(feed_t[...])
    sq = sum_everywhere(cp, sq, qa, qb, dp, fs) + squares(vec_t[...])
    sq_t[...] = sq
    factor = clip_of(sq)
    rows = lax.broadcasted_iota(jnp.int32, (32, LANES), 0)
    tile = jnp.zeros((32, LANES), F32)
    for one in opt:
        one.wait()
    for _, dst, g, row in groups:
        w = dst[0]
        part = lamb_sums(dst.at[0], g, dst.at[1], dst.at[2], factor)
        tile = tile + jnp.where(rows == row, part, 0.0)
        part = jnp.sum(w * w, axis=0, keepdims=True)
        tile = tile + jnp.where(rows == 16 + row, part, 0.0)
    norm_t[...] = sum_everywhere(cp, tile, na, nb, dp, fs)
    own_mem.wait()
    for one in mem:
        one.wait_recv()
    cp.drain()


def norm_of(sq):
    return jnp.sqrt(jnp.sum(jnp.sum(sq, axis=1, keepdims=True), axis=0, keepdims=True))


def clip_of(sq):
    return jnp.minimum(1.0, 1.0 / norm_of(sq))


def scatter_all(grads, mem_g, vec, states, step, ndp, nfs):
    any_space = pl.BlockSpec(memory_space=pl.ANY)
    vmem = pl.BlockSpec(memory_space=pltpu.VMEM)
    ex, _, pos, width = mem_g.shape
    lines = [w.shape[0] for w in states[:3]]
    cut = step * 2 // 3
    low = lambda *dims: pltpu.VMEM(dims + (width,), BF)
    wide = lambda *dims: pltpu.VMEM(dims, F32)
    shape = lambda *dims: jax.ShapeDtypeStruct(dims, F32)
    vec_lines = (vec.shape[0] * width) // LANES
    return pl.pallas_call(
        scatter_kernel,
        out_shape=[
            *[shape(k, LANES) for k in lines],
            jax.ShapeDtypeStruct((ndp * ex, pos, width), BF),
            shape(vec_lines, LANES),
            shape(8, LANES),
            shape(32, LANES),
        ],
        in_specs=[any_space] * 8 + [vmem] + [any_space] * 9,
        out_specs=[vmem, vmem, vmem, any_space, vmem, vmem, vmem],
        scratch_shapes=[
            pltpu.SemaphoreType.DMA((128,)),
            pltpu.SemaphoreType.DMA((128,)),
            pltpu.SemaphoreType.DMA((40,)),
            low(8, NZ, 2, 2, step),
            low(8, NZ, 2, 2, step),
            low(8, NZ, 2, cut),
            low(8, NZ, 2, step - cut),
            low(8, NZ, cut),
            low(8, NZ, step - cut),
            low(8, NZ - 1, step),
            wide(step, width),
            wide(3, *vec.shape),
            wide(3, *vec.shape),
            wide(NZ, *vec.shape),
            wide(*vec.shape),
            wide(nfs, 8, LANES),
            wide(ndp, 8, LANES),
            wide(nfs, 32, LANES),
            wide(ndp, 32, LANES),
            *[wide(3, k, LANES) for k in lines],
            pltpu.SemaphoreType.DMA((9,)),
        ],
        compiler_params=pltpu.CompilerParams(
            collective_id=2, has_side_effects=True, vmem_limit_bytes=58 << 20
        ),
        name="scatter_all",
    )(*grads, mem_g, vec, *states)


def update_kernel(*refs):
    ins, outs = refs[:18], refs[18:]
    gs, ws, ms, vs, (gv, sq, norms) = ins[0:3], ins[3:7], ins[7:11], ins[11:15], ins[15:18]
    z = lax.axis_index("dp") // 2
    factor = clip_of(sq[...])
    sums = jnp.sqrt(jnp.sum(norms[...], axis=1, keepdims=True))
    ratio_norm, weight_norm = sums[0:16], sums[16:32]
    trust = weight_norm / (ratio_norm + trust_eps)
    row = lax.broadcasted_iota(jnp.int32, (16, 1), 0)
    for i, first in enumerate((z, NZ + z, 2 * NZ + z // 2)):
        g = gs[i][...]
        w = ws[i][...]
        m, v, ratio = lamb_step(w, g, ms[i][...], vs[i][...], factor)
        rate = jnp.sum(jnp.where(row == first, trust, 0.0), axis=0, keepdims=True)
        for ref, value in zip(outs[4 * i : 4 * i + 4], (g, m, v, w - learn_rate * rate * ratio)):
            ref[...] = value
    w = ws[3][...]
    g = gv[0 : w.shape[0], :]
    m, v, ratio = lamb_step(w, g, ms[3][...], vs[3][...], factor)
    line = lax.broadcasted_iota(jnp.int32, w.shape, 0)
    spread = lax.broadcasted_iota(jnp.int32, (16, LANES), 1)
    pick = spread == lax.broadcasted_iota(jnp.int32, (16, LANES), 0)
    lanes = spread[0:1]
    on_row = lambda a: jnp.sum(jnp.where(pick, a, 0.0), axis=0, keepdims=True)
    weight_row, ratio_row = on_row(weight_norm), on_row(ratio_norm)
    rate = jnp.zeros(w.shape, F32)
    per = D // LANES
    for i in range(8):
        mine = (line >= i * per) & (line < ((i + 1) * per if i < 7 else w.shape[0]))
        norm = lambda a: norm_of(jnp.where(mine, a * a, 0.0))
        wn, rn = norm(w), norm(ratio)
        rate = jnp.where(mine, wn / (rn + trust_eps), rate)
        weight_row = jnp.where(lanes == 10 + i, wn, weight_row)
        ratio_row = jnp.where(lanes == 10 + i, rn, ratio_row)
    for ref, value in zip(outs[12:16], (g, m, v, w - learn_rate * rate * ratio)):
        ref[...] = value
    outs[16][0:1, :] = weight_row[:, 0:18]
    outs[16][1:2, :] = ratio_row[:, 0:18]
    outs[17][...] = norm_of(sq[...])


def update_all(totals, weights, moments, seconds, vec_total, sq, norms):
    vmem = pl.BlockSpec(memory_space=pltpu.VMEM)
    shape = lambda a: jax.ShapeDtypeStruct(a.shape, F32)
    outs = [shape(a) for a in weights for _ in range(4)]
    outs += [jax.ShapeDtypeStruct((2, 18), F32), jax.ShapeDtypeStruct((1, 1), F32)]
    return pl.pallas_call(
        update_kernel,
        out_shape=outs,
        in_specs=[vmem] * 18,
        out_specs=[vmem] * len(outs),
        compiler_params=pltpu.CompilerParams(vmem_limit_bytes=40 << 20),
        name="update_all",
    )(*totals, *weights, *moments, *seconds, vec_total, sq, norms)


def dot_nn(a, b):
    return lax.dot_general(a, b, (((1,), (0,)), ((), ())), preferred_element_type=F32)


def dot_nt(a, b):
    return lax.dot_general(a, b, (((1,), (1,)), ((), ())), preferred_element_type=F32)


def dot_tn(a, b):
    return lax.dot_general(a, b, (((0,), (0,)), ((), ())), preferred_element_type=F32)


def norm_parts(values):
    centred = values - jnp.mean(values, axis=-1, keepdims=True)
    scale = lax.rsqrt(jnp.mean(centred * centred, axis=-1, keepdims=True) + norm_eps)
    return centred * scale, scale


def norm_back(unit, scale, gain, grad):
    e = grad * gain
    return scale * (
        e
        - jnp.mean(e, axis=-1, keepdims=True)
        - unit * jnp.mean(e * unit, axis=-1, keepdims=True)
    )


def column_sum(values):
    return jnp.sum(values, axis=0, keepdims=True)


def split_heads(pair):
    low = lax.broadcasted_iota(jnp.int32, pair.shape, 1) < HD
    zero = jnp.zeros_like(pair)
    return jnp.concatenate([jnp.where(low, pair, zero), jnp.where(low, zero, pair)], axis=0)


def join_heads(stacked):
    rows = stacked.shape[0] // 2
    low = lax.broadcasted_iota(jnp.int32, (rows, 2 * HD), 1) < HD
    return jnp.where(low, stacked[:rows], stacked[rows:])


def soft_rows(scores, allowed):
    scores = jnp.where(allowed, scores * HD ** (-0.5), masked_score)
    top = jnp.max(scores, axis=-1, keepdims=True)
    p = jnp.exp(scores - top)
    return p / jnp.sum(p, axis=-1, keepdims=True)


def self_mask(lens):
    shape = (2 * SUF, SUF)
    query = lax.broadcasted_iota(jnp.int32, shape, 0) % SUF
    key = lax.broadcasted_iota(jnp.int32, shape, 1)
    return (key <= query) & (key < lens[0:1, 0:SUF])


def cross_mask(lens):
    key = lax.broadcasted_iota(jnp.int32, (2 * SUF, MEMLEN), 1)
    seen = jnp.concatenate([lens[0:1]] * (MEMLEN // 128), axis=1)
    return key < PATCH + seen


PAIRS = H // 2


def attend(mask_of, lens, q_ref, k_ref, v_ref, o_ref, p_ref, key_rows):
    def body(ex, _):
        allowed = mask_of(lens[ex])
        rows = pl.ds(pl.multiple_of(ex * SUF, SUF), SUF)
        keys = pl.ds(pl.multiple_of(ex * key_rows, key_rows), key_rows)
        for pair in range(PAIRS):
            lanes = pl.ds(pair * 2 * HD, 2 * HD)
            p = soft_rows(dot_nt(split_heads(q_ref[rows, lanes]), k_ref[keys, lanes]), allowed)
            p_ref[ex * PAIRS + pair] = p
            o_ref[rows, lanes] = join_heads(dot_nn(p.astype(BF), v_ref[keys, lanes])).astype(BF)
        return 0

    lax.fori_loop(0, EX_DEV, body, 0)


def attend_back(q_ref, k_ref, v_ref, p_ref, do_ref, dq_ref, dk_ref, dv_ref, key_rows):
    scale = HD ** (-0.5)

    def body(ex, _):
        rows = pl.ds(pl.multiple_of(ex * SUF, SUF), SUF)
        keys = pl.ds(pl.multiple_of(ex * key_rows, key_rows), key_rows)
        for pair in range(PAIRS):
            lanes = pl.ds(pair * 2 * HD, 2 * HD)
            p = p_ref[ex * PAIRS + pair]
            d_out = split_heads(do_ref[rows, lanes])
            dv_ref[keys, lanes] = dot_tn(p.astype(BF), d_out).astype(BF)
            dp = dot_nt(d_out, v_ref[keys, lanes])
            ds = (p * (dp - jnp.sum(p * dp, axis=-1, keepdims=True))).astype(BF)
            dq_ref[rows, lanes] = (join_heads(dot_nn(ds, k_ref[keys, lanes])) * scale).astype(BF)
            dk_ref[keys, lanes] = (
                dot_tn(ds, split_heads(q_ref[rows, lanes])) * scale
            ).astype(BF)
        return 0

    lax.fori_loop(0, EX_DEV, body, 0)


def gelu_parts(u):
    rate = (2.0 / jnp.pi) ** 0.5
    square = u * u
    t = jnp.tanh(rate * (u + 0.044715 * u * square))
    half = 0.5 * (1.0 + t)
    slope = half + 0.5 * u * (1.0 - t * t) * (rate * (1.0 + 3 * 0.044715 * square))
    return u * half, slope


def layer_kernel(
    x_ref, cot_ref, vec_ref, slen_ref, plen_ref, self_h, cross_h, up_h, dn_h, mem_h,
    out_ref, sg_ref, vecg_ref, qkv_g, wo_g, cq_g, ckv_g, co_g, up_g, dn_g, mem_g,
    sw, cw, uw, dw, mem, ring, dmem, a1, q1, k1, v1, o1, a2, q2, o2, a3, k2, v2,
    db, dq, dk1, dv1, dk2, dv2, e3, z_ref, slope, unit1, unit2, unit3, h1, h2, dh, ps, pc,
    loads, stores, mem_sem,
):
    sources = (
        [(self_h.at[i], sw.at[i]) for i in range(4)]
        + [(mem_h, mem)]
        + [(cross_h.at[i], cw.at[i]) for i in range(4)]
        + [(up_h.at[pl.ds(0, uw.shape[1]), j], uw.at[j]) for j in range(4)]
        + [(dn_h.at[4 + j], dw.at[j]) for j in range(4)]
    )
    fetched = []
    for i, (src, dst) in enumerate(sources):
        fetched.append(pltpu.make_async_copy(src, dst, loads.at[i]))
        fetched[-1].start()
    self_ok, mem_ok, cross_ok = fetched[0:4], fetched[4], fetched[5:9]
    up_ok, dn_ok = fetched[9:13], fetched[13:17]

    depth = ring.shape[0]
    pending = []

    def give(value, dst):
        slot = len(pending) % depth
        if len(pending) >= depth:
            pending[-depth].wait()
        ring[slot] = value.astype(BF)
        pending.append(pltpu.make_async_copy(ring.at[slot], dst, stores.at[slot]))
        pending[-1].start()

    vecg_ref[8:16] = jnp.zeros((8, D), F32)

    def row(i):
        return vec_ref[i : i + 1, :]

    g1, b1, g2, b2, g3, b3, bdn = [row(i) for i in range(7)]

    x = x_ref[...].astype(F32)
    unit, r1 = norm_parts(x)
    unit1[...] = unit
    a1[...] = (unit * g1 + b1).astype(BF)
    for i, ref in enumerate((q1, k1, v1)):
        self_ok[i].wait()
        ref[...] = dot_nn(a1[...], sw[i]).astype(BF)
    attend(self_mask, slen_ref, q1, k1, v1, o1, ps, SUF)
    self_ok[3].wait()
    h1[...] = x_ref[...].astype(F32) + dot_nn(o1[...], sw[3])

    unit, r2 = norm_parts(h1[...])
    unit2[...] = unit
    a2[...] = (unit * g2 + b2).astype(BF)
    cross_ok[0].wait()
    q2[...] = dot_nn(a2[...], cw[0]).astype(BF)
    mem_ok.wait()
    for i, ref in ((1, k2), (2, v2)):
        cross_ok[i].wait()
        ref[...] = dot_nn(mem[...], cw[i]).astype(BF)
    attend(cross_mask, plen_ref, q2, k2, v2, o2, pc, MEMLEN)
    cross_ok[3].wait()
    h2[...] = h1[...] + dot_nn(o2[...], cw[3])

    unit, r3 = norm_parts(h2[...])
    unit3[...] = unit
    a3[...] = (unit * g3 + b3).astype(BF)
    out_ref[...] = h2[...] + bdn
    ones = lax.broadcasted_iota(jnp.int32, (SUF, D), 0)
    for ex in range(EX_DEV):
        rows = pl.ds(ex * SUF, SUF)
        length = jnp.concatenate([slen_ref[ex, 0:1]] * (D // 128), axis=1)
        seed = cot_ref[rows].astype(F32) * (ones < length).astype(F32)
        dh[rows] = seed
        e3[rows] = seed.astype(BF)
    vecg_ref[6:7] = column_sum(e3[...].astype(F32))
    width = uw.shape[1] * uw.shape[2]
    for j in range(4):
        up_ok[j].wait()
        dn_ok[j].wait()
        u = dot_nn(a3[...], uw[j].reshape(width, D)) + row(7 + j)
        act, bend = gelu_parts(u)
        z_ref[...] = act.astype(BF)
        slope[...] = bend
        out_ref[...] += dot_nn(z_ref[...], dw[j])
        give(dot_tn(z_ref[...], e3[...]), dn_g.at[j])
        db[...] = (dot_nt(e3[...], dw[j]) * slope[...]).astype(BF)
        vecg_ref[7 + j : 8 + j] = column_sum(db[...].astype(F32))
        give(dot_tn(a3[...], db[...]), up_g.at[j])
        part = dot_nt(db[...], uw[j].reshape(width, D))
        if j == 0:
            h2[...] = part
        else:
            h2[...] += part

    grad = h2[...]
    vecg_ref[4:5] = column_sum(grad * unit3[...])
    vecg_ref[5:6] = column_sum(grad)
    dh[...] += norm_back(unit3[...], r3, g3, grad)
    db[...] = dh[...].astype(BF)
    give(dot_tn(o2[...], db[...]), co_g)
    e3[...] = dot_nt(db[...], cw[3]).astype(BF)
    attend_back(q2, k2, v2, pc, e3, dq, dk2, dv2, MEMLEN)
    give(dot_tn(a2[...], dq[...]), cq_g)
    give(dot_tn(mem[...], dk2[...]), ckv_g.at[0])
    give(dot_tn(mem[...], dv2[...]), ckv_g.at[1])
    outs = []
    for ex in range(EX_DEV):
        keys = pl.ds(ex * MEMLEN, MEMLEN)
        dmem[ex] = (dot_nt(dk2[keys], cw[1]) + dot_nt(dv2[keys], cw[2])).astype(BF)
        outs.append(pltpu.make_async_copy(dmem.at[ex], mem_g.at[ex], mem_sem.at[ex]))
        outs[-1].start()
    grad = dot_nt(dq[...], cw[0])
    vecg_ref[2:3] = column_sum(grad * unit2[...])
    vecg_ref[3:4] = column_sum(grad)
    dh[...] += norm_back(unit2[...], r2, g2, grad)
    db[...] = dh[...].astype(BF)
    give(dot_tn(o1[...], db[...]), wo_g)
    e3[...] = dot_nt(db[...], sw[3]).astype(BF)
    attend_back(q1, k1, v1, ps, e3, dq, dk1, dv1, SUF)
    for i, ref in enumerate((dq, dk1, dv1)):
        give(dot_tn(a1[...], ref[...]), qkv_g.at[i])
    grad = dot_nt(dq[...], sw[0]) + dot_nt(dk1[...], sw[1]) + dot_nt(dv1[...], sw[2])
    vecg_ref[0:1] = column_sum(grad * unit1[...])
    vecg_ref[1:2] = column_sum(grad)
    sg_ref[...] = dh[...] + norm_back(unit1[...], r1, g1, grad)
    for one in outs + pending[-depth:]:
        one.wait()


def layer_all(x, cot, vec, slen, plen, self_mats, cross_mats, up_view, dn_view, mem_rows):
    anywhere = pl.BlockSpec(memory_space=pl.ANY)
    vmem = pl.BlockSpec(memory_space=pltpu.VMEM)
    rows, mem_count = x.shape[0], mem_rows.shape[0]
    mats = lambda n: pltpu.VMEM((n, D, D), BF)
    low = pltpu.VMEM((rows, D), BF)
    wide = pltpu.VMEM((rows, D), F32)
    mem_low = pltpu.VMEM((mem_count, D), BF)
    shape = lambda *dims, dtype=BF: jax.ShapeDtypeStruct(dims, dtype)
    half = up_view.shape[0] // 2
    return pl.pallas_call(
        layer_kernel,
        out_shape=[
            shape(rows, D, dtype=F32),
            shape(rows, D, dtype=F32),
            shape(16, D, dtype=F32),
            shape(3, D, D),
            shape(D, D),
            shape(D, D),
            shape(2, D, D),
            shape(D, D),
            shape(4, D, D),
            shape(4, D, D),
            shape(EX_DEV, MEMLEN, D),
        ],
        in_specs=[vmem] * 5 + [anywhere] * 5,
        out_specs=[vmem] * 3 + [anywhere] * 8,
        scratch_shapes=[
            mats(4), mats(4), pltpu.VMEM((4, half) + up_view.shape[2:], BF), mats(4),
            mem_low, mats(4), pltpu.VMEM((EX_DEV, MEMLEN, D), BF),
            low, low, low, low, low, low, low, low, low, mem_low, mem_low,
            low, low, low, low, mem_low, mem_low, low, low,
            wide, wide, wide, wide, wide, wide, wide,
            pltpu.VMEM((EX_DEV * PAIRS, 2 * SUF, SUF), F32),
            pltpu.VMEM((EX_DEV * PAIRS, 2 * SUF, MEMLEN), F32),
            pltpu.SemaphoreType.DMA((17,)),
            pltpu.SemaphoreType.DMA((4,)),
            pltpu.SemaphoreType.DMA((EX_DEV,)),
        ],
        compiler_params=pltpu.CompilerParams(vmem_limit_bytes=60 << 20),
        name="layer_all",
    )(x, cot, vec, slen, plen, self_mats, cross_mats, up_view, dn_view, mem_rows)


def fast_shards(
    suffix,
    memory,
    prefix_lengths,
    suffix_lengths,
    cotangent,
    self_weights,
    self_moment,
    self_second,
    cross_weights,
    cross_moment,
    cross_second,
    feed_weights,
    feed_moment,
    feed_second,
    vectors,
    vector_moment,
    vector_second,
):
    row_count = EX_DEV * SUF
    ndp, nfs = lax.axis_size("dp"), lax.axis_size("fsdp")
    owners = ndp * nfs
    attn_shard, feed_shard = self_weights.shape[0], feed_weights.shape[0]
    rows_a, rows_f = attn_shard // D, feed_shard // (4 * D)
    flat = lambda *group: [a.reshape(-1, 128) for a in group]
    weights = flat(self_weights, cross_weights, feed_weights, vectors)
    moments = flat(self_moment, cross_moment, feed_moment, vector_moment)
    seconds = flat(self_second, cross_second, feed_second, vector_second)
    self_full, cross_full, feed_full, own_memory = gather_all(
        *weights[:3], memory[0], rows_a, rows_f, ndp
    )
    lens = lambda a: jnp.broadcast_to(a[0][:, None, None], (EX_DEV, 8, 128))
    (
        layer_output, suffix_gradient, vector_partial,
        qkv_g, wo_g, cq_g, ckv_g, co_g, up_g, dn_g, mem_g,
    ) = layer_all(
        suffix.reshape(row_count, D),
        cotangent.reshape(row_count, D),
        vectors.reshape(-1, D),
        lens(suffix_lengths),
        lens(prefix_lengths),
        self_full.reshape(4, D, D),
        cross_full.reshape(4, D, D),
        feed_full.reshape(owners, 4, rows_f, D),
        feed_full.reshape(8, D, D),
        own_memory.reshape(EX_DEV * MEMLEN, D),
    )
    split = (2, 2, 2)
    *totals, memory_back, vec_sum, squared, norms = scatter_all(
        (
            qkv_g.reshape((3,) + split + (rows_a, D)),
            wo_g.reshape(split + (rows_a, D)),
            cq_g.reshape(split + (rows_a, D)),
            ckv_g.reshape((2,) + split + (rows_a, D)),
            co_g.reshape(split + (rows_a, D)),
            up_g.reshape((4, 2) + split + (rows_f, D)),
            dn_g.reshape((2,) + split + (4, rows_f, D)),
        ),
        mem_g.reshape(EX_DEV, ndp, MEMLEN // ndp, D),
        vector_partial,
        weights[:3] + moments[:3] + seconds[:3],
        rows_f,
        ndp,
        nfs,
    )
    *new, tensor_norms, global_norm = update_all(
        totals, weights, moments, seconds, vec_sum, squared, norms
    )
    return (
        layer_output.reshape(1, EX_DEV, SUF, D),
        suffix_gradient.reshape(1, EX_DEV, SUF, D),
        memory_back.astype(F32)[None],
        *[a.reshape(-1) for a in new],
        tensor_norms,
        global_norm.reshape(()),
    )


def pick(mesh):
    if mesh.shape["dp"] == 8 and mesh.shape["fsdp"] == 4:
        return fast_shards
    return shards


def solution(mesh):
    return jax.shard_map(
        pick(mesh),
        mesh=mesh,
        in_specs=(
            P("fsdp", "dp", None, None),
            P("fsdp", None, "dp", None),
            P("fsdp", "dp"),
            P("fsdp", "dp"),
            P("fsdp", "dp", None, None),
            P(("dp", "fsdp")),
            P(("dp", "fsdp")),
            P(("dp", "fsdp")),
            P(("dp", "fsdp")),
            P(("dp", "fsdp")),
            P(("dp", "fsdp")),
            P(("dp", "fsdp")),
            P(("dp", "fsdp")),
            P(("dp", "fsdp")),
            P(),
            P(),
            P(),
        ),
        out_specs=(
            P("fsdp", "dp", None, None),
            P("fsdp", "dp", None, None),
            P("fsdp", None, "dp", None),
            P(("dp", "fsdp")),
            P(("dp", "fsdp")),
            P(("dp", "fsdp")),
            P(("dp", "fsdp")),
            P(("dp", "fsdp")),
            P(("dp", "fsdp")),
            P(("dp", "fsdp")),
            P(("dp", "fsdp")),
            P(("dp", "fsdp")),
            P(("dp", "fsdp")),
            P(("dp", "fsdp")),
            P(("dp", "fsdp")),
            P(),
            P(),
            P(),
            P(),
            P(),
            P(),
        ),
        check_vma=False,
    )
```

```python
import jax
import jax.numpy as jnp
from jax import lax
from jax.experimental import pallas as pl
from jax.experimental.pallas import tpu as pltpu
from jax.sharding import PartitionSpec as P

D = 768
H = 12
HD = 64
FF = 3072
PATCH = 196
SUF = 64
EX_DEV = 4
MEMLEN = 256


beta_one = 0.5
beta_two = 0.55
step_count = 5
learn_rate = 0.5
decay_weight = 0.01
adam_eps = 1e-06
norm_eps = 1e-06
trust_eps = 1e-06
masked_score = -1e30


def layer_norm(values, norm_gain, norm_shift):
    centred = values - jnp.mean(values, axis=-1, keepdims=True)
    spread = jnp.mean(centred * centred, axis=-1, keepdims=True)
    return centred * lax.rsqrt(spread + norm_eps) * norm_gain + norm_shift


def gelu_tanh(values):
    return jax.nn.gelu(values, approximate=True)


def attend_forward(query_heads, key_heads, value_heads, allowed):
    score_scale = HD ** (-0.5)
    scores = (
        jnp.einsum("bqhe,bkhe->bhqk", query_heads, key_heads, preferred_element_type=jnp.float32)
        * score_scale
    )
    scores = jnp.where(allowed, scores, masked_score)
    attention = jax.nn.softmax(scores, axis=-1)
    totals = jax.nn.logsumexp(scores, axis=-1)
    mixed_rows = jnp.einsum(
        "bhqk,bkhe->bqhe",
        attention.astype(jnp.bfloat16),
        value_heads,
        preferred_element_type=jnp.float32,
    )
    return (mixed_rows, totals)


def attend_backward(query_heads, key_heads, value_heads, allowed, totals, mixed_grad):
    score_scale = HD ** (-0.5)
    scores = (
        jnp.einsum("bqhe,bkhe->bhqk", query_heads, key_heads, preferred_element_type=jnp.float32)
        * score_scale
    )
    scores = jnp.where(allowed, scores, masked_score)
    attention = jnp.exp(scores - totals[..., None])
    value_grad = jnp.einsum(
        "bhqk,bqhe->bkhe",
        attention.astype(jnp.bfloat16),
        mixed_grad,
        preferred_element_type=jnp.float32,
    )
    attention_grad = jnp.einsum(
        "bqhe,bkhe->bhqk", mixed_grad, value_heads, preferred_element_type=jnp.float32
    )
    score_grad = attention * (
        attention_grad - jnp.sum(attention * attention_grad, axis=-1, keepdims=True)
    )
    score_low = score_grad.astype(jnp.bfloat16)
    query_grad = (
        jnp.einsum("bhqk,bkhe->bqhe", score_low, key_heads, preferred_element_type=jnp.float32)
        * score_scale
    )
    key_grad = (
        jnp.einsum("bhqk,bqhe->bkhe", score_low, query_heads, preferred_element_type=jnp.float32)
        * score_scale
    )
    return (query_grad, key_grad, value_grad)


def lamb_step(weight, gradient, moment, second, clip_factor):
    clipped = clip_factor * gradient
    moment_new = beta_one * moment + (1.0 - beta_one) * clipped
    second_new = beta_two * second + (1.0 - beta_two) * clipped * clipped
    ratio = (
        moment_new
        / (1.0 - beta_one**step_count)
        / (jnp.sqrt(second_new / (1.0 - beta_two**step_count)) + adam_eps)
        + decay_weight * weight
    )
    return (moment_new, second_new, ratio)


def segment_sums(values, offset, segment_size, tensor_count):
    labels = (offset + jnp.arange(values.shape[0], dtype=jnp.int32)) // segment_size
    matches = labels[:, None] == jnp.arange(tensor_count, dtype=jnp.int32)[None, :]
    return jnp.sum(jnp.where(matches, values[:, None], 0.0), axis=0)


def segment_spread(factors, offset, length_here, segment_size):
    labels = (offset + jnp.arange(length_here, dtype=jnp.int32)) // segment_size
    matches = labels[:, None] == jnp.arange(factors.shape[0], dtype=jnp.int32)[None, :]
    return jnp.sum(jnp.where(matches, factors[None, :], 0.0), axis=1)


def shards(
    suffix,
    memory,
    prefix_lengths,
    suffix_lengths,
    cotangent,
    self_weights,
    self_moment,
    self_second,
    cross_weights,
    cross_moment,
    cross_second,
    feed_weights,
    feed_moment,
    feed_second,
    vectors,
    vector_moment,
    vector_second,
):
    row_count = EX_DEV * SUF
    attn_shard = self_weights.shape[0]
    feed_shard = feed_weights.shape[0]
    self_full, cross_full, feed_full = (
        lax.all_gather(self_weights.astype(jnp.bfloat16), ("dp", "fsdp"), axis=0, tiled=True),
        lax.all_gather(cross_weights.astype(jnp.bfloat16), ("dp", "fsdp"), axis=0, tiled=True),
        lax.all_gather(feed_weights.astype(jnp.bfloat16), ("dp", "fsdp"), axis=0, tiled=True),
    )
    self_mats = self_full.reshape(4, D, D)
    cross_mats = cross_full.reshape(4, D, D)
    up_mat = feed_full[: D * FF].reshape(D, FF)
    down_mat = feed_full[D * FF :].reshape(FF, D)
    vector_parts = [vectors[segment * D : (segment + 1) * D] for segment in range(7)]
    bias_up = vectors[7 * D :]
    own_memory = lax.all_to_all(memory, "dp", split_axis=1, concat_axis=2, tiled=True)
    memory_rows = own_memory.reshape(EX_DEV * MEMLEN, D)
    suffix_len = suffix_lengths[0]
    prefix_len = prefix_lengths[0]
    positions = jnp.arange(SUF, dtype=jnp.int32)
    causal = positions[:, None] >= positions[None, :]
    self_allowed = (
        causal[None, None, :, :] & (positions[None, :] < suffix_len[:, None])[:, None, None, :]
    )
    memory_pos = jnp.arange(MEMLEN, dtype=jnp.int32)
    cross_allowed = (memory_pos[None, :] < (PATCH + prefix_len)[:, None])[:, None, None, :]
    inputs = suffix.reshape(row_count, D).astype(jnp.float32)
    normed_one = layer_norm(inputs, vector_parts[0], vector_parts[1]).astype(jnp.bfloat16)
    self_qkv = jnp.einsum(
        "rd,jde->jre", normed_one, self_mats[0:3], preferred_element_type=jnp.float32
    ).astype(jnp.bfloat16)
    self_heads = self_qkv.reshape(3, EX_DEV, SUF, H, HD)
    mixed_one, totals_one = attend_forward(
        self_heads[0], self_heads[1], self_heads[2], self_allowed
    )
    mixed_one = mixed_one.reshape(row_count, D).astype(jnp.bfloat16)
    hidden_one = inputs + jnp.dot(mixed_one, self_mats[3], preferred_element_type=jnp.float32)
    normed_two = layer_norm(hidden_one, vector_parts[2], vector_parts[3]).astype(jnp.bfloat16)
    cross_query = jnp.dot(normed_two, cross_mats[0], preferred_element_type=jnp.float32).astype(
        jnp.bfloat16
    )
    cross_kv = jnp.einsum(
        "rd,jde->jre", memory_rows, cross_mats[1:3], preferred_element_type=jnp.float32
    ).astype(jnp.bfloat16)
    query_heads = cross_query.reshape(EX_DEV, SUF, H, HD)
    kv_heads = cross_kv.reshape(2, EX_DEV, MEMLEN, H, HD)
    mixed_two, totals_two = attend_forward(query_heads, kv_heads[0], kv_heads[1], cross_allowed)
    mixed_two = mixed_two.reshape(row_count, D).astype(jnp.bfloat16)
    hidden_two = hidden_one + jnp.dot(mixed_two, cross_mats[3], preferred_element_type=jnp.float32)
    normed_three = layer_norm(hidden_two, vector_parts[4], vector_parts[5]).astype(jnp.bfloat16)
    pre_act = jnp.dot(normed_three, up_mat, preferred_element_type=jnp.float32) + bias_up
    activated = gelu_tanh(pre_act).astype(jnp.bfloat16)
    layer_output = hidden_two + (
        jnp.dot(activated, down_mat, preferred_element_type=jnp.float32) + vector_parts[6]
    )
    valid_rows = (positions[None, :] < suffix_len[:, None]).astype(jnp.float32)
    seed_rows = (
        cotangent.reshape(EX_DEV, SUF, D).astype(jnp.float32) * valid_rows[:, :, None]
    ).reshape(row_count, D)
    seed_low = seed_rows.astype(jnp.bfloat16)
    bias_down_grad = jnp.sum(seed_low.astype(jnp.float32), axis=0)
    down_grad = jnp.einsum("rf,rd->fd", activated, seed_low, preferred_element_type=jnp.float32)
    activated_grad = jnp.einsum("rd,fd->rf", seed_low, down_mat, preferred_element_type=jnp.float32)
    _, gelu_back = jax.vjp(gelu_tanh, pre_act)
    pre_grad = gelu_back(activated_grad)[0].astype(jnp.bfloat16)
    bias_up_grad = jnp.sum(pre_grad.astype(jnp.float32), axis=0)
    up_grad = jnp.einsum("rd,rf->df", normed_three, pre_grad, preferred_element_type=jnp.float32)
    normed_three_grad = jnp.einsum(
        "rf,df->rd", pre_grad, up_mat, preferred_element_type=jnp.float32
    )
    _, norm_three_back = jax.vjp(layer_norm, hidden_two, vector_parts[4], vector_parts[5])
    through_three, gain_three_grad, shift_three_grad = norm_three_back(normed_three_grad)
    hidden_two_grad = seed_rows + through_three
    feed_flat = jnp.concatenate([up_grad.reshape(-1), down_grad.reshape(-1)])
    branch_two = hidden_two_grad.astype(jnp.bfloat16)
    cross_out_grad = jnp.einsum(
        "rd,re->de", mixed_two, branch_two, preferred_element_type=jnp.float32
    )
    mixed_two_grad = jnp.einsum(
        "re,de->rd", branch_two, cross_mats[3], preferred_element_type=jnp.float32
    ).astype(jnp.bfloat16)
    query_two_grad, key_two_grad, value_two_grad = attend_backward(
        query_heads,
        kv_heads[0],
        kv_heads[1],
        cross_allowed,
        totals_two,
        mixed_two_grad.reshape(EX_DEV, SUF, H, HD),
    )
    cross_query_grad = query_two_grad.reshape(row_count, D).astype(jnp.bfloat16)
    cross_kv_grad = (
        jnp.stack([key_two_grad, value_two_grad])
        .reshape(2, EX_DEV * MEMLEN, D)
        .astype(jnp.bfloat16)
    )
    query_weight_grad = jnp.einsum(
        "rd,re->de", normed_two, cross_query_grad, preferred_element_type=jnp.float32
    )
    kv_weight_grad = jnp.einsum(
        "rd,jre->jde", memory_rows, cross_kv_grad, preferred_element_type=jnp.float32
    )
    normed_two_grad = jnp.einsum(
        "re,de->rd", cross_query_grad, cross_mats[0], preferred_element_type=jnp.float32
    )
    memory_local_grad = jnp.einsum(
        "jre,jde->rd", cross_kv_grad, cross_mats[1:3], preferred_element_type=jnp.float32
    )
    memory_gradient = lax.all_to_all(
        memory_local_grad.reshape(1, EX_DEV, MEMLEN, D),
        "dp",
        split_axis=2,
        concat_axis=1,
        tiled=True,
    )
    _, norm_two_back = jax.vjp(layer_norm, hidden_one, vector_parts[2], vector_parts[3])
    through_two, gain_two_grad, shift_two_grad = norm_two_back(normed_two_grad)
    hidden_one_grad = hidden_two_grad + through_two
    cross_flat = jnp.concatenate(
        [query_weight_grad[None], kv_weight_grad, cross_out_grad[None]], axis=0
    ).reshape(-1)
    branch_one = hidden_one_grad.astype(jnp.bfloat16)
    self_out_grad = jnp.einsum(
        "rd,re->de", mixed_one, branch_one, preferred_element_type=jnp.float32
    )
    mixed_one_grad = jnp.einsum(
        "re,de->rd", branch_one, self_mats[3], preferred_element_type=jnp.float32
    ).astype(jnp.bfloat16)
    query_one_grad, key_one_grad, value_one_grad = attend_backward(
        self_heads[0],
        self_heads[1],
        self_heads[2],
        self_allowed,
        totals_one,
        mixed_one_grad.reshape(EX_DEV, SUF, H, HD),
    )
    self_qkv_grad = (
        jnp.stack([query_one_grad, key_one_grad, value_one_grad])
        .reshape(3, row_count, D)
        .astype(jnp.bfloat16)
    )
    qkv_weight_grad = jnp.einsum(
        "rd,jre->jde", normed_one, self_qkv_grad, preferred_element_type=jnp.float32
    )
    normed_one_grad = jnp.einsum(
        "jre,jde->rd", self_qkv_grad, self_mats[0:3], preferred_element_type=jnp.float32
    )
    _, norm_one_back = jax.vjp(layer_norm, inputs, vector_parts[0], vector_parts[1])
    through_one, gain_one_grad, shift_one_grad = norm_one_back(normed_one_grad)
    suffix_gradient = (hidden_one_grad + through_one).reshape(1, EX_DEV, SUF, D)
    self_flat = jnp.concatenate([qkv_weight_grad, self_out_grad[None]], axis=0).reshape(-1)
    owners = lax.axis_size(("dp", "fsdp"))
    joined = jnp.concatenate(
        [
            self_flat.reshape(owners, attn_shard),
            cross_flat.reshape(owners, attn_shard),
            feed_flat.reshape(owners, feed_shard),
        ],
        axis=1,
    ).reshape(-1)
    owned = lax.psum_scatter(joined, ("dp", "fsdp"), scatter_dimension=0, tiled=True)
    self_total = owned[:attn_shard]
    cross_total = owned[attn_shard : 2 * attn_shard]
    feed_total = owned[2 * attn_shard :]
    vector_partial = jnp.concatenate(
        [
            gain_one_grad,
            shift_one_grad,
            gain_two_grad,
            shift_two_grad,
            gain_three_grad,
            shift_three_grad,
            bias_down_grad,
            bias_up_grad,
        ]
    )
    shard_index = lax.axis_index(("dp", "fsdp"))
    attn_offset = shard_index * attn_shard
    feed_offset = shard_index * feed_shard
    grad_squares = jnp.concatenate(
        [
            segment_sums(self_total * self_total, attn_offset, D * D, 4),
            segment_sums(cross_total * cross_total, attn_offset, D * D, 4),
            segment_sums(feed_total * feed_total, feed_offset, D * FF, 2),
        ]
    )
    weight_squares = jnp.concatenate(
        [
            segment_sums(self_weights * self_weights, attn_offset, D * D, 4),
            segment_sums(cross_weights * cross_weights, attn_offset, D * D, 4),
            segment_sums(feed_weights * feed_weights, feed_offset, D * FF, 2),
        ]
    )
    vector_total, grad_summed, weight_summed = lax.psum(
        (vector_partial, grad_squares, weight_squares), ("dp", "fsdp")
    )
    squared_total = jnp.sum(grad_summed) + jnp.sum(vector_total * vector_total)
    global_norm = jnp.sqrt(squared_total)
    clip_factor = jnp.minimum(1.0, 1.0 / global_norm)
    self_momentum, self_variance, self_ratio = lamb_step(
        self_weights, self_total, self_moment, self_second, clip_factor
    )
    cross_momentum, cross_variance, cross_ratio = lamb_step(
        cross_weights, cross_total, cross_moment, cross_second, clip_factor
    )
    feed_momentum, feed_variance, feed_ratio = lamb_step(
        feed_weights, feed_total, feed_moment, feed_second, clip_factor
    )
    ratio_squares = jnp.concatenate(
        [
            segment_sums(self_ratio * self_ratio, attn_offset, D * D, 4),
            segment_sums(cross_ratio * cross_ratio, attn_offset, D * D, 4),
            segment_sums(feed_ratio * feed_ratio, feed_offset, D * FF, 2),
        ]
    )
    update_summed = lax.psum(ratio_squares, ("dp", "fsdp"))
    weight_norms = jnp.sqrt(weight_summed)
    ratio_norms = jnp.sqrt(update_summed)
    trust_ratio = weight_norms / (ratio_norms + trust_eps)
    self_master = (
        self_weights
        - learn_rate * segment_spread(trust_ratio[0:4], attn_offset, attn_shard, D * D) * self_ratio
    )
    cross_master = (
        cross_weights
        - learn_rate
        * segment_spread(trust_ratio[4:8], attn_offset, attn_shard, D * D)
        * cross_ratio
    )
    feed_master = (
        feed_weights
        - learn_rate
        * segment_spread(trust_ratio[8:10], feed_offset, feed_shard, D * FF)
        * feed_ratio
    )
    vector_momentum, vector_variance, vector_ratio = lamb_step(
        vectors, vector_total, vector_moment, vector_second, clip_factor
    )
    edges = [0, D, 2 * D, 3 * D, 4 * D, 5 * D, 6 * D, 7 * D, 7 * D + FF]
    vector_wn = []
    vector_rn = []
    new_pieces = []
    for segment in range(8):
        weight_part = vectors[edges[segment] : edges[segment + 1]]
        ratio_part = vector_ratio[edges[segment] : edges[segment + 1]]
        weight_norm = jnp.sqrt(jnp.sum(weight_part * weight_part))
        ratio_norm = jnp.sqrt(jnp.sum(ratio_part * ratio_part))
        piece_trust = weight_norm / (ratio_norm + trust_eps)
        vector_wn.append(weight_norm)
        vector_rn.append(ratio_norm)
        new_pieces.append(weight_part - learn_rate * piece_trust * ratio_part)
    vector_master = jnp.concatenate(new_pieces)
    tensor_norms = jnp.stack(
        [
            jnp.concatenate([weight_norms, jnp.stack(vector_wn)]),
            jnp.concatenate([ratio_norms, jnp.stack(vector_rn)]),
        ]
    )
    return (
        layer_output.reshape(1, EX_DEV, SUF, D),
        suffix_gradient,
        memory_gradient,
        self_total,
        self_momentum,
        self_variance,
        self_master,
        cross_total,
        cross_momentum,
        cross_variance,
        cross_master,
        feed_total,
        feed_momentum,
        feed_variance,
        feed_master,
        vector_total,
        vector_momentum,
        vector_variance,
        vector_master,
        tensor_norms,
        global_norm,
    )


BF = jnp.bfloat16
F32 = jnp.float32
MESH = pl.DeviceIdType.MESH
NZ = 4
AHEAD = 6
MEM_AT = 3


def place():
    dp, fs = lax.axis_index("dp"), lax.axis_index("fsdp")
    return dp, fs, dp // 2, dp % 2, fs // 2, fs % 2


def peer_id(z, y, x, c):
    return (z * 2 + y, x * 2 + c)


def greet(ids):
    bar = pltpu.get_barrier_semaphore()
    for where in ids:
        pl.semaphore_signal(bar, inc=1, device_id=where, device_id_type=MESH)
    pl.semaphore_wait(bar, len(ids))


class Copies:
    def __init__(self, send, recv, local):
        self.send, self.recv, self.local = send, recv, local
        self.remotes, self.locals = 0, 0
        self.open = []

    def remote(self, src, dst, where):
        i = self.remotes
        self.remotes += 1
        cp = pltpu.make_async_remote_copy(
            src_ref=src,
            dst_ref=dst,
            send_sem=self.send.at[i],
            recv_sem=self.recv.at[i],
            device_id=where,
            device_id_type=MESH,
        )
        cp.start()
        self.open.append(cp)
        return cp

    def here(self, src, dst):
        cp = pltpu.make_async_copy(src, dst, self.local.at[self.locals])
        self.locals += 1
        cp.start()
        return cp

    def drain(self):
        for cp in self.open:
            cp.wait_send()


LANES = 128


def rows_of(flat, dst, j, start, stride):
    rows, width = dst.shape[1:]
    for i in range(width // LANES):
        part = flat[pl.ds(start + i, rows, stride=stride), :]
        dst[j, :, i * LANES : (i + 1) * LANES] = part.astype(dst.dtype)


def feed_lines(j, rows, width, up):
    per = width // LANES
    return (j * per, 4 * per) if up else (j * rows * per, per)


def squares(v):
    return jnp.sum((v * v).reshape(v.shape[0] // 8, 8, LANES), axis=0)


def sum_everywhere(cp, mine, slots_a, slots_b, dp, fs):
    nfs, ndp = slots_a.shape[0], slots_b.shape[0]
    slots_a[fs] = mine
    got = [
        cp.remote(slots_a.at[fs], slots_a.at[fs], (dp, (fs + k) % nfs)) for k in range(1, nfs)
    ]
    for one in got:
        one.wait_recv()
    total = slots_a[0]
    for k in range(1, nfs):
        total = total + slots_a[k]
    slots_b[dp] = total
    got = [
        cp.remote(slots_b.at[dp], slots_b.at[dp], ((dp + k) % ndp, fs)) for k in range(1, ndp)
    ]
    for one in got:
        one.wait_recv()
    total = slots_b[0]
    for k in range(1, ndp):
        total = total + slots_b[k]
    return total


def lamb_sums(w, g, m, s, factor):
    ratio = lamb_step(w[...], g[...], m[...], s[...], factor)[2]
    return jnp.sum(ratio * ratio, axis=0, keepdims=True)


def norm_of(sq):
    return jnp.sqrt(jnp.sum(jnp.sum(sq, axis=1, keepdims=True), axis=0, keepdims=True))


def clip_of(sq):
    return jnp.minimum(1.0, 1.0 / norm_of(sq))


def dot_nn(a, b):
    return lax.dot_general(a, b, (((1,), (0,)), ((), ())), preferred_element_type=F32)


def dot_nt(a, b):
    return lax.dot_general(a, b, (((1,), (1,)), ((), ())), preferred_element_type=F32)


def dot_tn(a, b):
    return lax.dot_general(a, b, (((0,), (0,)), ((), ())), preferred_element_type=F32)


def norm_parts(values):
    centred = values - jnp.mean(values, axis=-1, keepdims=True)
    scale = lax.rsqrt(jnp.mean(centred * centred, axis=-1, keepdims=True) + norm_eps)
    return centred * scale, scale


def norm_back(unit, scale, gain, grad):
    e = grad * gain
    return scale * (
        e
        - jnp.mean(e, axis=-1, keepdims=True)
        - unit * jnp.mean(e * unit, axis=-1, keepdims=True)
    )


def column_sum(values):
    return jnp.sum(values, axis=0, keepdims=True)


def split_heads(pair):
    low = lax.broadcasted_iota(jnp.int32, pair.shape, 1) < HD
    zero = jnp.zeros_like(pair)
    return jnp.concatenate([jnp.where(low, pair, zero), jnp.where(low, zero, pair)], axis=0)


def join_heads(stacked):
    rows = stacked.shape[0] // 2
    low = lax.broadcasted_iota(jnp.int32, (rows, 2 * HD), 1) < HD
    return jnp.where(low, stacked[:rows], stacked[rows:])


def soft_rows(scores, allowed):
    scores = jnp.where(allowed, scores * HD ** (-0.5), masked_score)
    top = jnp.max(scores, axis=-1, keepdims=True)
    p = jnp.exp(scores - top)
    return p / jnp.sum(p, axis=-1, keepdims=True)


def self_mask(lens):
    shape = (2 * SUF, SUF)
    query = lax.broadcasted_iota(jnp.int32, shape, 0) % SUF
    key = lax.broadcasted_iota(jnp.int32, shape, 1)
    return (key <= query) & (key < lens[0:1, 0:SUF])


def cross_mask(lens):
    key = lax.broadcasted_iota(jnp.int32, (2 * SUF, MEMLEN), 1)
    seen = jnp.concatenate([lens[0:1]] * (MEMLEN // 128), axis=1)
    return key < PATCH + seen


PAIRS = H // 2


def gelu_parts(u):
    rate = (2.0 / jnp.pi) ** 0.5
    square = u * u
    t = jnp.tanh(rate * (u + 0.044715 * u * square))
    half = 0.5 * (1.0 + t)
    slope = half + 0.5 * u * (1.0 - t * t) * (rate * (1.0 + 3 * 0.044715 * square))
    return u * half, slope


def head_rows(ex, key_rows):
    rows = pl.ds(pl.multiple_of(ex * SUF, SUF), SUF)
    return rows, pl.ds(pl.multiple_of(ex * key_rows, key_rows), key_rows)


def attend(mask_of, lens, q_ref, k_ref, v_ref, o_ref, key_rows):
    def body(ex, _):
        allowed = mask_of(lens[ex])
        rows, keys = head_rows(ex, key_rows)
        for pair in range(PAIRS):
            lanes = pl.ds(pair * 2 * HD, 2 * HD)
            p = soft_rows(dot_nt(split_heads(q_ref[rows, lanes]), k_ref[keys, lanes]), allowed)
            o_ref[rows, lanes] = join_heads(dot_nn(p.astype(BF), v_ref[keys, lanes])).astype(BF)
        return 0

    lax.fori_loop(0, EX_DEV, body, 0)


def attend_back(first, count, mask_of, lens, q_ref, k_ref, v_ref, do_ref, key_rows):
    scale = HD ** (-0.5)

    def body(ex, _):
        allowed = mask_of(lens[ex])
        rows, keys = head_rows(ex, key_rows)
        for pair in range(PAIRS):
            lanes = pl.ds(pair * 2 * HD, 2 * HD)
            q, k, v = split_heads(q_ref[rows, lanes]), k_ref[keys, lanes], v_ref[keys, lanes]
            p = soft_rows(dot_nt(q, k), allowed)
            d_out = split_heads(do_ref[rows, lanes])
            v_ref[keys, lanes] = dot_tn(p.astype(BF), d_out).astype(BF)
            dp = dot_nt(d_out, v)
            ds = (p * (dp - jnp.sum(p * dp, axis=-1, keepdims=True))).astype(BF)
            q_ref[rows, lanes] = (join_heads(dot_nn(ds, k)) * scale).astype(BF)
            k_ref[keys, lanes] = (dot_tn(ds, q) * scale).astype(BF)
        return 0

    lax.fori_loop(first, first + count, body, 0)


def seed_of(cot_ref, lens, ex):
    line = lax.broadcasted_iota(jnp.int32, (SUF, D), 0)
    length = jnp.concatenate([lens[ex, 0:1]] * (D // LANES), axis=1)
    return cot_ref[pl.ds(ex * SUF, SUF)].astype(F32) * (line < length).astype(F32)


class Local:
    def __init__(self, sems):
        self.sems, self.used, self.open = sems, 0, []

    def start(self, src, dst):
        cp = pltpu.make_async_copy(src, dst, self.sems.at[self.used])
        self.used += 1
        cp.start()
        return cp

    def out(self, src, dst):
        self.open.append(self.start(src, dst))

    def drain(self):
        for cp in self.open:
            cp.wait()


def forward_kernel(
    self_w, cross_w, feed_w, mem_in, x_ref, cot_ref, vec_ref, slen_ref, plen_ref,
    attn_h, feed_h, mem_h, q1_h, k1_h, v1_h, o1_h, q2_h, o2_h, a3_h, k2_h, v2_h, z_h, slope_h,
    h1_h, h2_h, dn_g,
    self_in, cross_in, feed_in, self_v, cross_v, feed_v, mem_v, a1, q1, k1, v1, o1, a2, q2, o2, a3,
    e3, k2, v2, z_v, slope_v, h1, h2, ring, send, recv, local,
):
    dp, fs, z, y, x, c = place()
    ex, ndp = mem_v.shape[0], mem_v.shape[1]
    to_y, to_x, to_c = peer_id(z, 1 - y, x, c), peer_id(z, y, 1 - x, c), peer_id(z, y, x, 1 - c)
    per = D // LANES
    cp, loc = Copies(send, recv, None), Local(local)
    rows_of(self_w, self_in, 0, 0, per)
    greet([((dp + k) % ndp, fs) for k in range(1, ndp)] + [to_x, to_c])

    step = feed_in.shape[1]
    cut = step * 2 // 3
    chunks = []
    for src, dst in ((self_in, self_v), (cross_in, cross_v), (feed_in, feed_v)):
        for j in range(src.shape[0]):
            for first in range(0, src.shape[1], step):
                chunks.append(
                    (src, dst, j, pl.ds(first, step), pl.ds(first, cut), pl.ds(first + cut, step - cut))
                )
    zc, s2, s3, s4, mem, own = {}, {}, {}, {}, [], {}

    def send_z(t):
        src, dst, j, rows, r0, r1 = chunks[t]
        own[t] = loc.start(src.at[j, rows], dst.at[z, y, x, c, j, rows])
        for k in range(1, NZ):
            zc[t, k] = cp.remote(
                src.at[j, rows], dst.at[z, y, x, c, j, rows], peer_id((z + k) % NZ, y, x, c)
            )
        send_2(t, 0)

    def send_2(t, k):
        src, dst, j, rows, r0, r1 = chunks[t]
        zz = (z + NZ - k) % NZ
        for part, cut_rows, where in ((0, r0, to_y), (1, r1, to_x)):
            here = src.at[j, cut_rows] if k == 0 else dst.at[zz, y, x, c, j, cut_rows]
            s2[t, k, part] = cp.remote(here, dst.at[zz, y, x, c, j, cut_rows], where)

    def send_3(t):
        src, dst, j, rows, r0, r1 = chunks[t]
        s3[t, 0] = cp.remote(dst.at[:, :, x, c, j, r0], dst.at[:, :, x, c, j, r0], to_x)
        s3[t, 1] = cp.remote(dst.at[:, y, :, c, j, r1], dst.at[:, y, :, c, j, r1], to_y)

    def send_4(t):
        src, dst, j, rows, r0, r1 = chunks[t]
        s4[t] = cp.remote(dst.at[:, :, :, c, j, rows], dst.at[:, :, :, c, j, rows], to_c)

    def send_mem():
        mem.append(loc.start(mem_in.at[pl.ds(ex * dp, ex)], mem_v.at[:, dp]))
        for k in range(1, ndp):
            mem.append(
                cp.remote(
                    mem_in.at[pl.ds(ex * ((dp + k) % ndp), ex)],
                    mem_v.at[:, dp],
                    ((dp + k) % ndp, fs),
                )
            )

    row = lambda i: vec_ref[i : i + 1, :]
    g1, b1, g2, b2, g3, b3 = [row(i) for i in range(6)]
    square = lambda a: a.reshape(D, D)
    self_mat = lambda m: square(self_v[m])
    cross_mat = lambda m: square(cross_v[m])
    mem_rows = lambda: mem_v[...].reshape(ex * MEMLEN, D)

    def begin():
        unit, _ = norm_parts(x_ref[...].astype(F32))
        a1[...] = (unit * g1 + b1).astype(BF)
        for i in range(EX_DEV):
            e3[pl.ds(i * SUF, SUF)] = seed_of(cot_ref, slen_ref, i).astype(BF)

    def self_qkv():
        s4[0].wait_recv()
        s4[1].wait_recv()
        loc.out(self_v.at[:, :, :, :, 0], attn_h.at[pl.ds(0, 4)])
        for i, (ref, dst) in enumerate(((q1, q1_h), (k1, k1_h), (v1, v1_h))):
            ref[...] = dot_nn(a1[...], self_mat(i)).astype(BF)
            loc.out(ref, dst)

    def self_attention():
        attend(self_mask, slen_ref, q1, k1, v1, o1, SUF)
        loc.out(o1, o1_h)
        h1[...] = x_ref[...].astype(F32) + dot_nn(o1[...], self_mat(3))
        loc.out(h1, h1_h)
        unit, _ = norm_parts(h1[...])
        a2[...] = (unit * g2 + b2).astype(BF)

    def cross_query():
        s4[2].wait_recv()
        s4[3].wait_recv()
        loc.out(cross_v.at[:, :, :, :, 0], attn_h.at[pl.ds(4, 4)])
        q2[...] = dot_nn(a2[...], cross_mat(0)).astype(BF)
        loc.out(q2, q2_h)

    def cross_keys():
        mem[0].wait()
        for one in mem[1:]:
            one.wait_recv()
        loc.out(mem_v, mem_h)
        for i, ref, dst in ((1, k2, k2_h), (2, v2, v2_h)):
            ref[...] = dot_nn(mem_rows(), cross_mat(i)).astype(BF)
            loc.out(ref, dst)

    def cross_attention():
        attend(cross_mask, plen_ref, q2, k2, v2, o2, MEMLEN)
        loc.out(o2, o2_h)

    def cross_out():
        h2[...] = h1[...] + dot_nn(o2[...], cross_mat(3))
        loc.out(h2, h2_h)
        unit, _ = norm_parts(h2[...])
        a3[...] = (unit * g3 + b3).astype(BF)
        loc.out(a3, a3_h)

    def feed(j):
        s4[4 + j].wait_recv()
        u = dot_nn(a3[...], square(feed_v[0:2, :, :, :, j])) + row(7 + j)
        act, bend = gelu_parts(u)
        z_v[j] = act.astype(BF)
        slope_v[j] = bend
        loc.out(z_v.at[j], z_h.at[j])
        loc.out(slope_v.at[j], slope_h.at[j])
        ring[j] = dot_tn(z_v[j], e3[...]).astype(BF).reshape(ring.shape[1:])
        loc.out(ring.at[j], dn_g.at[j // 2, j % 2])
        if j == 3:
            loc.out(feed_v, feed_h)

    slots = {
        0: [begin],
        4: [self_qkv],
        5: [self_attention],
        6: [cross_query],
        7: [cross_keys],
        8: [cross_attention],
        9: [cross_out, lambda: feed(0), lambda: feed(1), lambda: feed(2), lambda: feed(3)],
    }
    n = len(chunks)
    send_z(0)
    send_z(1)
    rows_of(cross_w, cross_in, 0, 0, per)
    send_z(2)
    send_z(3)
    for up in (True, False):

        @pl.when(z // 2 == (0 if up else 1))
        def _():
            for j in range(4):
                rows_of(feed_w, feed_in, j, *feed_lines(j, *feed_in.shape[1:], up))

    for t in range(4, min(AHEAD, n)):
        send_z(t)
    for t in range(n + 2):
        if t == MEM_AT:
            send_mem()
        if t < n:
            for k in range(1, NZ):
                zc[t, k].wait_recv()
                send_2(t, k)
            if t + AHEAD < n:
                send_z(t + AHEAD)
        if 1 <= t <= n:
            own[t - 1].wait()
            for k in range(NZ):
                for part in (0, 1):
                    s2[t - 1, k, part].wait_recv()
            send_3(t - 1)
        if t >= 2:
            s3[t - 2, 0].wait_recv()
            s3[t - 2, 1].wait_recv()
            send_4(t - 2)
        for piece in slots.get(t, ()):
            piece()
    loc.drain()
    cp.drain()


def forward_all(weights, mem_in, x, cot, vec, slen, plen, rows_a, rows_f, ndp):
    anywhere = pl.BlockSpec(memory_space=pl.ANY)
    vmem = pl.BlockSpec(memory_space=pltpu.VMEM)
    rows = x.shape[0]
    ex = mem_in.shape[0] // ndp
    count = ex * MEMLEN
    split = (2, 2, 2)
    arrays = {
        "attn": ((8,) + split + (rows_a, D), BF),
        "feed": ((NZ,) + split + (4, rows_f, D), BF),
        "mem": ((ex, ndp) + mem_in.shape[1:], BF),
        "low": ((rows, D), BF),
        "keys": ((count, D), BF),
        "z": ((4, rows, D), BF),
        "slope": ((4, rows, D), F32),
        "wide": ((rows, D), F32),
        "dn": ((2,) + split + (4, rows_f, D), BF),
    }
    kinds = ["attn", "feed", "mem"] + ["low"] * 7 + ["keys"] * 2 + ["z", "slope", "wide", "wide", "dn"]
    low = pltpu.VMEM((rows, D), BF)
    return pl.pallas_call(
        forward_kernel,
        out_shape=[jax.ShapeDtypeStruct(*arrays[k]) for k in kinds],
        in_specs=[vmem] * 3 + [anywhere] + [vmem] * 5,
        out_specs=[anywhere] * len(kinds),
        scratch_shapes=[
            pltpu.VMEM((1, rows_a, D), BF),
            pltpu.VMEM((1, rows_a, D), BF),
            pltpu.VMEM((4, rows_f, D), BF),
            pltpu.VMEM((NZ,) + split + (1, rows_a, D), BF),
            pltpu.VMEM((NZ,) + split + (1, rows_a, D), BF),
            pltpu.VMEM(*arrays["feed"]),
            pltpu.VMEM(*arrays["mem"]),
            *[low] * 10,
            pltpu.VMEM(*arrays["keys"]),
            pltpu.VMEM(*arrays["keys"]),
            pltpu.VMEM(*arrays["z"]),
            pltpu.VMEM(*arrays["slope"]),
            pltpu.VMEM(*arrays["wide"]),
            pltpu.VMEM(*arrays["wide"]),
            pltpu.VMEM((4, 2, 2, 4, rows_f, D), BF),
            pltpu.SemaphoreType.DMA((128,)),
            pltpu.SemaphoreType.DMA((128,)),
            pltpu.SemaphoreType.DMA((48,)),
        ],
        compiler_params=pltpu.CompilerParams(
            collective_id=1, has_side_effects=True, vmem_limit_bytes=60 << 20
        ),
        name="forward_all",
    )(*weights, mem_in, x, cot, vec, slen, plen)


def backward_kernel(
    attn_h, dn_h, up_h, mem_h, q1_h, k1_h, v1_h, o1_h, q2_h, o2_h, a3_h, k2_h, v2_h, z_h, slope_h,
    h1_h, h2_h, dn_g, x_ref, cot_ref, vec_ref, slen_ref, plen_ref,
    ws, wc, wf, ms, mc, mf, ss, sc_, sf,
    out_ref, sg_ref, self_t, cross_t, feed_t, mem_t, vec_t, sq_t, norm_t, attn_g, up_g,
    wr, ur, mem_v, q1, k1, v1, o1, q2, o2, a1, a2, a3, k2, v2, z_v, slope_v, h1, h2, e3, du, db,
    ring_a, ring_u, held, r1, r2a, r2b, r3a, r3b, rz, whole, vecg, v_send, v_recv, v_z,
    qa, qb, na, nb, opt_s, opt_c, opt_f, send, recv, local,
):
    dp, fs, z, y, x, c = place()
    ex_count, ndp = mem_v.shape[0], mem_v.shape[1]
    nfs = qa.shape[0]
    step, width = r1.shape[4], r1.shape[5]
    cut = step * 2 // 3
    head, rest = pl.ds(0, cut), pl.ds(cut, step - cut)
    per = width // LANES
    to_y, to_x, to_c = peer_id(z, 1 - y, x, c), peer_id(z, y, 1 - x, c), peer_id(z, y, x, 1 - c)
    cp, loc = Copies(send, recv, None), Local(local)

    fetch_order = [dn_h.at[4 + j] for j in range(4)] + [
        attn_h.at[m] for m in (7, 5, 6, 4, 3, 0, 1, 2)
    ]
    depth = wr.shape[0]
    fetched, used = [], [0]
    up_got = []

    def fetch():
        if len(fetched) < len(fetch_order):
            i = len(fetched)
            fetched.append(loc.start(fetch_order[i], wr.at[i % depth]))

    def weight():
        i = used[0]
        used[0] += 1
        fetched[i].wait()
        return wr[i % depth]

    def fetch_up():
        i = len(up_got)
        if i < 4:
            up_got.append(loc.start(up_h.at[pl.ds(0, ur.shape[1]), i], ur.at[i % ur.shape[0]]))

    fetch()
    a3_ok = loc.start(a3_h, a3)
    slope_ok = [loc.start(slope_h.at[0], slope_v.at[0])]
    for j in range(1, 4):
        fetch()
        slope_ok.append(loc.start(slope_h.at[j], slope_v.at[j]))
    for _ in range(ur.shape[0]):
        fetch_up()
    z_ok = loc.start(z_h, z_v)
    h2_ok = loc.start(h2_h, h2)
    cross_ok = [
        loc.start(a, b)
        for a, b in ((o2_h, o2), (q2_h, q2), (k2_h, k2), (v2_h, v2), (mem_h, mem_v), (h1_h, h1))
    ]
    self_ok = [loc.start(a, b) for a, b in ((o1_h, o1), (q1_h, q1), (k1_h, k1), (v1_h, v1))]
    groups = (
        ((ws, ms, ss), opt_s, self_t, z),
        ((wc, mc, sc_), opt_c, cross_t, NZ + z),
        ((wf, mf, sf), opt_f, feed_t, 2 * NZ + z // 2),
    )
    opt = [
        loc.start(src, dst.at[i]) for srcs, dst, _, _ in groups for i, src in enumerate(srcs)
    ]
    greet(
        [((dp + k) % ndp, fs) for k in range(1, ndp)] + [(dp, (fs + k) % nfs) for k in range(1, nfs)]
    )

    def attn_src(base, r):
        rows = pl.ds(r * step, step)
        return lambda zz, cc: attn_g.at[base + zz, :, :, cc, rows]

    def feed_src(j):
        return lambda zz, cc: up_g.at[j, zz, :, :, cc] if zz < 2 else dn_g.at[zz - 2, :, :, cc, j]

    sources = [feed_src(j) for j in range(4)] + [attn_src(b, r) for b in (4, 0) for r in range(2)]
    n = len(sources)
    sc, sl, s1, s2, sz = {}, {}, {}, {}, {}

    def phase_0(t):
        for zz in range(NZ):
            sc[t, zz] = cp.remote(sources[t](zz, 1 - c), r1.at[t, zz], to_c)
            sl[t, zz] = loc.start(sources[t](zz, c), held.at[t % held.shape[0], zz])

    def add_c(t, fixed_y, fixed_x, rows):
        slot = t % held.shape[0]

        def body(i, _):
            zz, o = i // 2, i % 2
            yy = o if fixed_y is None else fixed_y
            xx = o if fixed_x is None else fixed_x
            r1[t, zz, yy, xx, rows] = r1[t, zz, yy, xx, rows] + held[slot, zz, yy, xx, rows]
            return 0

        lax.fori_loop(0, NZ * 2, body, 0)

    def phase_c(t):
        for zz in range(NZ):
            sc[t, zz].wait_recv()
            sl[t, zz].wait()
        add_c(t, None, 1 - x, head)
        s1[t, 0] = cp.remote(r1.at[t, :, :, 1 - x, head], r2a.at[t], to_x)
        add_c(t, 1 - y, None, rest)
        s1[t, 1] = cp.remote(r1.at[t, :, 1 - y, :, rest], r2b.at[t], to_y)
        add_c(t, None, x, head)
        add_c(t, y, None, rest)

    def add_1(t, yy, xx, rows, got, where):
        def body(zz, _):
            r1[t, zz, yy, xx, rows] = r1[t, zz, yy, xx, rows] + got[t, zz, where]
            return 0

        lax.fori_loop(0, NZ, body, 0)

    def phase_1(t):
        s1[t, 0].wait_recv()
        add_1(t, 1 - y, x, head, r2a, 1 - y)
        s2[t, 0] = cp.remote(r1.at[t, :, 1 - y, x, head], r3a.at[t], to_y)
        s1[t, 1].wait_recv()
        add_1(t, y, 1 - x, rest, r2b, 1 - x)
        s2[t, 1] = cp.remote(r1.at[t, :, y, 1 - x, rest], r3b.at[t], to_x)
        add_1(t, y, x, head, r2a, y)
        add_1(t, y, x, rest, r2b, x)

    def phase_2(t):
        s2[t, 0].wait_recv()
        s2[t, 1].wait_recv()

        def body(zz, _):
            r1[t, zz, y, x, head] = r1[t, zz, y, x, head] + r3a[t, zz]
            r1[t, zz, y, x, rest] = r1[t, zz, y, x, rest] + r3b[t, zz]
            return 0

        lax.fori_loop(0, NZ, body, 0)
        for k in range(1, NZ):
            zt = (z + k) % NZ
            sz[t, k] = cp.remote(r1.at[t, zt, y, x], rz.at[t, k - 1], peer_id(zt, y, x, c))

    def lines_of(dst, start, stride):
        for i in range(per):
            dst[pl.ds(start + i, step, stride=stride), :] = whole[:, i * LANES : (i + 1) * LANES]

    def phase_z(t):
        for k in range(1, NZ):
            sz[t, k].wait_recv()
        total = r1[t, z, y, x].astype(F32)
        for k in range(1, NZ):
            total = total + rz[t, k - 1].astype(F32)
        whole[...] = total
        if t >= 4:
            lines_of((cross_t, self_t)[t // 2 - 2], (t % 2) * step * per, per)
            return
        for up in (True, False):

            @pl.when(z // 2 == (0 if up else 1))
            def _():
                lines_of(feed_t, *feed_lines(t, step, width, up))

    row = lambda i: vec_ref[i : i + 1, :]
    gains = [row(2 * i) for i in range(3)]
    shifts = [row(2 * i + 1) for i in range(3)]
    mem_rows = lambda: mem_v[...].reshape(ex_count * MEMLEN, D)
    up_mat = lambda j: ur[j % ur.shape[0]].reshape(D, D)
    stores, order_a, waited = {}, [], set()

    def stored(*which):
        for m in which:
            if m not in waited:
                stores[m].wait()
                waited.add(m)

    def give(m, value):
        slots, i = ring_a.shape[0], len(order_a)
        if i >= slots:
            stored(order_a[i - slots])
        ring_a[i % slots] = value.astype(BF).reshape(ring_a.shape[1:])
        order_a.append(m)
        stores[m] = loc.start(ring_a.at[i % slots], attn_g.at[m])

    def begin():
        for i in range(EX_DEV):
            rows = pl.ds(i * SUF, SUF)
            seed = seed_of(cot_ref, slen_ref, i)
            sg_ref[rows] = seed
            e3[rows] = seed.astype(BF)
        vecg[...] = jnp.zeros_like(vecg)
        vecg[6:7] = column_sum(e3[...].astype(F32))

    def feed(j):
        dn = weight()
        if j == 0:
            a3_ok.wait()
        slope_ok[j].wait()
        du[j] = (dot_nt(e3[...], dn) * slope_v[j]).astype(BF)
        slot = j % ring_u.shape[0]
        if j >= ring_u.shape[0]:
            stored(8 + j - ring_u.shape[0])
        ring_u[slot] = dot_tn(a3[...], du[j]).astype(BF).reshape(ring_u.shape[1:])
        stores[8 + j] = loc.start(ring_u.at[slot], up_g.at[j])
        vecg[7 + j : 8 + j] = column_sum(du[j].astype(F32))
        if j == 0:
            z_ok.wait()
            h2_ok.wait()
            out_ref[...] = h2[...] + row(6)
        out_ref[...] += dot_nn(z_v[j], dn)
        fetch()

    def feed_down():
        unit, scale = norm_parts(h2[...])
        for j in range(4):
            up_got[j].wait()
            part = dot_nt(du[j], up_mat(j))
            if j == 0:
                h2[...] = part
            else:
                h2[...] += part
            fetch_up()
        grad = h2[...]
        vecg[4:5] = column_sum(grad * unit)
        vecg[5:6] = column_sum(grad)
        sg_ref[...] += norm_back(unit, scale, gains[2], grad)
        db[...] = sg_ref[...].astype(BF)

    def cross_begin():
        cross_ok[0].wait()
        give(7, dot_tn(o2[...], db[...]))
        e3[...] = dot_nt(db[...], weight()).astype(BF)
        fetch()
        for one in cross_ok[1:4]:
            one.wait()

    def cross_part(first, count):
        attend_back(first, count, cross_mask, plen_ref, q2, k2, v2, e3, MEMLEN)

    def cross_query():
        cross_ok[5].wait()
        unit, _ = norm_parts(h1[...])
        a2[...] = (unit * gains[1] + shifts[1]).astype(BF)
        give(4, dot_tn(a2[...], q2[...]))

    def cross_key():
        cross_ok[4].wait()
        give(5, dot_tn(mem_rows(), k2[...]))

    def cross_value():
        give(6, dot_tn(mem_rows(), v2[...]))

    mem_sent = []

    def cross_memory():
        key_mat, value_mat = weight(), weight()
        for i in range(ex_count):
            keys = pl.ds(i * MEMLEN, MEMLEN)
            part = dot_nt(k2[keys], key_mat) + dot_nt(v2[keys], value_mat)
            mem_v[i] = part.astype(BF).reshape(mem_v.shape[1:])
        fetch()
        fetch()
        mem_sent.append(loc.start(mem_v.at[:, dp], mem_t.at[pl.ds(ex_count * dp, ex_count)]))
        for k in range(1, ndp):
            mem_sent.append(
                cp.remote(
                    mem_v.at[:, (dp + k) % ndp],
                    mem_t.at[pl.ds(ex_count * dp, ex_count)],
                    ((dp + k) % ndp, fs),
                )
            )

    def cross_end():
        grad = dot_nt(q2[...], weight())
        fetch()
        unit, scale = norm_parts(h1[...])
        vecg[2:3] = column_sum(grad * unit)
        vecg[3:4] = column_sum(grad)
        sg_ref[...] += norm_back(unit, scale, gains[1], grad)
        db[...] = sg_ref[...].astype(BF)

    def self_begin():
        for one in self_ok:
            one.wait()
        give(3, dot_tn(o1[...], db[...]))
        e3[...] = dot_nt(db[...], weight()).astype(BF)
        fetch()
        unit, _ = norm_parts(x_ref[...].astype(F32))
        a1[...] = (unit * gains[0] + shifts[0]).astype(BF)

    def self_part():
        attend_back(0, EX_DEV, self_mask, slen_ref, q1, k1, v1, e3, SUF)

    def self_weights():
        for i, ref in enumerate((q1, k1, v1)):
            give(i, dot_tn(a1[...], ref[...]))

    def self_end():
        grad = dot_nt(q1[...], weight())
        grad = grad + dot_nt(k1[...], weight())
        grad = grad + dot_nt(v1[...], weight())
        unit, scale = norm_parts(x_ref[...].astype(F32))
        vecg[0:1] = column_sum(grad * unit)
        vecg[1:2] = column_sum(grad)
        sg_ref[...] += norm_back(unit, scale, gains[0], grad)

    vec_cp = []

    def vec_step(i):
        if i == 0:
            vec_cp.append(cp.remote(vecg, v_recv.at[0], to_c))
            return
        vec_cp[-1].wait_recv()
        i -= 1
        v_send[i] = (vecg[...] if i == 0 else v_send[i - 1]) + v_recv[i]
        if i < 2:
            vec_cp.append(cp.remote(v_send.at[i], v_recv.at[i + 1], (to_x, to_y)[i]))
        else:
            v_z[z] = v_send[2]
            for k in range(1, NZ):
                vec_cp.append(cp.remote(v_send.at[2], v_z.at[z], peer_id((z + k) % NZ, y, x, c)))

    begin()
    feed(0)
    feed(1)
    stored(8)
    phase_0(0)
    feed(2)
    stored(9)
    phase_0(1)
    phase_c(0)
    feed(3)
    stored(10)
    phase_0(2)
    phase_c(1)
    stored(11)
    phase_0(3)
    feed_down()
    phase_c(2)
    cross_begin()
    phase_c(3)
    cross_part(0, 2)
    phase_1(0)
    cross_part(2, 2)
    cross_query()
    phase_2(0)
    phase_1(1)
    cross_key()
    cross_value()
    stored(4, 5, 6, 7)
    phase_0(4)
    phase_0(5)
    cross_memory()
    phase_2(1)
    phase_c(4)
    phase_1(2)
    phase_z(0)
    cross_end()
    self_begin()
    phase_c(5)
    self_part()
    self_weights()
    stored(0, 1, 2, 3)
    phase_0(6)
    phase_0(7)
    phase_2(2)
    phase_1(3)
    self_end()
    vec_step(0)
    phase_z(1)
    phase_c(6)
    phase_c(7)
    vec_step(1)
    phase_2(3)
    phase_1(4)
    phase_z(2)
    vec_step(2)
    phase_1(5)
    phase_2(4)
    phase_z(3)
    vec_step(3)
    phase_1(6)
    phase_2(5)
    phase_z(4)
    phase_1(7)
    phase_2(6)
    phase_z(5)
    phase_2(7)
    phase_z(6)
    for one in vec_cp[3:]:
        one.wait_recv()
    whole[0:16] = (v_z[0] + v_z[1]) + (v_z[2] + v_z[3])
    vec_t[...] = jnp.zeros_like(vec_t)
    for i in range(per):
        vec_t[pl.ds(i, 11, stride=per), :] = whole[0:11, i * LANES : (i + 1) * LANES]
    phase_z(7)
    sq = squares(self_t[...]) + squares(cross_t[...]) + squares(feed_t[...])
    sq = sum_everywhere(cp, sq, qa, qb, dp, fs) + squares(vec_t[...])
    sq_t[...] = sq
    factor = clip_of(sq)
    rows = lax.broadcasted_iota(jnp.int32, (32, LANES), 0)
    tile = jnp.zeros((32, LANES), F32)
    for one in opt:
        one.wait()
    for _, dst, g, line in groups:
        w = dst[0]
        ratio = lamb_step(w, g[...], dst[1], dst[2], factor)[2]
        for first, a in ((0, ratio), (16, w)):
            part = jnp.sum(a * a, axis=0, keepdims=True)
            tile = tile + jnp.where(rows == first + line, part, 0.0)
    norm_t[...] = sum_everywhere(cp, tile, na, nb, dp, fs)
    mem_sent[0].wait()
    for one in mem_sent[1:]:
        one.wait_recv()
    cp.drain()


def backward_all(kept, x, cot, vec, slen, plen, states, rows_a, rows_f, ndp, nfs):
    anywhere = pl.BlockSpec(memory_space=pl.ANY)
    vmem = pl.BlockSpec(memory_space=pltpu.VMEM)
    mem = kept[3]
    ex, _, pos, width = mem.shape
    rows = x.shape[0]
    lines = [w.shape[0] for w in states[:3]]
    step = rows_f
    cut = step * 2 // 3
    split = (2, 2, 2)
    low = lambda *dims: pltpu.VMEM(dims + (width,), BF)
    wide = lambda *dims: pltpu.VMEM(dims, F32)
    shape = lambda *dims: jax.ShapeDtypeStruct(dims, F32)
    vec_rows = 16
    return pl.pallas_call(
        backward_kernel,
        out_shape=[
            shape(rows, width),
            shape(rows, width),
            *[shape(k, LANES) for k in lines],
            jax.ShapeDtypeStruct((ndp * ex, pos, width), BF),
            shape(vec_rows * width // LANES, LANES),
            shape(8, LANES),
            shape(32, LANES),
            jax.ShapeDtypeStruct((8,) + split + (rows_a, width), BF),
            jax.ShapeDtypeStruct((4, 2) + split + (rows_f, width), BF),
        ],
        in_specs=[anywhere] * 18 + [vmem] * 5 + [anywhere] * 9,
        out_specs=[vmem] * 5 + [anywhere] + [vmem] * 3 + [anywhere] * 2,
        scratch_shapes=[
            low(4, width),
            low(2, up_rows(kept[2]), rows_f),
            low(ex, ndp, pos),
            *[low(rows)] * 9,
            low(ex * MEMLEN),
            low(ex * MEMLEN),
            low(4, rows),
            wide(4, rows, width),
            wide(rows, width),
            wide(rows, width),
            low(rows),
            low(4, rows),
            low(rows),
            low(2, *split, rows_a),
            low(2, 2, *split, rows_f),
            low(2, NZ, 2, 2, step),
            low(8, NZ, 2, 2, step),
            low(8, NZ, 2, cut),
            low(8, NZ, 2, step - cut),
            low(8, NZ, cut),
            low(8, NZ, step - cut),
            low(8, NZ - 1, step),
            wide(step, width),
            wide(vec_rows, width),
            wide(3, vec_rows, width),
            wide(3, vec_rows, width),
            wide(NZ, vec_rows, width),
            wide(nfs, 8, LANES),
            wide(ndp, 8, LANES),
            wide(nfs, 32, LANES),
            wide(ndp, 32, LANES),
            *[wide(3, k, LANES) for k in lines],
            pltpu.SemaphoreType.DMA((128,)),
            pltpu.SemaphoreType.DMA((128,)),
            pltpu.SemaphoreType.DMA((96,)),
        ],
        compiler_params=pltpu.CompilerParams(
            collective_id=2, has_side_effects=True, vmem_limit_bytes=60 << 20
        ),
        name="backward_all",
    )(*kept, x, cot, vec, slen, plen, *states)


def up_rows(view):
    return view.shape[0] // 2


def update_kernel(*refs):
    ins, outs = refs[:18], refs[18:]
    gs, ws, ms, vs, (gv, sq, norms) = ins[0:3], ins[3:7], ins[7:11], ins[11:15], ins[15:18]
    z = lax.axis_index("dp") // 2
    factor = clip_of(sq[...])
    sums = jnp.sqrt(jnp.sum(norms[...], axis=1, keepdims=True))
    ratio_norm, weight_norm = sums[0:16], sums[16:32]
    trust = weight_norm / (ratio_norm + trust_eps)
    row = lax.broadcasted_iota(jnp.int32, (16, 1), 0)
    for i, first in enumerate((z, NZ + z, 2 * NZ + z // 2)):
        g = gs[i][...]
        w = ws[i][...]
        m, v, ratio = lamb_step(w, g, ms[i][...], vs[i][...], factor)
        rate = jnp.sum(jnp.where(row == first, trust, 0.0), axis=0, keepdims=True)
        for ref, value in zip(outs[4 * i : 4 * i + 4], (g, m, v, w - learn_rate * rate * ratio)):
            ref[...] = value
    w = ws[3][...]
    g = gv[0 : w.shape[0], :]
    m, v, ratio = lamb_step(w, g, ms[3][...], vs[3][...], factor)
    line = lax.broadcasted_iota(jnp.int32, w.shape, 0)
    spread = lax.broadcasted_iota(jnp.int32, (16, LANES), 1)
    pick = spread == lax.broadcasted_iota(jnp.int32, (16, LANES), 0)
    lanes = spread[0:1]
    on_row = lambda a: jnp.sum(jnp.where(pick, a, 0.0), axis=0, keepdims=True)
    weight_row, ratio_row = on_row(weight_norm), on_row(ratio_norm)
    rate = jnp.zeros(w.shape, F32)
    per = D // LANES
    for i in range(8):
        mine = (line >= i * per) & (line < ((i + 1) * per if i < 7 else w.shape[0]))
        norm = lambda a: norm_of(jnp.where(mine, a * a, 0.0))
        wn, rn = norm(w), norm(ratio)
        rate = jnp.where(mine, wn / (rn + trust_eps), rate)
        weight_row = jnp.where(lanes == 10 + i, wn, weight_row)
        ratio_row = jnp.where(lanes == 10 + i, rn, ratio_row)
    for ref, value in zip(outs[12:16], (g, m, v, w - learn_rate * rate * ratio)):
        ref[...] = value
    outs[16][0:1, :] = weight_row[:, 0:18]
    outs[16][1:2, :] = ratio_row[:, 0:18]
    outs[17][...] = norm_of(sq[...])


def update_all(totals, weights, moments, seconds, vec_total, sq, norms):
    vmem = pl.BlockSpec(memory_space=pltpu.VMEM)
    shape = lambda a: jax.ShapeDtypeStruct(a.shape, F32)
    outs = [shape(a) for a in weights for _ in range(4)]
    outs += [jax.ShapeDtypeStruct((2, 18), F32), jax.ShapeDtypeStruct((1, 1), F32)]
    return pl.pallas_call(
        update_kernel,
        out_shape=outs,
        in_specs=[vmem] * 18,
        out_specs=[vmem] * len(outs),
        compiler_params=pltpu.CompilerParams(vmem_limit_bytes=40 << 20),
        name="update_all",
    )(*totals, *weights, *moments, *seconds, vec_total, sq, norms)


def fast_shards(
    suffix,
    memory,
    prefix_lengths,
    suffix_lengths,
    cotangent,
    self_weights,
    self_moment,
    self_second,
    cross_weights,
    cross_moment,
    cross_second,
    feed_weights,
    feed_moment,
    feed_second,
    vectors,
    vector_moment,
    vector_second,
):
    row_count = EX_DEV * SUF
    ndp, nfs = lax.axis_size("dp"), lax.axis_size("fsdp")
    owners = ndp * nfs
    rows_a, rows_f = self_weights.shape[0] // D, feed_weights.shape[0] // (4 * D)
    flat = lambda *group: [a.reshape(-1, LANES) for a in group]
    weights = flat(self_weights, cross_weights, feed_weights, vectors)
    moments = flat(self_moment, cross_moment, feed_moment, vector_moment)
    seconds = flat(self_second, cross_second, feed_second, vector_second)
    lens = lambda a: jnp.broadcast_to(a[0][:, None, None], (EX_DEV, 8, LANES))
    common = (
        suffix.reshape(row_count, D),
        cotangent.reshape(row_count, D),
        vectors.reshape(-1, D),
        lens(suffix_lengths),
        lens(prefix_lengths),
    )
    attn, feed, *kept = forward_all(weights[:3], memory[0], *common, rows_a, rows_f, ndp)
    kept = [
        attn.reshape(8, D, D),
        feed.reshape(8, D, D),
        feed.reshape(owners, 4, rows_f, D),
        *kept,
    ]
    layer_output, suffix_gradient, *totals, memory_back, vec_sum, squared, norms, _, _ = backward_all(
        kept, *common, weights[:3] + moments[:3] + seconds[:3], rows_a, rows_f, ndp, nfs
    )
    *new, tensor_norms, global_norm = update_all(
        totals, weights, moments, seconds, vec_sum, squared, norms
    )
    return (
        layer_output.reshape(1, EX_DEV, SUF, D),
        suffix_gradient.reshape(1, EX_DEV, SUF, D),
        memory_back.astype(F32)[None],
        *[a.reshape(-1) for a in new],
        tensor_norms,
        global_norm.reshape(()),
    )


def pick(mesh):
    if mesh.shape["dp"] == 8 and mesh.shape["fsdp"] == 4:
        return fast_shards
    return shards


def solution(mesh):
    return jax.shard_map(
        pick(mesh),
        mesh=mesh,
        in_specs=(
            P("fsdp", "dp", None, None),
            P("fsdp", None, "dp", None),
            P("fsdp", "dp"),
            P("fsdp", "dp"),
            P("fsdp", "dp", None, None),
            P(("dp", "fsdp")),
            P(("dp", "fsdp")),
            P(("dp", "fsdp")),
            P(("dp", "fsdp")),
            P(("dp", "fsdp")),
            P(("dp", "fsdp")),
            P(("dp", "fsdp")),
            P(("dp", "fsdp")),
            P(("dp", "fsdp")),
            P(),
            P(),
            P(),
        ),
        out_specs=(
            P("fsdp", "dp", None, None),
            P("fsdp", "dp", None, None),
            P("fsdp", None, "dp", None),
            P(("dp", "fsdp")),
            P(("dp", "fsdp")),
            P(("dp", "fsdp")),
            P(("dp", "fsdp")),
            P(("dp", "fsdp")),
            P(("dp", "fsdp")),
            P(("dp", "fsdp")),
            P(("dp", "fsdp")),
            P(("dp", "fsdp")),
            P(("dp", "fsdp")),
            P(("dp", "fsdp")),
            P(("dp", "fsdp")),
            P(),
            P(),
            P(),
            P(),
            P(),
            P(),
        ),
        check_vma=False,
    )
```

```python
import jax
import jax.numpy as jnp
from jax import lax
from jax.experimental import pallas as pl
from jax.experimental.pallas import tpu as pltpu
from jax.sharding import PartitionSpec as P

D = 768
H = 12
HD = 64
FF = 3072
PATCH = 196
SUF = 64
EX_DEV = 4
MEMLEN = 256


beta_one = 0.5
beta_two = 0.55
step_count = 5
learn_rate = 0.5
decay_weight = 0.01
adam_eps = 1e-06
norm_eps = 1e-06
trust_eps = 1e-06
masked_score = -1e30


def layer_norm(values, norm_gain, norm_shift):
    centred = values - jnp.mean(values, axis=-1, keepdims=True)
    spread = jnp.mean(centred * centred, axis=-1, keepdims=True)
    return centred * lax.rsqrt(spread + norm_eps) * norm_gain + norm_shift


def gelu_tanh(values):
    return jax.nn.gelu(values, approximate=True)


def attend_forward(query_heads, key_heads, value_heads, allowed):
    score_scale = HD ** (-0.5)
    scores = (
        jnp.einsum("bqhe,bkhe->bhqk", query_heads, key_heads, preferred_element_type=jnp.float32)
        * score_scale
    )
    scores = jnp.where(allowed, scores, masked_score)
    attention = jax.nn.softmax(scores, axis=-1)
    totals = jax.nn.logsumexp(scores, axis=-1)
    mixed_rows = jnp.einsum(
        "bhqk,bkhe->bqhe",
        attention.astype(jnp.bfloat16),
        value_heads,
        preferred_element_type=jnp.float32,
    )
    return (mixed_rows, totals)


def attend_backward(query_heads, key_heads, value_heads, allowed, totals, mixed_grad):
    score_scale = HD ** (-0.5)
    scores = (
        jnp.einsum("bqhe,bkhe->bhqk", query_heads, key_heads, preferred_element_type=jnp.float32)
        * score_scale
    )
    scores = jnp.where(allowed, scores, masked_score)
    attention = jnp.exp(scores - totals[..., None])
    value_grad = jnp.einsum(
        "bhqk,bqhe->bkhe",
        attention.astype(jnp.bfloat16),
        mixed_grad,
        preferred_element_type=jnp.float32,
    )
    attention_grad = jnp.einsum(
        "bqhe,bkhe->bhqk", mixed_grad, value_heads, preferred_element_type=jnp.float32
    )
    score_grad = attention * (
        attention_grad - jnp.sum(attention * attention_grad, axis=-1, keepdims=True)
    )
    score_low = score_grad.astype(jnp.bfloat16)
    query_grad = (
        jnp.einsum("bhqk,bkhe->bqhe", score_low, key_heads, preferred_element_type=jnp.float32)
        * score_scale
    )
    key_grad = (
        jnp.einsum("bhqk,bqhe->bkhe", score_low, query_heads, preferred_element_type=jnp.float32)
        * score_scale
    )
    return (query_grad, key_grad, value_grad)


def lamb_step(weight, gradient, moment, second, clip_factor):
    clipped = clip_factor * gradient
    moment_new = beta_one * moment + (1.0 - beta_one) * clipped
    second_new = beta_two * second + (1.0 - beta_two) * clipped * clipped
    ratio = (
        moment_new
        / (1.0 - beta_one**step_count)
        / (jnp.sqrt(second_new / (1.0 - beta_two**step_count)) + adam_eps)
        + decay_weight * weight
    )
    return (moment_new, second_new, ratio)


def segment_sums(values, offset, segment_size, tensor_count):
    labels = (offset + jnp.arange(values.shape[0], dtype=jnp.int32)) // segment_size
    matches = labels[:, None] == jnp.arange(tensor_count, dtype=jnp.int32)[None, :]
    return jnp.sum(jnp.where(matches, values[:, None], 0.0), axis=0)


def segment_spread(factors, offset, length_here, segment_size):
    labels = (offset + jnp.arange(length_here, dtype=jnp.int32)) // segment_size
    matches = labels[:, None] == jnp.arange(factors.shape[0], dtype=jnp.int32)[None, :]
    return jnp.sum(jnp.where(matches, factors[None, :], 0.0), axis=1)


def shards(
    suffix,
    memory,
    prefix_lengths,
    suffix_lengths,
    cotangent,
    self_weights,
    self_moment,
    self_second,
    cross_weights,
    cross_moment,
    cross_second,
    feed_weights,
    feed_moment,
    feed_second,
    vectors,
    vector_moment,
    vector_second,
):
    row_count = EX_DEV * SUF
    attn_shard = self_weights.shape[0]
    feed_shard = feed_weights.shape[0]
    self_full, cross_full, feed_full = (
        lax.all_gather(self_weights.astype(jnp.bfloat16), ("dp", "fsdp"), axis=0, tiled=True),
        lax.all_gather(cross_weights.astype(jnp.bfloat16), ("dp", "fsdp"), axis=0, tiled=True),
        lax.all_gather(feed_weights.astype(jnp.bfloat16), ("dp", "fsdp"), axis=0, tiled=True),
    )
    self_mats = self_full.reshape(4, D, D)
    cross_mats = cross_full.reshape(4, D, D)
    up_mat = feed_full[: D * FF].reshape(D, FF)
    down_mat = feed_full[D * FF :].reshape(FF, D)
    vector_parts = [vectors[segment * D : (segment + 1) * D] for segment in range(7)]
    bias_up = vectors[7 * D :]
    own_memory = lax.all_to_all(memory, "dp", split_axis=1, concat_axis=2, tiled=True)
    memory_rows = own_memory.reshape(EX_DEV * MEMLEN, D)
    suffix_len = suffix_lengths[0]
    prefix_len = prefix_lengths[0]
    positions = jnp.arange(SUF, dtype=jnp.int32)
    causal = positions[:, None] >= positions[None, :]
    self_allowed = (
        causal[None, None, :, :] & (positions[None, :] < suffix_len[:, None])[:, None, None, :]
    )
    memory_pos = jnp.arange(MEMLEN, dtype=jnp.int32)
    cross_allowed = (memory_pos[None, :] < (PATCH + prefix_len)[:, None])[:, None, None, :]
    inputs = suffix.reshape(row_count, D).astype(jnp.float32)
    normed_one = layer_norm(inputs, vector_parts[0], vector_parts[1]).astype(jnp.bfloat16)
    self_qkv = jnp.einsum(
        "rd,jde->jre", normed_one, self_mats[0:3], preferred_element_type=jnp.float32
    ).astype(jnp.bfloat16)
    self_heads = self_qkv.reshape(3, EX_DEV, SUF, H, HD)
    mixed_one, totals_one = attend_forward(
        self_heads[0], self_heads[1], self_heads[2], self_allowed
    )
    mixed_one = mixed_one.reshape(row_count, D).astype(jnp.bfloat16)
    hidden_one = inputs + jnp.dot(mixed_one, self_mats[3], preferred_element_type=jnp.float32)
    normed_two = layer_norm(hidden_one, vector_parts[2], vector_parts[3]).astype(jnp.bfloat16)
    cross_query = jnp.dot(normed_two, cross_mats[0], preferred_element_type=jnp.float32).astype(
        jnp.bfloat16
    )
    cross_kv = jnp.einsum(
        "rd,jde->jre", memory_rows, cross_mats[1:3], preferred_element_type=jnp.float32
    ).astype(jnp.bfloat16)
    query_heads = cross_query.reshape(EX_DEV, SUF, H, HD)
    kv_heads = cross_kv.reshape(2, EX_DEV, MEMLEN, H, HD)
    mixed_two, totals_two = attend_forward(query_heads, kv_heads[0], kv_heads[1], cross_allowed)
    mixed_two = mixed_two.reshape(row_count, D).astype(jnp.bfloat16)
    hidden_two = hidden_one + jnp.dot(mixed_two, cross_mats[3], preferred_element_type=jnp.float32)
    normed_three = layer_norm(hidden_two, vector_parts[4], vector_parts[5]).astype(jnp.bfloat16)
    pre_act = jnp.dot(normed_three, up_mat, preferred_element_type=jnp.float32) + bias_up
    activated = gelu_tanh(pre_act).astype(jnp.bfloat16)
    layer_output = hidden_two + (
        jnp.dot(activated, down_mat, preferred_element_type=jnp.float32) + vector_parts[6]
    )
    valid_rows = (positions[None, :] < suffix_len[:, None]).astype(jnp.float32)
    seed_rows = (
        cotangent.reshape(EX_DEV, SUF, D).astype(jnp.float32) * valid_rows[:, :, None]
    ).reshape(row_count, D)
    seed_low = seed_rows.astype(jnp.bfloat16)
    bias_down_grad = jnp.sum(seed_low.astype(jnp.float32), axis=0)
    down_grad = jnp.einsum("rf,rd->fd", activated, seed_low, preferred_element_type=jnp.float32)
    activated_grad = jnp.einsum("rd,fd->rf", seed_low, down_mat, preferred_element_type=jnp.float32)
    _, gelu_back = jax.vjp(gelu_tanh, pre_act)
    pre_grad = gelu_back(activated_grad)[0].astype(jnp.bfloat16)
    bias_up_grad = jnp.sum(pre_grad.astype(jnp.float32), axis=0)
    up_grad = jnp.einsum("rd,rf->df", normed_three, pre_grad, preferred_element_type=jnp.float32)
    normed_three_grad = jnp.einsum(
        "rf,df->rd", pre_grad, up_mat, preferred_element_type=jnp.float32
    )
    _, norm_three_back = jax.vjp(layer_norm, hidden_two, vector_parts[4], vector_parts[5])
    through_three, gain_three_grad, shift_three_grad = norm_three_back(normed_three_grad)
    hidden_two_grad = seed_rows + through_three
    feed_flat = jnp.concatenate([up_grad.reshape(-1), down_grad.reshape(-1)])
    branch_two = hidden_two_grad.astype(jnp.bfloat16)
    cross_out_grad = jnp.einsum(
        "rd,re->de", mixed_two, branch_two, preferred_element_type=jnp.float32
    )
    mixed_two_grad = jnp.einsum(
        "re,de->rd", branch_two, cross_mats[3], preferred_element_type=jnp.float32
    ).astype(jnp.bfloat16)
    query_two_grad, key_two_grad, value_two_grad = attend_backward(
        query_heads,
        kv_heads[0],
        kv_heads[1],
        cross_allowed,
        totals_two,
        mixed_two_grad.reshape(EX_DEV, SUF, H, HD),
    )
    cross_query_grad = query_two_grad.reshape(row_count, D).astype(jnp.bfloat16)
    cross_kv_grad = (
        jnp.stack([key_two_grad, value_two_grad])
        .reshape(2, EX_DEV * MEMLEN, D)
        .astype(jnp.bfloat16)
    )
    query_weight_grad = jnp.einsum(
        "rd,re->de", normed_two, cross_query_grad, preferred_element_type=jnp.float32
    )
    kv_weight_grad = jnp.einsum(
        "rd,jre->jde", memory_rows, cross_kv_grad, preferred_element_type=jnp.float32
    )
    normed_two_grad = jnp.einsum(
        "re,de->rd", cross_query_grad, cross_mats[0], preferred_element_type=jnp.float32
    )
    memory_local_grad = jnp.einsum(
        "jre,jde->rd", cross_kv_grad, cross_mats[1:3], preferred_element_type=jnp.float32
    )
    memory_gradient = lax.all_to_all(
        memory_local_grad.reshape(1, EX_DEV, MEMLEN, D),
        "dp",
        split_axis=2,
        concat_axis=1,
        tiled=True,
    )
    _, norm_two_back = jax.vjp(layer_norm, hidden_one, vector_parts[2], vector_parts[3])
    through_two, gain_two_grad, shift_two_grad = norm_two_back(normed_two_grad)
    hidden_one_grad = hidden_two_grad + through_two
    cross_flat = jnp.concatenate(
        [query_weight_grad[None], kv_weight_grad, cross_out_grad[None]], axis=0
    ).reshape(-1)
    branch_one = hidden_one_grad.astype(jnp.bfloat16)
    self_out_grad = jnp.einsum(
        "rd,re->de", mixed_one, branch_one, preferred_element_type=jnp.float32
    )
    mixed_one_grad = jnp.einsum(
        "re,de->rd", branch_one, self_mats[3], preferred_element_type=jnp.float32
    ).astype(jnp.bfloat16)
    query_one_grad, key_one_grad, value_one_grad = attend_backward(
        self_heads[0],
        self_heads[1],
        self_heads[2],
        self_allowed,
        totals_one,
        mixed_one_grad.reshape(EX_DEV, SUF, H, HD),
    )
    self_qkv_grad = (
        jnp.stack([query_one_grad, key_one_grad, value_one_grad])
        .reshape(3, row_count, D)
        .astype(jnp.bfloat16)
    )
    qkv_weight_grad = jnp.einsum(
        "rd,jre->jde", normed_one, self_qkv_grad, preferred_element_type=jnp.float32
    )
    normed_one_grad = jnp.einsum(
        "jre,jde->rd", self_qkv_grad, self_mats[0:3], preferred_element_type=jnp.float32
    )
    _, norm_one_back = jax.vjp(layer_norm, inputs, vector_parts[0], vector_parts[1])
    through_one, gain_one_grad, shift_one_grad = norm_one_back(normed_one_grad)
    suffix_gradient = (hidden_one_grad + through_one).reshape(1, EX_DEV, SUF, D)
    self_flat = jnp.concatenate([qkv_weight_grad, self_out_grad[None]], axis=0).reshape(-1)
    owners = lax.axis_size(("dp", "fsdp"))
    joined = jnp.concatenate(
        [
            self_flat.reshape(owners, attn_shard),
            cross_flat.reshape(owners, attn_shard),
            feed_flat.reshape(owners, feed_shard),
        ],
        axis=1,
    ).reshape(-1)
    owned = lax.psum_scatter(joined, ("dp", "fsdp"), scatter_dimension=0, tiled=True)
    self_total = owned[:attn_shard]
    cross_total = owned[attn_shard : 2 * attn_shard]
    feed_total = owned[2 * attn_shard :]
    vector_partial = jnp.concatenate(
        [
            gain_one_grad,
            shift_one_grad,
            gain_two_grad,
            shift_two_grad,
            gain_three_grad,
            shift_three_grad,
            bias_down_grad,
            bias_up_grad,
        ]
    )
    shard_index = lax.axis_index(("dp", "fsdp"))
    attn_offset = shard_index * attn_shard
    feed_offset = shard_index * feed_shard
    grad_squares = jnp.concatenate(
        [
            segment_sums(self_total * self_total, attn_offset, D * D, 4),
            segment_sums(cross_total * cross_total, attn_offset, D * D, 4),
            segment_sums(feed_total * feed_total, feed_offset, D * FF, 2),
        ]
    )
    weight_squares = jnp.concatenate(
        [
            segment_sums(self_weights * self_weights, attn_offset, D * D, 4),
            segment_sums(cross_weights * cross_weights, attn_offset, D * D, 4),
            segment_sums(feed_weights * feed_weights, feed_offset, D * FF, 2),
        ]
    )
    vector_total, grad_summed, weight_summed = lax.psum(
        (vector_partial, grad_squares, weight_squares), ("dp", "fsdp")
    )
    squared_total = jnp.sum(grad_summed) + jnp.sum(vector_total * vector_total)
    global_norm = jnp.sqrt(squared_total)
    clip_factor = jnp.minimum(1.0, 1.0 / global_norm)
    self_momentum, self_variance, self_ratio = lamb_step(
        self_weights, self_total, self_moment, self_second, clip_factor
    )
    cross_momentum, cross_variance, cross_ratio = lamb_step(
        cross_weights, cross_total, cross_moment, cross_second, clip_factor
    )
    feed_momentum, feed_variance, feed_ratio = lamb_step(
        feed_weights, feed_total, feed_moment, feed_second, clip_factor
    )
    ratio_squares = jnp.concatenate(
        [
            segment_sums(self_ratio * self_ratio, attn_offset, D * D, 4),
            segment_sums(cross_ratio * cross_ratio, attn_offset, D * D, 4),
            segment_sums(feed_ratio * feed_ratio, feed_offset, D * FF, 2),
        ]
    )
    update_summed = lax.psum(ratio_squares, ("dp", "fsdp"))
    weight_norms = jnp.sqrt(weight_summed)
    ratio_norms = jnp.sqrt(update_summed)
    trust_ratio = weight_norms / (ratio_norms + trust_eps)
    self_master = (
        self_weights
        - learn_rate * segment_spread(trust_ratio[0:4], attn_offset, attn_shard, D * D) * self_ratio
    )
    cross_master = (
        cross_weights
        - learn_rate
        * segment_spread(trust_ratio[4:8], attn_offset, attn_shard, D * D)
        * cross_ratio
    )
    feed_master = (
        feed_weights
        - learn_rate
        * segment_spread(trust_ratio[8:10], feed_offset, feed_shard, D * FF)
        * feed_ratio
    )
    vector_momentum, vector_variance, vector_ratio = lamb_step(
        vectors, vector_total, vector_moment, vector_second, clip_factor
    )
    edges = [0, D, 2 * D, 3 * D, 4 * D, 5 * D, 6 * D, 7 * D, 7 * D + FF]
    vector_wn = []
    vector_rn = []
    new_pieces = []
    for segment in range(8):
        weight_part = vectors[edges[segment] : edges[segment + 1]]
        ratio_part = vector_ratio[edges[segment] : edges[segment + 1]]
        weight_norm = jnp.sqrt(jnp.sum(weight_part * weight_part))
        ratio_norm = jnp.sqrt(jnp.sum(ratio_part * ratio_part))
        piece_trust = weight_norm / (ratio_norm + trust_eps)
        vector_wn.append(weight_norm)
        vector_rn.append(ratio_norm)
        new_pieces.append(weight_part - learn_rate * piece_trust * ratio_part)
    vector_master = jnp.concatenate(new_pieces)
    tensor_norms = jnp.stack(
        [
            jnp.concatenate([weight_norms, jnp.stack(vector_wn)]),
            jnp.concatenate([ratio_norms, jnp.stack(vector_rn)]),
        ]
    )
    return (
        layer_output.reshape(1, EX_DEV, SUF, D),
        suffix_gradient,
        memory_gradient,
        self_total,
        self_momentum,
        self_variance,
        self_master,
        cross_total,
        cross_momentum,
        cross_variance,
        cross_master,
        feed_total,
        feed_momentum,
        feed_variance,
        feed_master,
        vector_total,
        vector_momentum,
        vector_variance,
        vector_master,
        tensor_norms,
        global_norm,
    )


BF = jnp.bfloat16
F32 = jnp.float32
MESH = pl.DeviceIdType.MESH
NZ = 4
AHEAD = 6
MEM_AT = 3


def place():
    dp, fs = lax.axis_index("dp"), lax.axis_index("fsdp")
    return dp, fs, dp // 2, dp % 2, fs // 2, fs % 2


def peer_id(z, y, x, c):
    return (z * 2 + y, x * 2 + c)


def greet(ids):
    bar = pltpu.get_barrier_semaphore()
    for where in ids:
        pl.semaphore_signal(bar, inc=1, device_id=where, device_id_type=MESH)
    pl.semaphore_wait(bar, len(ids))


class Copies:
    def __init__(self, send, recv, local):
        self.send, self.recv, self.local = send, recv, local
        self.remotes, self.locals = 0, 0
        self.open = []

    def remote(self, src, dst, where):
        i = self.remotes
        self.remotes += 1
        cp = pltpu.make_async_remote_copy(
            src_ref=src,
            dst_ref=dst,
            send_sem=self.send.at[i],
            recv_sem=self.recv.at[i],
            device_id=where,
            device_id_type=MESH,
        )
        cp.start()
        self.open.append(cp)
        return cp

    def here(self, src, dst):
        cp = pltpu.make_async_copy(src, dst, self.local.at[self.locals])
        self.locals += 1
        cp.start()
        return cp

    def drain(self):
        for cp in self.open:
            cp.wait_send()


LANES = 128


def rows_of(flat, dst, j, start, stride):
    rows, width = dst.shape[1:]
    for i in range(width // LANES):
        part = flat[pl.ds(start + i, rows, stride=stride), :]
        dst[j, :, i * LANES : (i + 1) * LANES] = part.astype(dst.dtype)


def feed_lines(j, rows, width, up):
    per = width // LANES
    return (j * per, 4 * per) if up else (j * rows * per, per)


def squares(v):
    return jnp.sum((v * v).reshape(v.shape[0] // 8, 8, LANES), axis=0)


def sum_everywhere(cp, mine, slots_a, slots_b, dp, fs):
    nfs, ndp = slots_a.shape[0], slots_b.shape[0]
    slots_a[fs] = mine
    got = [
        cp.remote(slots_a.at[fs], slots_a.at[fs], (dp, (fs + k) % nfs)) for k in range(1, nfs)
    ]
    for one in got:
        one.wait_recv()
    total = slots_a[0]
    for k in range(1, nfs):
        total = total + slots_a[k]
    slots_b[dp] = total
    got = [
        cp.remote(slots_b.at[dp], slots_b.at[dp], ((dp + k) % ndp, fs)) for k in range(1, ndp)
    ]
    for one in got:
        one.wait_recv()
    total = slots_b[0]
    for k in range(1, ndp):
        total = total + slots_b[k]
    return total


def lamb_sums(w, g, m, s, factor):
    ratio = lamb_step(w[...], g[...], m[...], s[...], factor)[2]
    return jnp.sum(ratio * ratio, axis=0, keepdims=True)


def norm_of(sq):
    return jnp.sqrt(jnp.sum(jnp.sum(sq, axis=1, keepdims=True), axis=0, keepdims=True))


def clip_of(sq):
    return jnp.minimum(1.0, 1.0 / norm_of(sq))


def dot_nn(a, b):
    return lax.dot_general(a, b, (((1,), (0,)), ((), ())), preferred_element_type=F32)


def dot_nt(a, b):
    return lax.dot_general(a, b, (((1,), (1,)), ((), ())), preferred_element_type=F32)


def dot_tn(a, b):
    return lax.dot_general(a, b, (((0,), (0,)), ((), ())), preferred_element_type=F32)


def norm_parts(values):
    centred = values - jnp.mean(values, axis=-1, keepdims=True)
    scale = lax.rsqrt(jnp.mean(centred * centred, axis=-1, keepdims=True) + norm_eps)
    return centred * scale, scale


def norm_back(unit, scale, gain, grad):
    e = grad * gain
    return scale * (
        e
        - jnp.mean(e, axis=-1, keepdims=True)
        - unit * jnp.mean(e * unit, axis=-1, keepdims=True)
    )


def column_sum(values):
    return jnp.sum(values, axis=0, keepdims=True)


def split_heads(pair):
    low = lax.broadcasted_iota(jnp.int32, pair.shape, 1) < HD
    zero = jnp.zeros_like(pair)
    return jnp.concatenate([jnp.where(low, pair, zero), jnp.where(low, zero, pair)], axis=0)


def join_heads(stacked):
    rows = stacked.shape[0] // 2
    low = lax.broadcasted_iota(jnp.int32, (rows, 2 * HD), 1) < HD
    return jnp.where(low, stacked[:rows], stacked[rows:])


def soft_rows(scores, allowed):
    scores = jnp.where(allowed, scores * HD ** (-0.5), masked_score)
    top = jnp.max(scores, axis=-1, keepdims=True)
    p = jnp.exp(scores - top)
    return p / jnp.sum(p, axis=-1, keepdims=True)


def self_mask(lens):
    shape = (2 * SUF, SUF)
    query = lax.broadcasted_iota(jnp.int32, shape, 0) % SUF
    key = lax.broadcasted_iota(jnp.int32, shape, 1)
    return (key <= query) & (key < lens[0:1, 0:SUF])


def cross_mask(lens):
    key = lax.broadcasted_iota(jnp.int32, (2 * SUF, MEMLEN), 1)
    seen = jnp.concatenate([lens[0:1]] * (MEMLEN // 128), axis=1)
    return key < PATCH + seen


PAIRS = H // 2


def gelu_parts(u):
    rate = (2.0 / jnp.pi) ** 0.5
    square = u * u
    t = jnp.tanh(rate * (u + 0.044715 * u * square))
    half = 0.5 * (1.0 + t)
    slope = half + 0.5 * u * (1.0 - t * t) * (rate * (1.0 + 3 * 0.044715 * square))
    return u * half, slope


def head_rows(ex, key_rows):
    rows = pl.ds(pl.multiple_of(ex * SUF, SUF), SUF)
    return rows, pl.ds(pl.multiple_of(ex * key_rows, key_rows), key_rows)


def attend_back(mask_of, lens, q_ref, k_ref, v_ref, do_ref, key_rows):
    scale = HD ** (-0.5)

    def body(ex, _):
        allowed = mask_of(lens[ex])
        rows, keys = head_rows(ex, key_rows)
        lanes = [pl.ds(m * 2 * HD, 2 * HD) for m in range(PAIRS)]
        qs = [split_heads(q_ref[rows, at]) for at in lanes]
        ks = [k_ref[keys, at] for at in lanes]
        vs = [v_ref[keys, at] for at in lanes]
        ds_out = [split_heads(do_ref[rows, at]) for at in lanes]
        scores = [dot_nt(q, k) for q, k in zip(qs, ks)]
        dps = [dot_nt(d, v) for d, v in zip(ds_out, vs)]
        ps = [soft_rows(s, allowed) for s in scores]
        dss = [
            (p * (dp - jnp.sum(p * dp, axis=-1, keepdims=True))).astype(BF) for p, dp in zip(ps, dps)
        ]
        dvs = [dot_tn(p.astype(BF), d) for p, d in zip(ps, ds_out)]
        dqs = [join_heads(dot_nn(ds, k)) * scale for ds, k in zip(dss, ks)]
        dks = [dot_tn(ds, q) * scale for ds, q in zip(dss, qs)]
        for at, dq, dk, dv in zip(lanes, dqs, dks, dvs):
            v_ref[keys, at] = dv.astype(BF)
            q_ref[rows, at] = dq.astype(BF)
            k_ref[keys, at] = dk.astype(BF)
        return 0

    lax.fori_loop(0, EX_DEV, body, 0)


def attend(mask_of, lens, q_ref, k_ref, v_ref, o_ref, key_rows):
    def body(ex, _):
        allowed = mask_of(lens[ex])
        rows, keys = head_rows(ex, key_rows)
        lanes = [pl.ds(m * 2 * HD, 2 * HD) for m in range(PAIRS)]
        qs = [split_heads(q_ref[rows, at]) for at in lanes]
        scores = [dot_nt(q, k_ref[keys, at]) for q, at in zip(qs, lanes)]
        ps = [soft_rows(s, allowed).astype(BF) for s in scores]
        outs = [join_heads(dot_nn(p, v_ref[keys, at])).astype(BF) for p, at in zip(ps, lanes)]
        for at, out in zip(lanes, outs):
            o_ref[rows, at] = out
        return 0

    lax.fori_loop(0, EX_DEV, body, 0)


def seed_of(cot_ref, lens, ex):
    line = lax.broadcasted_iota(jnp.int32, (SUF, D), 0)
    length = jnp.concatenate([lens[ex, 0:1]] * (D // LANES), axis=1)
    return cot_ref[pl.ds(ex * SUF, SUF)].astype(F32) * (line < length).astype(F32)


class Local:
    def __init__(self, sems):
        self.sems, self.used, self.open = sems, 0, []

    def start(self, src, dst):
        cp = pltpu.make_async_copy(src, dst, self.sems.at[self.used])
        self.used += 1
        cp.start()
        return cp

    def out(self, src, dst):
        self.open.append(self.start(src, dst))

    def drain(self):
        for cp in self.open:
            cp.wait()


def forward_kernel(
    self_w, cross_w, feed_w, mem_in, x_ref, cot_ref, vec_ref, slen_ref, plen_ref,
    attn_h, feed_h, mem_h, q1_h, k1_h, v1_h, o1_h, q2_h, o2_h, a3_h, k2_h, v2_h, z_h, slope_h,
    h1_h, h2_h, dn_g,
    self_in, cross_in, feed_in, self_v, cross_v, feed_v, mem_v, a1, q1, k1, v1, o1, a2, q2, o2, a3,
    e3, k2, v2, z_v, slope_v, h1, h2, ring, send, recv, local,
):
    dp, fs, z, y, x, c = place()
    ex, ndp = mem_v.shape[0], mem_v.shape[1]
    to_y, to_x, to_c = peer_id(z, 1 - y, x, c), peer_id(z, y, 1 - x, c), peer_id(z, y, x, 1 - c)
    per = D // LANES
    cp, loc = Copies(send, recv, None), Local(local)
    rows_of(self_w, self_in, 0, 0, per)
    greet([((dp + k) % ndp, fs) for k in range(1, ndp)] + [to_x, to_c])

    step = feed_in.shape[1]
    cut = step * 2 // 3
    chunks = []
    for src, dst in ((self_in, self_v), (cross_in, cross_v), (feed_in, feed_v)):
        for j in range(src.shape[0]):
            for first in range(0, src.shape[1], step):
                chunks.append(
                    (src, dst, j, pl.ds(first, step), pl.ds(first, cut), pl.ds(first + cut, step - cut))
                )
    zc, s2, s3, s4, mem, own = {}, {}, {}, {}, [], {}

    def send_z(t):
        src, dst, j, rows, r0, r1 = chunks[t]
        own[t] = loc.start(src.at[j, rows], dst.at[z, y, x, c, j, rows])
        for k in range(1, NZ):
            zc[t, k] = cp.remote(
                src.at[j, rows], dst.at[z, y, x, c, j, rows], peer_id((z + k) % NZ, y, x, c)
            )
        send_2(t, 0)

    def send_2(t, k):
        src, dst, j, rows, r0, r1 = chunks[t]
        zz = (z + NZ - k) % NZ
        for part, cut_rows, where in ((0, r0, to_y), (1, r1, to_x)):
            here = src.at[j, cut_rows] if k == 0 else dst.at[zz, y, x, c, j, cut_rows]
            s2[t, k, part] = cp.remote(here, dst.at[zz, y, x, c, j, cut_rows], where)

    def send_3(t):
        src, dst, j, rows, r0, r1 = chunks[t]
        s3[t, 0] = cp.remote(dst.at[:, :, x, c, j, r0], dst.at[:, :, x, c, j, r0], to_x)
        s3[t, 1] = cp.remote(dst.at[:, y, :, c, j, r1], dst.at[:, y, :, c, j, r1], to_y)

    def send_4(t):
        src, dst, j, rows, r0, r1 = chunks[t]
        s4[t] = cp.remote(dst.at[:, :, :, c, j, rows], dst.at[:, :, :, c, j, rows], to_c)

    def send_mem():
        mem.append(loc.start(mem_in.at[pl.ds(ex * dp, ex)], mem_v.at[:, dp]))
        for k in range(1, ndp):
            mem.append(
                cp.remote(
                    mem_in.at[pl.ds(ex * ((dp + k) % ndp), ex)],
                    mem_v.at[:, dp],
                    ((dp + k) % ndp, fs),
                )
            )

    row = lambda i: vec_ref[i : i + 1, :]
    g1, b1, g2, b2, g3, b3 = [row(i) for i in range(6)]
    square = lambda a: a.reshape(D, D)
    self_mat = lambda m: square(self_v[m])
    cross_mat = lambda m: square(cross_v[m])
    mem_rows = lambda: mem_v[...].reshape(ex * MEMLEN, D)

    def begin():
        unit, _ = norm_parts(x_ref[...].astype(F32))
        a1[...] = (unit * g1 + b1).astype(BF)
        for i in range(EX_DEV):
            e3[pl.ds(i * SUF, SUF)] = seed_of(cot_ref, slen_ref, i).astype(BF)

    def self_qkv():
        s4[0].wait_recv()
        s4[1].wait_recv()
        loc.out(self_v.at[:, :, :, :, 0], attn_h.at[pl.ds(0, 4)])
        for i, (ref, dst) in enumerate(((q1, q1_h), (k1, k1_h), (v1, v1_h))):
            ref[...] = dot_nn(a1[...], self_mat(i)).astype(BF)
            loc.out(ref, dst)

    def self_attention():
        attend(self_mask, slen_ref, q1, k1, v1, o1, SUF)
        loc.out(o1, o1_h)
        h1[...] = x_ref[...].astype(F32) + dot_nn(o1[...], self_mat(3))
        loc.out(h1, h1_h)
        unit, _ = norm_parts(h1[...])
        a2[...] = (unit * g2 + b2).astype(BF)

    def cross_query():
        s4[2].wait_recv()
        s4[3].wait_recv()
        loc.out(cross_v.at[:, :, :, :, 0], attn_h.at[pl.ds(4, 4)])
        q2[...] = dot_nn(a2[...], cross_mat(0)).astype(BF)
        loc.out(q2, q2_h)

    def cross_keys():
        mem[0].wait()
        for one in mem[1:]:
            one.wait_recv()
        loc.out(mem_v, mem_h)
        for i, ref, dst in ((1, k2, k2_h), (2, v2, v2_h)):
            ref[...] = dot_nn(mem_rows(), cross_mat(i)).astype(BF)
            loc.out(ref, dst)

    def cross_attention():
        attend(cross_mask, plen_ref, q2, k2, v2, o2, MEMLEN)
        loc.out(o2, o2_h)

    def cross_out():
        h2[...] = h1[...] + dot_nn(o2[...], cross_mat(3))
        loc.out(h2, h2_h)
        unit, _ = norm_parts(h2[...])
        a3[...] = (unit * g3 + b3).astype(BF)
        loc.out(a3, a3_h)

    def feed(j):
        s4[4 + j].wait_recv()
        u = dot_nn(a3[...], square(feed_v[0:2, :, :, :, j])) + row(7 + j)
        act, bend = gelu_parts(u)
        z_v[j] = act.astype(BF)
        slope_v[j] = bend
        loc.out(z_v.at[j], z_h.at[j])
        loc.out(slope_v.at[j], slope_h.at[j])
        ring[j] = dot_tn(z_v[j], e3[...]).astype(BF).reshape(ring.shape[1:])
        loc.out(ring.at[j], dn_g.at[j // 2, j % 2])
        if j == 3:
            loc.out(feed_v, feed_h)

    def prepare_cross():
        rows_of(cross_w, cross_in, 0, 0, per)

    def prepare_feed():
        for up in (True, False):

            @pl.when(z // 2 == (0 if up else 1))
            def _():
                for j in range(4):
                    rows_of(feed_w, feed_in, j, *feed_lines(j, *feed_in.shape[1:], up))

    def pass_2(t, k):
        zc[t, k].wait_recv()
        send_2(t, k)

    def pass_3(t):
        own[t].wait()
        for k in range(NZ):
            for part in (0, 1):
                s2[t, k, part].wait_recv()
        send_3(t)

    def pass_4(t):
        s3[t, 0].wait_recv()
        s3[t, 1].wait_recv()
        send_4(t)

    for step_of, *which in (
        (send_z, 0), (send_z, 1), (begin,), (prepare_cross,), (send_z, 2), (pass_2, 0, 1),
        (pass_2, 0, 2), (pass_2, 0, 3), (send_z, 3), (pass_2, 1, 1), (pass_3, 0), (pass_2, 1, 2),
        (pass_2, 1, 3), (prepare_feed,), (send_z, 4), (pass_2, 2, 1), (pass_2, 2, 2),
        (pass_2, 2, 3), (pass_4, 0), (send_z, 5), (pass_3, 1), (pass_2, 3, 1), (pass_3, 2),
        (pass_2, 3, 2), (pass_2, 3, 3), (send_z, 6), (pass_2, 4, 1), (pass_2, 4, 2), (pass_4, 1),
        (pass_2, 4, 3), (send_z, 7), (pass_2, 5, 1), (self_qkv,), (pass_2, 5, 2),
        (self_attention,), (pass_4, 2), (pass_2, 5, 3), (pass_2, 6, 1), (send_mem,), (pass_3, 3),
        (pass_2, 6, 2), (pass_3, 4), (pass_2, 6, 3), (pass_3, 5), (pass_2, 7, 1), (pass_2, 7, 2),
        (pass_2, 7, 3), (pass_4, 3), (cross_query,), (pass_4, 4), (pass_3, 6), (pass_4, 5),
        (pass_3, 7), (pass_4, 6), (cross_keys,), (cross_attention,), (cross_out,), (feed, 0),
        (pass_4, 7), (feed, 1), (feed, 2), (feed, 3),
    ):
        step_of(*which)
    loc.drain()
    cp.drain()


def forward_all(weights, mem_in, x, cot, vec, slen, plen, rows_a, rows_f, ndp):
    anywhere = pl.BlockSpec(memory_space=pl.ANY)
    vmem = pl.BlockSpec(memory_space=pltpu.VMEM)
    rows = x.shape[0]
    ex = mem_in.shape[0] // ndp
    count = ex * MEMLEN
    split = (2, 2, 2)
    arrays = {
        "attn": ((8,) + split + (rows_a, D), BF),
        "feed": ((NZ,) + split + (4, rows_f, D), BF),
        "mem": ((ex, ndp) + mem_in.shape[1:], BF),
        "low": ((rows, D), BF),
        "keys": ((count, D), BF),
        "z": ((4, rows, D), BF),
        "slope": ((4, rows, D), F32),
        "wide": ((rows, D), F32),
        "dn": ((2,) + split + (4, rows_f, D), BF),
    }
    kinds = ["attn", "feed", "mem"] + ["low"] * 7 + ["keys"] * 2 + ["z", "slope", "wide", "wide", "dn"]
    low = pltpu.VMEM((rows, D), BF)
    return pl.pallas_call(
        forward_kernel,
        out_shape=[jax.ShapeDtypeStruct(*arrays[k]) for k in kinds],
        in_specs=[vmem] * 3 + [anywhere] + [vmem] * 5,
        out_specs=[anywhere] * len(kinds),
        scratch_shapes=[
            pltpu.VMEM((1, rows_a, D), BF),
            pltpu.VMEM((1, rows_a, D), BF),
            pltpu.VMEM((4, rows_f, D), BF),
            pltpu.VMEM((NZ,) + split + (1, rows_a, D), BF),
            pltpu.VMEM((NZ,) + split + (1, rows_a, D), BF),
            pltpu.VMEM(*arrays["feed"]),
            pltpu.VMEM(*arrays["mem"]),
            *[low] * 10,
            pltpu.VMEM(*arrays["keys"]),
            pltpu.VMEM(*arrays["keys"]),
            pltpu.VMEM(*arrays["z"]),
            pltpu.VMEM(*arrays["slope"]),
            pltpu.VMEM(*arrays["wide"]),
            pltpu.VMEM(*arrays["wide"]),
            pltpu.VMEM((4, 2, 2, 4, rows_f, D), BF),
            pltpu.SemaphoreType.DMA((128,)),
            pltpu.SemaphoreType.DMA((128,)),
            pltpu.SemaphoreType.DMA((48,)),
        ],
        compiler_params=pltpu.CompilerParams(
            collective_id=1, has_side_effects=True, vmem_limit_bytes=60 << 20
        ),
        name="forward_all",
    )(*weights, mem_in, x, cot, vec, slen, plen)


def backward_kernel(
    attn_h, dn_h, up_h, mem_h, q1_h, k1_h, v1_h, o1_h, q2_h, o2_h, a3_h, k2_h, v2_h, z_h, slope_h,
    h1_h, h2_h, dn_g, x_ref, cot_ref, vec_ref, slen_ref, plen_ref,
    ws, wc, wf, ms, mc, mf, ss, sc_, sf,
    out_ref, sg_ref, self_t, cross_t, feed_t, mem_t, vec_t, sq_t, norm_t, attn_g, up_g,
    wr, ur, mem_v, q1, k1, v1, o1, q2, o2, a1, a2, a3, k2, v2, z_v, slope_v, h1, h2, e3, du, db,
    ring_a, ring_u, held, r1, r2a, r2b, r3a, r3b, rz, whole, vw, vecg, v_send, v_recv, v_z,
    qa, qb, na, nb, opt_s, opt_c, opt_f, send, recv, local,
):
    dp, fs, z, y, x, c = place()
    ex_count, ndp = mem_v.shape[0], mem_v.shape[1]
    nfs = qa.shape[0]
    step, width = r1.shape[4], r1.shape[5]
    cut = step * 2 // 3
    head, rest = pl.ds(0, cut), pl.ds(cut, step - cut)
    per = width // LANES
    to_y, to_x, to_c = peer_id(z, 1 - y, x, c), peer_id(z, y, 1 - x, c), peer_id(z, y, x, 1 - c)
    cp, loc = Copies(send, recv, None), Local(local)

    fetch_order = [dn_h.at[4 + j] for j in range(4)] + [
        attn_h.at[m] for m in (7, 5, 6, 4, 3, 0, 1, 2)
    ]
    depth = wr.shape[0]
    fetched, used = [], [0]
    up_got = []

    def fetch():
        if len(fetched) < len(fetch_order):
            i = len(fetched)
            fetched.append(loc.start(fetch_order[i], wr.at[i % depth]))

    def weight():
        i = used[0]
        used[0] += 1
        fetched[i].wait()
        return wr[i % depth]

    def fetch_up():
        i = len(up_got)
        if i < 4:
            up_got.append(loc.start(up_h.at[pl.ds(0, ur.shape[1]), i], ur.at[i % ur.shape[0]]))

    fetch()
    a3_ok = loc.start(a3_h, a3)
    slope_ok = [loc.start(slope_h.at[0], slope_v.at[0])]
    for j in range(1, 4):
        fetch()
        slope_ok.append(loc.start(slope_h.at[j], slope_v.at[j]))
    for _ in range(ur.shape[0]):
        fetch_up()
    z_ok = loc.start(z_h, z_v)
    h2_ok = loc.start(h2_h, h2)
    cross_ok = [
        loc.start(a, b)
        for a, b in ((o2_h, o2), (q2_h, q2), (k2_h, k2), (v2_h, v2), (mem_h, mem_v), (h1_h, h1))
    ]
    self_ok = [loc.start(a, b) for a, b in ((o1_h, o1), (q1_h, q1), (k1_h, k1), (v1_h, v1))]
    groups = (
        ((ws, ms, ss), opt_s, self_t, z),
        ((wc, mc, sc_), opt_c, cross_t, NZ + z),
        ((wf, mf, sf), opt_f, feed_t, 2 * NZ + z // 2),
    )
    opt = [
        loc.start(src, dst.at[i]) for srcs, dst, _, _ in groups for i, src in enumerate(srcs)
    ]
    greet(
        [((dp + k) % ndp, fs) for k in range(1, ndp)] + [(dp, (fs + k) % nfs) for k in range(1, nfs)]
    )

    def attn_src(base, r):
        rows = pl.ds(r * step, step)
        return lambda zz, cc: attn_g.at[base + zz, :, :, cc, rows]

    def feed_src(j):
        return lambda zz, cc: up_g.at[j, zz, :, :, cc] if zz < 2 else dn_g.at[zz - 2, :, :, cc, j]

    sources = [feed_src(j) for j in range(4)] + [attn_src(b, r) for b in (4, 0) for r in range(2)]
    n = len(sources)
    sc, sl, s1, s2, sz = {}, {}, {}, {}, {}

    def phase_0(t):
        stored(*((8 + t,) if t < 4 else (4, 5, 6, 7) if t < 6 else (0, 1, 2, 3)))
        for zz in range(NZ):
            sc[t, zz] = cp.remote(sources[t](zz, 1 - c), r1.at[t, zz], to_c)
            sl[t, zz] = loc.start(sources[t](zz, c), held.at[t % held.shape[0], zz])

    def add_c(t, fixed_y, fixed_x, rows):
        slot = t % held.shape[0]

        def body(i, _):
            zz, o = i // 2, i % 2
            yy = o if fixed_y is None else fixed_y
            xx = o if fixed_x is None else fixed_x
            r1[t, zz, yy, xx, rows] = r1[t, zz, yy, xx, rows] + held[slot, zz, yy, xx, rows]
            return 0

        lax.fori_loop(0, NZ * 2, body, 0)

    def phase_c(t):
        for zz in range(NZ):
            sc[t, zz].wait_recv()
            sl[t, zz].wait()
        add_c(t, None, 1 - x, head)
        s1[t, 0] = cp.remote(r1.at[t, :, :, 1 - x, head], r2a.at[t], to_x)
        add_c(t, 1 - y, None, rest)
        s1[t, 1] = cp.remote(r1.at[t, :, 1 - y, :, rest], r2b.at[t], to_y)
        add_c(t, None, x, head)
        add_c(t, y, None, rest)

    def add_1(t, yy, xx, rows, got, where):
        def body(zz, _):
            r1[t, zz, yy, xx, rows] = r1[t, zz, yy, xx, rows] + got[t, zz, where]
            return 0

        lax.fori_loop(0, NZ, body, 0)

    def phase_1(t):
        s1[t, 0].wait_recv()
        add_1(t, 1 - y, x, head, r2a, 1 - y)
        s2[t, 0] = cp.remote(r1.at[t, :, 1 - y, x, head], r3a.at[t], to_y)
        s1[t, 1].wait_recv()
        add_1(t, y, 1 - x, rest, r2b, 1 - x)
        s2[t, 1] = cp.remote(r1.at[t, :, y, 1 - x, rest], r3b.at[t], to_x)
        add_1(t, y, x, head, r2a, y)
        add_1(t, y, x, rest, r2b, x)

    def phase_2(t):
        s2[t, 0].wait_recv()
        s2[t, 1].wait_recv()

        def body(zz, _):
            r1[t, zz, y, x, head] = r1[t, zz, y, x, head] + r3a[t, zz]
            r1[t, zz, y, x, rest] = r1[t, zz, y, x, rest] + r3b[t, zz]
            return 0

        lax.fori_loop(0, NZ, body, 0)
        for k in range(1, NZ):
            zt = (z + k) % NZ
            sz[t, k] = cp.remote(r1.at[t, zt, y, x], rz.at[t, k - 1], peer_id(zt, y, x, c))

    def lines_of(dst, start, stride):
        for i in range(per):
            dst[pl.ds(start + i, step, stride=stride), :] = whole[:, i * LANES : (i + 1) * LANES]

    def phase_z(t):
        for k in range(1, NZ):
            sz[t, k].wait_recv()
        total = r1[t, z, y, x].astype(F32)
        for k in range(1, NZ):
            total = total + rz[t, k - 1].astype(F32)
        whole[...] = total
        if t >= 4:
            lines_of((cross_t, self_t)[t // 2 - 2], (t % 2) * step * per, per)
            return
        for up in (True, False):

            @pl.when(z // 2 == (0 if up else 1))
            def _():
                lines_of(feed_t, *feed_lines(t, step, width, up))

    row = lambda i: vec_ref[i : i + 1, :]
    gains = [row(2 * i) for i in range(3)]
    shifts = [row(2 * i + 1) for i in range(3)]
    mem_rows = lambda: mem_v[...].reshape(ex_count * MEMLEN, D)
    up_mat = lambda j: ur[j % ur.shape[0]].reshape(D, D)
    stores, order_a, waited = {}, [], set()

    def stored(*which):
        for m in which:
            if m not in waited:
                stores[m].wait()
                waited.add(m)

    def give(m, value):
        slots, i = ring_a.shape[0], len(order_a)
        if i >= slots:
            stored(order_a[i - slots])
        ring_a[i % slots] = value.astype(BF).reshape(ring_a.shape[1:])
        order_a.append(m)
        stores[m] = loc.start(ring_a.at[i % slots], attn_g.at[m])

    def begin():
        for i in range(EX_DEV):
            rows = pl.ds(i * SUF, SUF)
            seed = seed_of(cot_ref, slen_ref, i)
            sg_ref[rows] = seed
            e3[rows] = seed.astype(BF)
        vecg[...] = jnp.zeros_like(vecg)
        vecg[6:7] = column_sum(e3[...].astype(F32))

    def feed(j):
        dn = weight()
        if j == 0:
            a3_ok.wait()
        slope_ok[j].wait()
        du[j] = (dot_nt(e3[...], dn) * slope_v[j]).astype(BF)
        slot = j % ring_u.shape[0]
        if j >= ring_u.shape[0]:
            stored(8 + j - ring_u.shape[0])
        ring_u[slot] = dot_tn(a3[...], du[j]).astype(BF).reshape(ring_u.shape[1:])
        stores[8 + j] = loc.start(ring_u.at[slot], up_g.at[j])
        vecg[7 + j : 8 + j] = column_sum(du[j].astype(F32))
        if j == 0:
            z_ok.wait()
            h2_ok.wait()
            out_ref[...] = h2[...] + row(6)
        out_ref[...] += dot_nn(z_v[j], dn)
        fetch()

    def feed_down():
        unit, scale = norm_parts(h2[...])
        for j in range(4):
            up_got[j].wait()
            part = dot_nt(du[j], up_mat(j))
            if j == 0:
                h2[...] = part
            else:
                h2[...] += part
            fetch_up()
        grad = h2[...]
        vecg[4:5] = column_sum(grad * unit)
        vecg[5:6] = column_sum(grad)
        sg_ref[...] += norm_back(unit, scale, gains[2], grad)
        db[...] = sg_ref[...].astype(BF)

    def cross_begin():
        cross_ok[0].wait()
        give(7, dot_tn(o2[...], db[...]))
        e3[...] = dot_nt(db[...], weight()).astype(BF)
        fetch()
        for one in cross_ok[1:4]:
            one.wait()

    def cross_part():
        attend_back(cross_mask, plen_ref, q2, k2, v2, e3, MEMLEN)

    def cross_query():
        cross_ok[5].wait()
        unit, _ = norm_parts(h1[...])
        a2[...] = (unit * gains[1] + shifts[1]).astype(BF)
        give(4, dot_tn(a2[...], q2[...]))

    def cross_key():
        cross_ok[4].wait()
        give(5, dot_tn(mem_rows(), k2[...]))

    def cross_value():
        give(6, dot_tn(mem_rows(), v2[...]))

    mem_sent = []

    def cross_memory():
        key_mat, value_mat = weight(), weight()
        for i in range(ex_count):
            keys = pl.ds(i * MEMLEN, MEMLEN)
            part = dot_nt(k2[keys], key_mat) + dot_nt(v2[keys], value_mat)
            mem_v[i] = part.astype(BF).reshape(mem_v.shape[1:])
        fetch()
        fetch()

    def send_mem():
        mem_sent.append(loc.start(mem_v.at[:, dp], mem_t.at[pl.ds(ex_count * dp, ex_count)]))
        for k in range(1, ndp):
            mem_sent.append(
                cp.remote(
                    mem_v.at[:, (dp + k) % ndp],
                    mem_t.at[pl.ds(ex_count * dp, ex_count)],
                    ((dp + k) % ndp, fs),
                )
            )

    def cross_end():
        grad = dot_nt(q2[...], weight())
        fetch()
        unit, scale = norm_parts(h1[...])
        vecg[2:3] = column_sum(grad * unit)
        vecg[3:4] = column_sum(grad)
        sg_ref[...] += norm_back(unit, scale, gains[1], grad)
        db[...] = sg_ref[...].astype(BF)

    def self_begin():
        for one in self_ok:
            one.wait()
        give(3, dot_tn(o1[...], db[...]))
        e3[...] = dot_nt(db[...], weight()).astype(BF)
        fetch()
        unit, _ = norm_parts(x_ref[...].astype(F32))
        a1[...] = (unit * gains[0] + shifts[0]).astype(BF)

    def self_part():
        attend_back(self_mask, slen_ref, q1, k1, v1, e3, SUF)

    def self_weights():
        for i, ref in enumerate((q1, k1, v1)):
            give(i, dot_tn(a1[...], ref[...]))

    def self_end():
        grad = dot_nt(q1[...], weight())
        grad = grad + dot_nt(k1[...], weight())
        grad = grad + dot_nt(v1[...], weight())
        unit, scale = norm_parts(x_ref[...].astype(F32))
        vecg[0:1] = column_sum(grad * unit)
        vecg[1:2] = column_sum(grad)
        sg_ref[...] += norm_back(unit, scale, gains[0], grad)

    vec_cp = []

    def vec_step(i):
        if i == 0:
            vec_cp.append(cp.remote(vecg, v_recv.at[0], to_c))
            return
        if i == 4:
            for one in vec_cp[3:]:
                one.wait_recv()
            vw[...] = (v_z[0] + v_z[1]) + (v_z[2] + v_z[3])
            vec_t[...] = jnp.zeros_like(vec_t)
            for i in range(per):
                vec_t[pl.ds(i, 11, stride=per), :] = vw[0:11, i * LANES : (i + 1) * LANES]
            return
        vec_cp[-1].wait_recv()
        i -= 1
        v_send[i] = (vecg[...] if i == 0 else v_send[i - 1]) + v_recv[i]
        if i < 2:
            vec_cp.append(cp.remote(v_send.at[i], v_recv.at[i + 1], (to_x, to_y)[i]))
        else:
            v_z[z] = v_send[2]
            for k in range(1, NZ):
                vec_cp.append(cp.remote(v_send.at[2], v_z.at[z], peer_id((z + k) % NZ, y, x, c)))

    for step_of, *which in (
        (begin,), (feed, 0), (phase_0, 0), (feed, 1), (feed, 2), (phase_c, 0), (feed, 3),
        (phase_0, 1), (feed_down,), (cross_begin,), (cross_part,), (phase_1, 0), (phase_0, 2),
        (cross_query,), (phase_c, 1), (cross_key,), (phase_c, 2), (phase_2, 0), (cross_value,),
        (cross_memory,), (send_mem,), (phase_0, 3), (cross_end,), (phase_0, 4), (self_begin,),
        (self_part,), (phase_c, 3), (phase_1, 2), (self_weights,), (phase_0, 5), (phase_c, 5),
        (self_end,), (phase_1, 1), (phase_0, 7), (phase_2, 2), (phase_c, 7), (vec_step, 0),
        (phase_1, 3), (phase_2, 1), (phase_1, 7), (phase_1, 5), (phase_2, 3), (phase_c, 4),
        (phase_0, 6), (vec_step, 1), (phase_c, 6), (phase_2, 7), (phase_z, 3), (phase_2, 5),
        (vec_step, 2), (vec_step, 3), (phase_1, 4), (phase_z, 5), (phase_z, 0), (phase_z, 2),
        (phase_2, 4), (phase_1, 6), (phase_z, 7), (phase_2, 6), (phase_z, 1), (phase_z, 4),
        (vec_step, 4), (phase_z, 6),
    ):
        step_of(*which)
    sq = squares(self_t[...]) + squares(cross_t[...]) + squares(feed_t[...])
    sq = sum_everywhere(cp, sq, qa, qb, dp, fs) + squares(vec_t[...])
    sq_t[...] = sq
    factor = clip_of(sq)
    rows = lax.broadcasted_iota(jnp.int32, (32, LANES), 0)
    tile = jnp.zeros((32, LANES), F32)
    for one in opt:
        one.wait()
    for _, dst, g, line in groups:
        w = dst[0]
        ratio = lamb_step(w, g[...], dst[1], dst[2], factor)[2]
        for first, a in ((0, ratio), (16, w)):
            part = jnp.sum(a * a, axis=0, keepdims=True)
            tile = tile + jnp.where(rows == first + line, part, 0.0)
    norm_t[...] = sum_everywhere(cp, tile, na, nb, dp, fs)
    mem_sent[0].wait()
    for one in mem_sent[1:]:
        one.wait_recv()
    cp.drain()


def backward_all(kept, x, cot, vec, slen, plen, states, rows_a, rows_f, ndp, nfs):
    anywhere = pl.BlockSpec(memory_space=pl.ANY)
    vmem = pl.BlockSpec(memory_space=pltpu.VMEM)
    mem = kept[3]
    ex, _, pos, width = mem.shape
    rows = x.shape[0]
    lines = [w.shape[0] for w in states[:3]]
    step = rows_f
    cut = step * 2 // 3
    split = (2, 2, 2)
    low = lambda *dims: pltpu.VMEM(dims + (width,), BF)
    wide = lambda *dims: pltpu.VMEM(dims, F32)
    shape = lambda *dims: jax.ShapeDtypeStruct(dims, F32)
    vec_rows = 16
    return pl.pallas_call(
        backward_kernel,
        out_shape=[
            shape(rows, width),
            shape(rows, width),
            *[shape(k, LANES) for k in lines],
            jax.ShapeDtypeStruct((ndp * ex, pos, width), BF),
            shape(vec_rows * width // LANES, LANES),
            shape(8, LANES),
            shape(32, LANES),
            jax.ShapeDtypeStruct((8,) + split + (rows_a, width), BF),
            jax.ShapeDtypeStruct((4, 2) + split + (rows_f, width), BF),
        ],
        in_specs=[anywhere] * 18 + [vmem] * 5 + [anywhere] * 9,
        out_specs=[vmem] * 5 + [anywhere] + [vmem] * 3 + [anywhere] * 2,
        scratch_shapes=[
            low(4, width),
            low(2, up_rows(kept[2]), rows_f),
            low(ex, ndp, pos),
            *[low(rows)] * 9,
            low(ex * MEMLEN),
            low(ex * MEMLEN),
            low(4, rows),
            wide(4, rows, width),
            wide(rows, width),
            wide(rows, width),
            low(rows),
            low(4, rows),
            low(rows),
            low(2, *split, rows_a),
            low(2, 2, *split, rows_f),
            low(2, NZ, 2, 2, step),
            low(8, NZ, 2, 2, step),
            low(8, NZ, 2, cut),
            low(8, NZ, 2, step - cut),
            low(8, NZ, cut),
            low(8, NZ, step - cut),
            low(8, NZ - 1, step),
            wide(step, width),
            wide(vec_rows, width),
            wide(vec_rows, width),
            wide(3, vec_rows, width),
            wide(3, vec_rows, width),
            wide(NZ, vec_rows, width),
            wide(nfs, 8, LANES),
            wide(ndp, 8, LANES),
            wide(nfs, 32, LANES),
            wide(ndp, 32, LANES),
            *[wide(3, k, LANES) for k in lines],
            pltpu.SemaphoreType.DMA((128,)),
            pltpu.SemaphoreType.DMA((128,)),
            pltpu.SemaphoreType.DMA((96,)),
        ],
        compiler_params=pltpu.CompilerParams(
            collective_id=2, has_side_effects=True, vmem_limit_bytes=62 << 20
        ),
        name="backward_all",
    )(*kept, x, cot, vec, slen, plen, *states)


def up_rows(view):
    return view.shape[0] // 2


def update_kernel(*refs):
    ins, outs = refs[:18], refs[18:]
    gs, ws, ms, vs, (gv, sq, norms) = ins[0:3], ins[3:7], ins[7:11], ins[11:15], ins[15:18]
    z = lax.axis_index("dp") // 2
    factor = clip_of(sq[...])
    sums = jnp.sqrt(jnp.sum(norms[...], axis=1, keepdims=True))
    ratio_norm, weight_norm = sums[0:16], sums[16:32]
    trust = weight_norm / (ratio_norm + trust_eps)
    row = lax.broadcasted_iota(jnp.int32, (16, 1), 0)
    for i, first in enumerate((z, NZ + z, 2 * NZ + z // 2)):
        g = gs[i][...]
        w = ws[i][...]
        m, v, ratio = lamb_step(w, g, ms[i][...], vs[i][...], factor)
        rate = jnp.sum(jnp.where(row == first, trust, 0.0), axis=0, keepdims=True)
        for ref, value in zip(outs[4 * i : 4 * i + 4], (g, m, v, w - learn_rate * rate * ratio)):
            ref[...] = value
    w = ws[3][...]
    g = gv[0 : w.shape[0], :]
    m, v, ratio = lamb_step(w, g, ms[3][...], vs[3][...], factor)
    line = lax.broadcasted_iota(jnp.int32, w.shape, 0)
    spread = lax.broadcasted_iota(jnp.int32, (16, LANES), 1)
    pick = spread == lax.broadcasted_iota(jnp.int32, (16, LANES), 0)
    lanes = spread[0:1]
    on_row = lambda a: jnp.sum(jnp.where(pick, a, 0.0), axis=0, keepdims=True)
    weight_row, ratio_row = on_row(weight_norm), on_row(ratio_norm)
    rate = jnp.zeros(w.shape, F32)
    per = D // LANES
    for i in range(8):
        mine = (line >= i * per) & (line < ((i + 1) * per if i < 7 else w.shape[0]))
        norm = lambda a: norm_of(jnp.where(mine, a * a, 0.0))
        wn, rn = norm(w), norm(ratio)
        rate = jnp.where(mine, wn / (rn + trust_eps), rate)
        weight_row = jnp.where(lanes == 10 + i, wn, weight_row)
        ratio_row = jnp.where(lanes == 10 + i, rn, ratio_row)
    for ref, value in zip(outs[12:16], (g, m, v, w - learn_rate * rate * ratio)):
        ref[...] = value
    outs[16][0:1, :] = weight_row[:, 0:18]
    outs[16][1:2, :] = ratio_row[:, 0:18]
    outs[17][...] = norm_of(sq[...])


def update_all(totals, weights, moments, seconds, vec_total, sq, norms):
    vmem = pl.BlockSpec(memory_space=pltpu.VMEM)
    shape = lambda a: jax.ShapeDtypeStruct(a.shape, F32)
    outs = [shape(a) for a in weights for _ in range(4)]
    outs += [jax.ShapeDtypeStruct((2, 18), F32), jax.ShapeDtypeStruct((1, 1), F32)]
    return pl.pallas_call(
        update_kernel,
        out_shape=outs,
        in_specs=[vmem] * 18,
        out_specs=[vmem] * len(outs),
        compiler_params=pltpu.CompilerParams(vmem_limit_bytes=40 << 20),
        name="update_all",
    )(*totals, *weights, *moments, *seconds, vec_total, sq, norms)


def fast_shards(
    suffix,
    memory,
    prefix_lengths,
    suffix_lengths,
    cotangent,
    self_weights,
    self_moment,
    self_second,
    cross_weights,
    cross_moment,
    cross_second,
    feed_weights,
    feed_moment,
    feed_second,
    vectors,
    vector_moment,
    vector_second,
):
    row_count = EX_DEV * SUF
    ndp, nfs = lax.axis_size("dp"), lax.axis_size("fsdp")
    owners = ndp * nfs
    rows_a, rows_f = self_weights.shape[0] // D, feed_weights.shape[0] // (4 * D)
    flat = lambda *group: [a.reshape(-1, LANES) for a in group]
    weights = flat(self_weights, cross_weights, feed_weights, vectors)
    moments = flat(self_moment, cross_moment, feed_moment, vector_moment)
    seconds = flat(self_second, cross_second, feed_second, vector_second)
    lens = lambda a: jnp.broadcast_to(a[0][:, None, None], (EX_DEV, 8, LANES))
    common = (
        suffix.reshape(row_count, D),
        cotangent.reshape(row_count, D),
        vectors.reshape(-1, D),
        lens(suffix_lengths),
        lens(prefix_lengths),
    )
    attn, feed, *kept = forward_all(weights[:3], memory[0], *common, rows_a, rows_f, ndp)
    kept = [
        attn.reshape(8, D, D),
        feed.reshape(8, D, D),
        feed.reshape(owners, 4, rows_f, D),
        *kept,
    ]
    layer_output, suffix_gradient, *totals, memory_back, vec_sum, squared, norms, _, _ = backward_all(
        kept, *common, weights[:3] + moments[:3] + seconds[:3], rows_a, rows_f, ndp, nfs
    )
    *new, tensor_norms, global_norm = update_all(
        totals, weights, moments, seconds, vec_sum, squared, norms
    )
    return (
        layer_output.reshape(1, EX_DEV, SUF, D),
        suffix_gradient.reshape(1, EX_DEV, SUF, D),
        memory_back.astype(F32)[None],
        *[a.reshape(-1) for a in new],
        tensor_norms,
        global_norm.reshape(()),
    )


def pick(mesh):
    if mesh.shape["dp"] == 8 and mesh.shape["fsdp"] == 4:
        return fast_shards
    return shards


def solution(mesh):
    return jax.shard_map(
        pick(mesh),
        mesh=mesh,
        in_specs=(
            P("fsdp", "dp", None, None),
            P("fsdp", None, "dp", None),
            P("fsdp", "dp"),
            P("fsdp", "dp"),
            P("fsdp", "dp", None, None),
            P(("dp", "fsdp")),
            P(("dp", "fsdp")),
            P(("dp", "fsdp")),
            P(("dp", "fsdp")),
            P(("dp", "fsdp")),
            P(("dp", "fsdp")),
            P(("dp", "fsdp")),
            P(("dp", "fsdp")),
            P(("dp", "fsdp")),
            P(),
            P(),
            P(),
        ),
        out_specs=(
            P("fsdp", "dp", None, None),
            P("fsdp", "dp", None, None),
            P("fsdp", None, "dp", None),
            P(("dp", "fsdp")),
            P(("dp", "fsdp")),
            P(("dp", "fsdp")),
            P(("dp", "fsdp")),
            P(("dp", "fsdp")),
            P(("dp", "fsdp")),
            P(("dp", "fsdp")),
            P(("dp", "fsdp")),
            P(("dp", "fsdp")),
            P(("dp", "fsdp")),
            P(("dp", "fsdp")),
            P(("dp", "fsdp")),
            P(),
            P(),
            P(),
            P(),
            P(),
            P(),
        ),
        check_vma=False,
    )
```
